32 devices in a mesh: seq: 8 (over z, x), grp: 4 (over y, core).
Axes of the slice: x: 2, y: 2, z: 4, core: 2. Of those that a mesh axis runs over, the one named last changes fastest.
Arguments:
- tokens: bfloat16 [16, 2048, 1024], P('seq', 'grp'), may hold values from -6 to 6
- segments: int32 [16, 2048], P('seq'), may hold values from 0 to 3, never falling along the last dimension, each value on 1 to 1024 neighbouring positions
- routed: int32 [16, 256], P('seq'), may hold values from 0 to 2047, as said below
- qkv_weight: bfloat16 [1024, 3072], P(('seq', 'grp')), may hold values from -0.1875 to 0.1875
- out_weight: bfloat16 [1024, 1024], P(('seq', 'grp')), may hold values from -0.75 to 0.75
- up_weight: bfloat16 [1024, 4096], P(('seq', 'grp')), may hold values from -0.1875 to 0.1875
- down_weight: bfloat16 [4096, 1024], P(('seq', 'grp')), may hold values from -0.09375 to 0.09375
- attn_gain: bfloat16 [1024], P(('seq', 'grp')), may hold values from 0.5 to 1.5
- mlp_gain: bfloat16 [1024], P(('seq', 'grp')), may hold values from 0.5 to 1.5
- router_weight: bfloat16 [1024], P(('seq', 'grp')), may hold values from -0.1875 to 0.1875
- cotangent: bfloat16 [16, 2048, 1024], P('seq', 'grp'), may hold values from -6 to 6
Outputs:
- mixed: bfloat16 [16, 2048, 1024], P('seq', 'grp')
- input_grad: bfloat16 [16, 2048, 1024], P('seq', 'grp')
- qkv_grad: float32 [1024, 3072], P(('seq', 'grp'))
- out_grad: float32 [1024, 1024], P(('seq', 'grp'))
- up_grad: float32 [1024, 4096], P(('seq', 'grp'))
- down_grad: float32 [4096, 1024], P(('seq', 'grp'))
- attn_gain_grad: float32 [1024], P(('seq', 'grp'))
- mlp_gain_grad: float32 [1024], P(('seq', 'grp'))
- router_grad: float32 [1024], P(('seq', 'grp'))
The draws below stay inside these ranges and needn't reach their ends.
Inputs may be any that keep to these rules, and one draw needn't show every extreme that they name: Each sequence's 256 routed positions are distinct and ascending. In the aligned blocks of 512 positions (positions 0 to 511, and so on) at most 128 routed positions lie in one block, and in every sequence some block holds exactly 128.
All inputs are finite; a program needn't handle non-finite values.
Results may differ from the reference program's by a relative error of at most 0.01.
Values may be sent and summed in bfloat16 or wider, within the bound.
No kernel may reach another device: no remote copies, remote signals or barrier semaphores. Data moves between devices by JAX's collectives and lax.ppermute only.
A program may use at most 256 MiB of HBM per device.

```python
import math
import jax
import jax.numpy as jnp
import numpy as np
from jax import lax

D = 1024
FF = 4096
HEADS = 16
HEAD_DIM = 64
LEN = 2048
SEG_COUNT = 4
K = 256
STRETCH = 512
MOST = 128
SEQS = 16
N_GRP = 4


def routed_sequence(seq_key):
    cut_key, order_key, place_key = jax.random.split(seq_key, 3)
    remainder = K - MOST
    cut_points = jnp.sort(jax.random.randint(cut_key, (N_GRP - 2,), 0, remainder + 1)).astype(jnp.int32)
    edge_points = jnp.concatenate([jnp.zeros((1,), jnp.int32), cut_points, jnp.full((1,), remainder, jnp.int32)])
    block_counts = jnp.concatenate([jnp.full((1,), MOST, jnp.int32), edge_points[1:] - edge_points[:-1]])
    block_counts = jax.random.permutation(order_key, block_counts)
    place_keys = jax.random.split(place_key, N_GRP)
    ranking = jax.vmap(lambda sub_key: jax.random.permutation(sub_key, STRETCH))(place_keys)
    chosen = (ranking < block_counts[:, None]).reshape(LEN)
    return jnp.nonzero(chosen, size=K)[0].astype(jnp.int32)


def draw_routed(key, part):
    return jax.vmap(routed_sequence)(jax.random.split(key, SEQS))


def block_levels(own_key, shape, cuts, low, top_value):
    factor_of, own = 1.0, jax.random.fold_in(own_key, 6)
    for dim, shards_of in cuts:
        steps = jnp.exp(jax.random.uniform(jax.random.fold_in(own, dim), (shards_of,), jnp.float32, low / len(cuts), top_value / len(cuts)))
        factor_of = factor_of * jnp.repeat(steps, shape[dim] // shards_of).reshape([-1 if axis == dim else 1 for axis in range(len(shape))])
    return factor_of


def length_profile(number_of, total, bound, lean):
    weights = [(1 << 20) // math.isqrt(rank ** lean) + 1 for rank in range(2, number_of + 1)]
    surplus, holding = total - bound - (number_of - 1), [1] * (number_of - 1)
    while surplus > 0:
        movable = [i for i in range(number_of - 1) if holding[i] < bound]
        mass, remaining = sum([weights[i] for i in movable]), surplus
        for i in movable:
            more = min(bound - holding[i], max(1, remaining * weights[i] // mass), surplus)
            holding[i] = holding[i] + more
            surplus = surplus - more
    return np.array([bound] + holding)


def ragged(key, amount, total, bound, lean):
    if amount == 2:
        one = jax.random.randint(key, (), max(1, total - bound), min(bound, total - 1) + 1)
        return jnp.stack([one, total - one])
    sizes = jnp.asarray(length_profile(amount, total, bound, lean), jnp.int32)
    couples = (amount - 1) // 2
    donor, sink = sizes[1:1 + 2 * couples:2], sizes[2:2 + 2 * couples:2]
    margin = jnp.minimum(donor - 1, bound - sink)
    shifted = jax.random.randint(jax.random.fold_in(key, 1), (couples,), 0, 1 << 20) % (margin + 1)
    sizes = sizes.at[1:1 + 2 * couples:2].set(donor - shifted).at[2:2 + 2 * couples:2].set(sink + shifted)
    return sizes[jax.random.permutation(jax.random.fold_in(key, 2), amount)]


def normal_values(key, extent, width, limit, pieces=(), kind=jnp.bfloat16):
    array = width * jax.random.normal(key, extent, jnp.float32)
    if pieces:
        array = array * block_levels(key, extent, pieces, -0.22, 0.18)
    return jnp.clip(array, -limit, limit).astype(kind)


def setup_inputs(seed: int = 0) -> dict:
    keys = jax.random.split(jax.random.key(seed), 12)
    return {
        "tokens": normal_values(keys[0], (SEQS, LEN, D), 1.0, 6.0, ((0, 8), (1, 4))),
        "segments": jax.vmap(lambda own: jnp.searchsorted(jnp.cumsum(ragged(own, SEG_COUNT, LEN, LEN // 2, 1)), jnp.arange(LEN), side="right"))(jax.random.split(keys[1], SEQS)).reshape((SEQS, LEN)).astype(jnp.int32),
        "routed": draw_routed(jax.random.fold_in(keys[11], 71), 0),
        "qkv_weight": normal_values(keys[3], (D, 3 * D), D ** -0.5, 0.1875, ((0, 32),)),
        "out_weight": normal_values(keys[4], (D, D), (D // 16) ** -0.5, 0.75, ((0, 32),)),
        "up_weight": normal_values(keys[5], (D, FF), D ** -0.5, 0.1875, ((0, 32),)),
        "down_weight": normal_values(keys[6], (FF, D), FF ** -0.5, 0.09375, ((0, 32),)),
        "attn_gain": jnp.clip(1.0 + 0.1 * jax.random.normal(keys[7], (D,), jnp.float32), 0.5, 1.5).astype(jnp.bfloat16),
        "mlp_gain": jnp.clip(1.0 + 0.1 * jax.random.normal(keys[8], (D,), jnp.float32), 0.5, 1.5).astype(jnp.bfloat16),
        "router_weight": normal_values(keys[9], (D,), D ** -0.5, 0.1875, ((0, 32),)),
        "cotangent": normal_values(keys[10], (SEQS, LEN, D), 1.0, 6.0, ((0, 8), (1, 4))),
    }


@jax.custom_vjp
def low(v):
    return lax.optimization_barrier(v.astype(jnp.bfloat16)).astype(jnp.float32)

@jax.custom_vjp
def low_back(v):
    return v

def low_keep(v):
    return (low(v), None)

def low_pass(kept, grad):
    return (grad,)

def back_keep(v):
    return (v, None)

def back_low(kept, grad):
    return (low(grad),)
low.defvjp(low_keep, low_pass)
low_back.defvjp(back_keep, back_low)
epsilon = 1e-06
masked = -1e+30
highest = lax.Precision.HIGHEST

def rms_norm(values, gain_vec):
    return values * lax.rsqrt(lax.optimization_barrier(jnp.mean(values * values, axis=-1, keepdims=True)) + epsilon) * gain_vec

def block_branch(routed_rows, row_pos, row_seg, weights):
    qkv_w, out_w, up_w, down_w, gain_one, gain_two, router_w = weights
    routed_rows = low_back(routed_rows)
    row_count = routed_rows.shape[0]
    router = jnp.dot(routed_rows, router_w, precision=highest)
    normed = low(rms_norm(routed_rows, gain_one))
    projected = low_back(low(jnp.dot(normed, qkv_w, precision=highest)))
    queries = projected[:, :D].reshape(row_count, HEADS, HEAD_DIM)
    keys_all = projected[:, D:2 * D].reshape(row_count, HEADS, HEAD_DIM)
    values_all = projected[:, 2 * D:].reshape(row_count, HEADS, HEAD_DIM)
    logits = low_back(jnp.einsum('qhe,khe->hqk', queries, keys_all, precision=highest) * HEAD_DIM ** (-0.5))
    allowed = (row_pos[None, :] <= row_pos[:, None]) & (row_seg[None, :] == row_seg[:, None])
    logits = jnp.where(allowed[None], logits, masked)
    row_peak = lax.optimization_barrier(jnp.max(logits, axis=-1, keepdims=True))
    weights_exp = jnp.exp(logits - row_peak)
    attn_probs = low(weights_exp / lax.optimization_barrier(jnp.sum(weights_exp, axis=-1, keepdims=True)))
    mixed_heads = low_back(low(jnp.einsum('hqk,khe->qhe', attn_probs, values_all, precision=highest)))
    mixed_heads = mixed_heads.reshape(row_count, D)
    branch_a = low_back(jnp.dot(mixed_heads, out_w, precision=highest))
    hidden = routed_rows + branch_a
    normed_two = low(rms_norm(hidden, gain_two))
    pre_act = low_back(jnp.dot(normed_two, up_w, precision=highest))
    active = low(jax.nn.gelu(pre_act, approximate=True))
    branch_m = low_back(jnp.dot(active, down_w, precision=highest))
    return low(router[:, None] * (branch_a + branch_m))

def sequence_out(seq_tokens, weights, positions, row_seg):
    routed_rows = jnp.take(seq_tokens, positions, axis=0)
    scaled_out = block_branch(routed_rows, positions, row_seg, weights)
    return seq_tokens + jnp.zeros_like(seq_tokens).at[positions].add(scaled_out)

def reference(tokens, segments, routed, qkv_weight, out_weight, up_weight, down_weight, attn_gain, mlp_gain, router_weight, cotangent):
    weights = tuple((item.astype(jnp.float32) for item in (qkv_weight, out_weight, up_weight, down_weight, attn_gain, mlp_gain, router_weight)))
    zero_grads = tuple((jnp.zeros_like(item) for item in weights))

    def per_sequence(grads_sum, inputs):
        seq_tokens, seq_cot, seq_seg, positions = inputs
        row_seg = jnp.take(seq_seg, positions)

        def forward(token_values, weight_set):
            return sequence_out(token_values, weight_set, positions, row_seg)
        result, pull_back = jax.vjp(forward, seq_tokens.astype(jnp.float32), weights)
        token_grad, weight_grads = pull_back(seq_cot.astype(jnp.float32))
        grads_sum = tuple((left + right for left, right in zip(grads_sum, weight_grads)))
        return (grads_sum, (result.astype(jnp.bfloat16), token_grad.astype(jnp.bfloat16)))
    grads_sum, outputs = lax.scan(per_sequence, zero_grads, (tokens, cotangent, segments, routed))
    return (outputs[0], outputs[1], grads_sum[0], grads_sum[1], grads_sum[2], grads_sum[3], grads_sum[4], grads_sum[5], grads_sum[6])
```

```python
import functools

import jax
import jax.numpy as jnp
from jax import lax
from jax.experimental import pallas as pl
from jax.experimental.pallas import tpu as pltpu
from jax.sharding import PartitionSpec as P

HEAD_DIM = 64
SEG_COUNT = 4
BLOCKS = 8
epsilon = 1e-06
masked = -1e30
f32 = jnp.float32
bf16 = jnp.bfloat16
gelu_scale = 0.7978845608028654
gelu_cubic = 0.044715

NN = (((1,), (0,)), ((), ()))
NT = (((1,), (1,)), ((), ()))
TN = (((0,), (0,)), ((), ()))


def mm(a, b, dims=NN):
    return lax.dot_general(a, b, dims, preferred_element_type=f32)


VM = pl.BlockSpec(memory_space=pltpu.VMEM)
SM = pl.BlockSpec(memory_space=pltpu.SMEM)


def call(body, args, outs, scratch=(), smem=0, flops=0, name=None):
    moved = sum(a.size * a.dtype.itemsize for a in args)
    moved += sum(o.size * o.dtype.itemsize for o in outs)
    return pl.pallas_call(
        body,
        out_shape=tuple(outs),
        in_specs=[SM] * smem + [VM] * (len(args) - smem),
        out_specs=tuple([VM] * len(outs)),
        scratch_shapes=list(scratch),
        cost_estimate=pl.CostEstimate(flops=flops, bytes_accessed=moved, transcendentals=0),
        compiler_params=pltpu.CompilerParams(vmem_limit_bytes=56 * 1024 * 1024),
        name=name,
    )(*args)


def out(shape, dtype):
    return jax.ShapeDtypeStruct(shape, dtype)


def pick_body(meta, pos_ref, src_ref, own_ref, oth_ref):
    rows, span = pos_ref.shape[1], src_ref.shape[1]
    core, base = meta[0], meta[1]
    lane = lax.broadcasted_iota(jnp.int32, (rows, span), 1) + base
    for half, ref in ((0, own_ref), (1, oth_ref)):
        seq = core if half == 0 else 1 - core
        hot = jnp.where(pos_ref[half] == lane, 1.0, 0.0).astype(bf16)
        src = src_ref[seq]
        ref[...] = mm(hot, src).astype(bf16)


def place_body(meta, pos_ref, base_ref, own_ref, oth_ref, out_ref):
    rows, span = pos_ref.shape[2], base_ref.shape[1]
    core, base = meta[0], meta[1]
    row = lax.broadcasted_iota(jnp.int32, (span, rows), 0) + base
    for half, ref in ((0, own_ref), (1, oth_ref)):
        seq = core if half == 0 else 1 - core
        hot = jnp.where(pos_ref[half] == row, 1.0, 0.0).astype(bf16)
        added = mm(hot, ref[...])
        out_ref[seq] = (base_ref[seq].astype(f32) + added).astype(bf16)


def attn_fwd_body(
    idx, xo_ref, xt_ref, segc_ref, segr_ref, *refs
):
    packs, (a_ref, qkv_ref, p_ref, o_ref, bo_ref, bt_ref, wq_ref, wo_ref, gr_ref, r_ref), (
        gcol,
    ) = refs[:BLOCKS], refs[BLOCKS : BLOCKS + 10], refs[BLOCKS + 10 :]
    rows, width = xo_ref.shape
    part = width // 4
    qcols = 3 * part
    blk = width // BLOCKS
    ob = part // BLOCKS
    for b, pk in enumerate(packs):
        s = idx[b]
        off = pl.multiple_of(s * blk, blk)
        wq_ref[pl.ds(off, blk), :] = pk[:, :qcols]
        gcol[pl.ds(off, blk), :] = pk[:, qcols : qcols + 128]
        off2 = pl.multiple_of(s * ob, ob)
        for j in range(4):
            wo_ref[pl.ds(off2, ob), j * part : (j + 1) * part] = pk[
                j * ob : (j + 1) * ob, qcols + 128 :
            ]
    eye = (
        lax.broadcasted_iota(jnp.int32, (8, 128), 0) == lax.broadcasted_iota(jnp.int32, (8, 128), 1)
    ).astype(f32).astype(bf16)
    gr = mm(eye, gcol[...], NT)
    gr_ref[...] = gr
    gain = gr[0:1]
    for half, x_ref in ((0, xo_ref), (1, xt_ref)):
        span = pl.ds(half * rows, rows)
        xb = x_ref[...]
        x = xb.astype(f32)
        scale = lax.rsqrt(jnp.mean(x * x, axis=-1, keepdims=True) + epsilon)
        a_ref[span, :] = (x * scale * gain).astype(bf16)
        r_ref[span, :] = mm(xb, gcol[...])

    def project(i, carry):
        cols = pl.ds(pl.multiple_of(i * part, part), part)
        qkv_ref[:, cols] = mm(a_ref[...], wq_ref[:, cols]).astype(bf16)
        return carry

    lax.fori_loop(0, 3, project, 0)
    ri = lax.broadcasted_iota(jnp.int32, (rows, rows), 0)
    ci = lax.broadcasted_iota(jnp.int32, (rows, rows), 1)
    causal = ci <= ri
    heads = part // HEAD_DIM
    score_scale = HEAD_DIM ** (-0.5)
    for half in range(2):
        allowed = causal & (segc_ref[half] == segr_ref[half])
        span = pl.ds(half * rows, rows)
        for h in range(heads):
            q = qkv_ref[span, h * HEAD_DIM : (h + 1) * HEAD_DIM]
            k = qkv_ref[span, part + h * HEAD_DIM : part + (h + 1) * HEAD_DIM]
            v = qkv_ref[span, 2 * part + h * HEAD_DIM : 2 * part + (h + 1) * HEAD_DIM]
            logits = jnp.where(allowed, mm(q, k, NT) * score_scale, masked)
            e = jnp.exp(logits - jnp.max(logits, axis=-1, keepdims=True))
            p = e / jnp.sum(e, axis=-1, keepdims=True)
            p_ref[half * heads + h] = p
            o_ref[span, h * HEAD_DIM : (h + 1) * HEAD_DIM] = mm(p.astype(bf16), v).astype(bf16)

    def project_out(i, carry):
        cols = pl.ds(pl.multiple_of(i * part, part), part)
        res = mm(o_ref[...], wo_ref[:, cols]).astype(bf16)
        bo_ref[:, cols] = res[:rows]
        bt_ref[:, cols] = res[rows:]
        return carry

    lax.fori_loop(0, 4, project_out, 0)


def norm_body(t_ref, u_ref, x_ref, gr_ref, m_ref):
    h = x_ref[...].astype(f32) + (t_ref[...].astype(f32) + u_ref[...].astype(f32))
    scale = lax.rsqrt(jnp.mean(h * h, axis=-1, keepdims=True) + epsilon)
    m_ref[...] = (h * scale * gr_ref[1:2]).astype(bf16)


def assemble(idx, packs, full_ref):
    blk = packs[0].shape[0]
    for b, pk in enumerate(packs):
        full_ref[pl.ds(pl.multiple_of(idx[b] * blk, blk), blk), :] = pk[...]


def up_body(idx, mo_ref, mt_ref, co_ref, ct_ref, r_ref, *refs):
    packs, rest = refs[:BLOCKS], refs[BLOCKS:]
    g_ref, gp_ref, db_ref, w_ref = rest[:4]
    grads = rest[4 : 4 + BLOCKS]
    gt = rest[4 + BLOCKS]
    rows, width = mo_ref.shape
    units = w_ref.shape[1]
    assemble(idx, packs, w_ref)
    r = r_ref[:, 2:3]
    db_ref[:rows, :] = (r[:rows] * co_ref[...].astype(f32)).astype(bf16)
    db_ref[rows:, :] = (r[rows:] * ct_ref[...].astype(f32)).astype(bf16)
    tile = 256

    def step(i, carry):
        cols = pl.ds(pl.multiple_of(i * tile, tile), tile)
        w = w_ref[:, cols]
        for half, m_ref in ((0, mo_ref), (1, mt_ref)):
            span = pl.ds(half * rows, rows)
            u = mm(m_ref[...], w)
            u2 = u * u
            th = jnp.tanh(gelu_scale * (u + gelu_cubic * (u2 * u)))
            half_up = 0.5 * (1.0 + th)
            g_ref[span, cols] = (u * half_up).astype(bf16)
            gp_ref[span, cols] = half_up + (0.5 * u) * (1.0 - th * th) * (
                gelu_scale * (1.0 + 3.0 * gelu_cubic * u2)
            )
        gt[cols, :] = g_ref[:, cols].T
        return carry

    lax.fori_loop(0, units // tile, step, 0)
    blk = units // BLOCKS
    for b, ref in enumerate(grads):
        off = pl.multiple_of(idx[b] * blk, blk)
        ref[...] = mm(gt[pl.ds(off, blk), :], db_ref[...]).astype(bf16)


def down_body(idx, mo_ref, mt_ref, db_ref, gp_ref, wu_ref, *refs):
    packs, rest = refs[:BLOCKS], refs[BLOCKS:]
    w_ref, dmo_ref, dmt_ref = rest[:3]
    grads = rest[3 : 3 + BLOCKS]
    du, mt = rest[3 + BLOCKS :]
    rows, width = mo_ref.shape
    assemble(idx, packs, w_ref)
    units = w_ref.shape[0]
    tile = 256

    def step(i, carry):
        cols = pl.ds(pl.multiple_of(i * tile, tile), tile)
        dg = mm(db_ref[...], w_ref[cols, :], NT)
        du[:, cols] = (dg * gp_ref[:, cols]).astype(bf16)
        return carry

    lax.fori_loop(0, units // tile, step, 0)

    def step2(i, carry):
        cols = pl.ds(pl.multiple_of(i * tile, tile), tile)
        dm = mm(du[...], wu_ref[cols, :], NT).astype(bf16)
        dmo_ref[:, cols] = dm[:rows]
        dmt_ref[:, cols] = dm[rows:]
        mt[cols, :rows] = mo_ref[:, cols].T
        mt[cols, rows:] = mt_ref[:, cols].T
        return carry

    lax.fori_loop(0, width // tile, step2, 0)
    blk = width // BLOCKS
    for b, ref in enumerate(grads):
        off = pl.multiple_of(idx[b] * blk, blk)
        ref[...] = mm(mt[pl.ds(off, blk), :], du[...]).astype(bf16)


def branch_body(g_ref, w_ref, bo_ref, bt_ref):
    rows, width = bo_ref.shape
    tile = 256

    def step(i, carry):
        cols = pl.ds(pl.multiple_of(i * tile, tile), tile)
        res = mm(g_ref[...], w_ref[:, cols]).astype(bf16)
        bo_ref[:, cols] = res[:rows]
        bt_ref[:, cols] = res[rows:]
        return carry

    lax.fori_loop(0, width // tile, step, 0)


def hidden_grad_body(dt_ref, du_ref, bt_ref, bu_ref, x_ref, c_ref, r_ref, gr_ref, da_ref, dh_ref, gg_ref):
    dm = dt_ref[...].astype(f32) + du_ref[...].astype(f32)
    h = x_ref[...].astype(f32) + (bt_ref[...].astype(f32) + bu_ref[...].astype(f32))
    rows = h.shape[0]
    n = lax.rsqrt(jnp.mean(h * h, axis=-1, keepdims=True) + epsilon)
    t = dm * gr_ref[1:2]
    dh = n * t - h * (n * n * n) * jnp.mean(t * h, axis=-1, keepdims=True)
    dh_ref[...] = dh
    de = r_ref[:rows, 2:3] * c_ref[...].astype(f32)
    da_ref[...] = (de + dh).astype(bf16)
    gg_ref[...] = jnp.sum(dm * h * n, axis=0, keepdims=True)


def result_body(at_ref, au_ref, mt_ref, mu_ref, x_ref, c_ref, r_ref, e_ref, dr_ref, rg_ref):
    branch = (at_ref[...].astype(f32) + au_ref[...].astype(f32)) + (
        mt_ref[...].astype(f32) + mu_ref[...].astype(f32)
    )
    rows = branch.shape[0]
    e_ref[...] = (r_ref[:rows, 2:3] * branch).astype(bf16)
    dr = jnp.sum(c_ref[...].astype(f32) * branch, axis=-1, keepdims=True)
    dr_ref[...] = jnp.broadcast_to(dr, dr_ref.shape)
    rg_ref[...] = jnp.sum(x_ref[...].astype(f32) * dr, axis=0, keepdims=True)


def attn_bwd_body(
    idx, meta, xo_ref, xt_ref, a_ref, qkv_ref, p_ref, o_ref, dao_ref, dat_ref, wq_ref, wo_ref,
    gr_ref, mg_ref, rg_ref, *refs
):
    dxo_ref, dxt_ref = refs[:2]
    grads = refs[2 : 2 + BLOCKS]
    da, dqkv, at, ot, acc, col = refs[2 + BLOCKS :]
    rows, width = xo_ref.shape
    part = width // 4
    qcols = 3 * part
    heads = part // HEAD_DIM
    score_scale = HEAD_DIM ** (-0.5)
    da[:rows, :] = dao_ref[...]
    da[rows:, :] = dat_ref[...]
    for half in range(2):
        span = pl.ds(half * rows, rows)
        dmix = mm(da[span, :], wo_ref[...], NT).astype(bf16)
        for h in range(heads):
            lo, hi = h * HEAD_DIM, (h + 1) * HEAD_DIM
            q = qkv_ref[span, lo:hi]
            k = qkv_ref[span, part + lo : part + hi]
            v = qkv_ref[span, 2 * part + lo : 2 * part + hi]
            do = dmix[:, lo:hi]
            p = p_ref[half * heads + h]
            dp = mm(do, v, NT)
            ds = (p * (dp - jnp.sum(p * dp, axis=-1, keepdims=True))).astype(bf16)
            dqkv[span, lo:hi] = (mm(ds, k) * score_scale).astype(bf16)
            dqkv[span, part + lo : part + hi] = (mm(ds, q, TN) * score_scale).astype(bf16)
            dqkv[span, 2 * part + lo : 2 * part + hi] = mm(p.astype(bf16), do, TN).astype(bf16)
    for half, ref in ((0, dxo_ref), (1, dxt_ref)):
        x_ref = (xo_ref, xt_ref)[half]
        span = pl.ds(half * rows, rows)
        x = x_ref[...].astype(f32)
        scale = lax.rsqrt(jnp.mean(x * x, axis=-1, keepdims=True) + epsilon)
        d = mm(dqkv[span, :], wq_ref[...], NT)
        ref[...] = d.astype(bf16)
        acc[half : half + 1, :] = jnp.sum(d * x * scale, axis=0, keepdims=True)
    first = jnp.where(meta[2] == 0, 1.0, 0.0).astype(f32)
    acc[0:1, :] = acc[0:1, :] + acc[1:2, :]
    acc[1:2, :] = mg_ref[...] * first
    acc[2:3, :] = rg_ref[...] * first
    acc[3:8, :] = jnp.zeros((5, width), f32)
    tile = 256

    def flip(i, carry):
        cols = pl.ds(pl.multiple_of(i * tile, tile), tile)
        at[cols, :] = a_ref[:, cols].T
        for sub in range(2):
            c2 = pl.ds(pl.multiple_of(i * tile + sub * 128, 128), 128)
            wide = jnp.concatenate([acc[:, c2], jnp.zeros((120, 128), f32)], axis=0)
            col[c2, :] = wide.T.astype(bf16)
        return carry

    lax.fori_loop(0, width // tile, flip, 0)
    ot[...] = o_ref[...].T
    blk = width // BLOCKS
    ob = part // BLOCKS
    for b, ref in enumerate(grads):
        s = idx[b]
        off = pl.multiple_of(s * blk, blk)
        ref[:, :qcols] = mm(at[pl.ds(off, blk), :], dqkv[...]).astype(bf16)
        ref[:, qcols : qcols + 128] = col[pl.ds(off, blk), :]
        og = mm(ot[pl.ds(pl.multiple_of(s * ob, ob), ob), :], da[...]).astype(bf16)
        for j in range(4):
            ref[j * ob : (j + 1) * ob, qcols + 128 :] = og[:, j * part : (j + 1) * part]


def input_grad_body(t_ref, u_ref, x_ref, dh_ref, dr_ref, gr_ref, dx_ref):
    d = t_ref[...].astype(f32) + u_ref[...].astype(f32)
    x = x_ref[...].astype(f32)
    m = lax.rsqrt(jnp.mean(x * x, axis=-1, keepdims=True) + epsilon)
    s = d * gr_ref[0:1]
    dxn = m * s - x * (m * m * m) * jnp.mean(s * x, axis=-1, keepdims=True)
    dx_ref[...] = (dxn + dh_ref[...] + dr_ref[:, 0:1] * gr_ref[2:3]).astype(bf16)


def flip_bit(v, axis, size, mask):
    return lax.ppermute(v, axis, [(i, i ^ mask) for i in range(size)])


def swap_core(v):
    return flip_bit(v, "grp", 4, 1)


def swap_pair(v):
    return flip_bit(v, "grp", 4, 2)


def swap_side(v, seqs):
    return flip_bit(v, "seq", seqs, 1)


def ring(v, seqs):
    return lax.ppermute(v, "seq", [(i, (i + 2) % seqs) for i in range(seqs)])


def reorder(parts, member):
    low = (member & 1) == 1
    high = (member & 2) == 2
    res = []
    for j in range(4):
        straight = jnp.where(low, parts[j ^ 1], parts[j])
        crossed = jnp.where(low, parts[j ^ 3], parts[j ^ 2])
        res.append(jnp.where(high, crossed, straight))
    return res


def exchange(chunks, member):
    rel = reorder(chunks, member)
    got = [rel[0]] + [flip_bit(rel[k], "grp", 4, k) for k in range(1, 4)]
    return reorder(got, member)


def gather_blocks(pack, seqs):
    if seqs == BLOCKS:
        blocks = []
        for k in range(BLOCKS // 2):
            blocks.append(pack)
            blocks.append(swap_side(pack, seqs))
            if k < BLOCKS // 2 - 1:
                pack = ring(pack, seqs)
        return blocks
    full = lax.all_gather(pack, "seq", axis=0, tiled=True)
    return list(full.reshape((BLOCKS, -1) + full.shape[1:]))


def scatter_blocks(blocks, seqs):
    if seqs == BLOCKS:
        acc = None
        for k in (1, 2, 3, 0):
            term = blocks[2 * k].astype(f32) + swap_side(blocks[2 * k + 1], seqs).astype(f32)
            if acc is not None:
                term = term + ring(acc, seqs).astype(f32)
            acc = term.astype(bf16)
        return term
    full = jnp.concatenate(blocks, axis=0)
    return lax.psum_scatter(full.astype(f32), "seq", scatter_dimension=0, tiled=True)


def sum_pair(own, other):
    t = (own.astype(f32) + swap_core(other).astype(f32)).astype(bf16)
    return t, swap_pair(t)


def on_device(
    tokens,
    segments,
    routed,
    qkv_weight,
    out_weight,
    up_weight,
    down_weight,
    attn_gain,
    mlp_gain,
    router_weight,
    cotangent,
):
    groups, seqs = lax.axis_size("grp"), lax.axis_size("seq")
    member, place = lax.axis_index("grp"), lax.axis_index("seq")
    seq_dev, span, width = tokens.shape
    rows = routed.shape[1]
    units = down_weight.shape[0] * groups * seqs
    if groups != 4 or seq_dev != 2:
        raise ValueError("mesh")
    native = seqs != BLOCKS
    part, ff = width // 4, units // 4
    core, pair = member & 1, member >> 1
    head_of = (0, 2, 1, 3)
    mine = qkv_weight.shape[0]
    wide = mine * groups

    gains = jnp.stack([attn_gain, mlp_gain, router_weight], axis=1)
    gains = jnp.pad(gains, ((0, 0), (0, 125)))
    qkv_view = qkv_weight.reshape(mine, 3, 4, 4, HEAD_DIM)
    qkv_chunks = [
        jnp.concatenate([qkv_view[:, :, :, p].reshape(mine, 3 * part), gains], axis=1)
        for p in head_of
    ]
    qkv_rows = jnp.concatenate(exchange(qkv_chunks, member), axis=0)
    if native:
        out_full = lax.all_gather(out_weight, ("seq", "grp"), axis=0, tiled=True)
        out_view = out_full.reshape(4, 4, HEAD_DIM, width)
        head_set = 2 * core + pair
        out_rows = lax.dynamic_index_in_dim(out_view, head_set, 1, keepdims=False)
        out_rows = out_rows.reshape(BLOCKS, part // BLOCKS, width)
        out_parts = [
            jnp.concatenate([o[:, j * part : (j + 1) * part] for j in range(4)], axis=0)
            for o in out_rows
        ]
        blocks = gather_blocks(qkv_rows, seqs)
        attn_packs = [jnp.concatenate(both, axis=1) for both in zip(blocks, out_parts)]
        order = jnp.arange(BLOCKS, dtype=jnp.int32)
    else:
        swaps = [
            (s * 4 + g, (s ^ 1) * 4 + (g ^ 1)) for s in range(seqs) for g in range(4) if (s ^ g) & 1
        ]
        moved = lax.ppermute(out_weight, ("seq", "grp"), swaps)
        out_own = jnp.where(((place ^ member) & 1) == 1, moved, out_weight)
        out_part = jnp.concatenate([out_own[:, j * part : (j + 1) * part] for j in range(4)], axis=0)
        attn_packs = gather_blocks(jnp.concatenate([qkv_rows, out_part], axis=1), seqs)
        order = jnp.stack(
            [((place ^ r) - 2 * k) % seqs for k in range(BLOCKS // 2) for r in range(2)]
        ).astype(jnp.int32)
    up_view = up_weight.reshape(mine, seqs, 4, ff // seqs)
    up_chunks = [up_view[:, :, j].reshape(mine, ff) for j in range(4)]
    up_rows = jnp.concatenate(exchange(up_chunks, member), axis=0)
    up_packs = gather_blocks(up_rows, seqs)
    down_packs = gather_blocks(down_weight, seqs)

    flip = core == 1
    meta = jnp.stack([core, member * span, pair]).astype(jnp.int32)
    pos = jnp.where(flip, routed[::-1], routed)
    starts = jnp.stack(
        [jnp.sum((segments < v).astype(jnp.int32), axis=1) for v in range(1, SEG_COUNT)], axis=0
    )
    seg = jnp.sum((routed[None] >= starts[:, :, None]).astype(jnp.int32), axis=0)
    seg = jnp.where(flip, seg[::-1], seg)
    pos_col, pos_row = pos[:, :, None], pos[:, None, :]
    seg_col, seg_row = seg[:, :, None], seg[:, None, :]
    half = out((rows, width), bf16)

    def fetch(source, name):
        own, other = call(
            pick_body, (meta, pos_col, source), (half, half), smem=1,
            flops=4 * rows * span * width, name=name,
        )
        t = own + swap_core(other)
        full = t + swap_pair(t)
        return full, swap_core(full)

    x_own, x_oth = fetch(tokens, "pick_tokens")
    c_own, c_oth = fetch(cotangent, "pick_cotangent")

    both = 2 * rows
    a, qkv, probs, mix, ba_o, ba_t, w_qkv, w_out, gain_rows, r = call(
        attn_fwd_body,
        (order, x_own, x_oth, seg_col, seg_row, *attn_packs),
        (
            out((both, width), bf16),
            out((both, 3 * part), bf16),
            out((2 * part // HEAD_DIM, rows, rows), f32),
            out((both, part), bf16),
            half,
            half,
            out((width, 3 * part), bf16),
            out((part, width), bf16),
            out((8, width), f32),
            out((both, 128), f32),
        ),
        scratch=[pltpu.VMEM((width, 128), bf16)],
        smem=1,
        flops=2 * both * width * width,
        name="attn_fwd",
    )
    ba1, ba2 = sum_pair(ba_o, ba_t)
    (m_own,) = call(norm_body, (ba1, ba2, x_own, gain_rows), (half,), name="norm_two")
    m_oth = swap_core(m_own)
    block = out((width // BLOCKS, width), bf16)
    g, gp, db, w_up, *down_grads = call(
        up_body,
        (order, m_own, m_oth, c_own, c_oth, r, *up_packs),
        (
            out((both, ff), bf16),
            out((both, ff), f32),
            out((both, width), bf16),
            out((width, ff), bf16),
            *([out((ff // BLOCKS, width), bf16)] * BLOCKS),
        ),
        scratch=[pltpu.VMEM((ff, both), bf16)],
        smem=1,
        flops=4 * both * width * ff,
        name="up",
    )
    down_grad = scatter_blocks(down_grads, seqs)
    w_down, dm_o, dm_t, *up_grads = call(
        down_body,
        (order, m_own, m_oth, db, gp, w_up, *down_packs),
        (
            out((ff, width), bf16),
            half,
            half,
            *([out((width // BLOCKS, ff), bf16)] * BLOCKS),
        ),
        scratch=[pltpu.VMEM((both, ff), bf16), pltpu.VMEM((width, both), bf16)],
        smem=1,
        flops=6 * both * width * ff,
        name="down",
    )
    dm1, dm2 = sum_pair(dm_o, dm_t)
    up_sum = scatter_blocks(up_grads, seqs)
    bm_o, bm_t = call(
        branch_body, (g, w_down), (half, half), flops=2 * both * width * ff, name="branch"
    )
    bm1, bm2 = sum_pair(bm_o, bm_t)

    line = out((1, width), f32)
    da_own, dh, mlp_line = call(
        hidden_grad_body,
        (dm1, dm2, ba1, ba2, x_own, c_own, r, gain_rows),
        (half, out((rows, width), f32), line),
        name="hidden_grad",
    )
    da_oth = swap_core(da_own)
    e_own, dr, router_line = call(
        result_body,
        (ba1, ba2, bm1, bm2, x_own, c_own, r),
        (half, out((rows, 128), f32), line),
        name="result",
    )
    dx_o, dx_t, *attn_grads = call(
        attn_bwd_body,
        (
            order, meta, x_own, x_oth, a, qkv, probs, mix, da_own, da_oth, w_qkv, w_out,
            gain_rows, mlp_line, router_line,
        ),
        (half, half, *([out((width // BLOCKS, width + 128), bf16)] * BLOCKS)),
        scratch=[
            pltpu.VMEM((both, width), bf16),
            pltpu.VMEM((both, 3 * part), bf16),
            pltpu.VMEM((width, both), bf16),
            pltpu.VMEM((part, both), bf16),
            pltpu.VMEM((8, width), f32),
            pltpu.VMEM((width, 128), bf16),
        ],
        smem=2,
        flops=4 * both * width * width,
        name="attn_bwd",
    )
    dx1, dx2 = sum_pair(dx_o, dx_t)
    (dx_own,) = call(
        input_grad_body, (dx1, dx2, x_own, dh, dr, gain_rows), (half,), name="input_grad"
    )
    dx_oth = swap_core(dx_own)
    e_oth = swap_core(e_own)

    def place_rows(base, own, other, name):
        return call(
            place_body, (meta, pos_row, base, own, other), (out(base.shape, bf16),), smem=1,
            flops=4 * rows * span * width, name=name,
        )[0]

    mixed = place_rows(tokens, e_own, e_oth, "place_mixed")
    input_grad = place_rows(cotangent, dx_own, dx_oth, "place_input_grad")

    up_back = exchange([up_sum[j * mine : (j + 1) * mine] for j in range(4)], member)
    up_grad = jnp.stack([v.reshape(mine, seqs, ff // seqs) for v in up_back], axis=2)
    up_grad = up_grad.reshape(mine, units)
    if native:
        out_blocks = [
            jnp.concatenate(
                [
                    b[j * part // BLOCKS : (j + 1) * part // BLOCKS, 3 * part + 128 :]
                    for j in range(4)
                ],
                axis=1,
            )
            for b in attn_grads
        ]
        attn_sum = scatter_blocks([b[:, : 3 * part + 128] for b in attn_grads], seqs)
        out_mine = jnp.concatenate(out_blocks, axis=0).astype(f32).reshape(4, HEAD_DIM, width)
        slots = (jnp.arange(4) == head_set).astype(f32)[None, :, None, None]
        out_all = (out_mine[:, None] * slots).reshape(width, width)
        out_grad = lax.psum_scatter(out_all, ("seq", "grp"), scatter_dimension=0, tiled=True)
    else:
        attn_sum = scatter_blocks(attn_grads, seqs)
        og = attn_sum[:, 3 * part + 128 :]
        og = jnp.concatenate([og[j * mine : (j + 1) * mine] for j in range(4)], axis=1)
        moved = lax.ppermute(og, ("seq", "grp"), swaps)
        out_grad = jnp.where(((place ^ member) & 1) == 1, moved, og)
    back = exchange(
        [attn_sum[j * mine : (j + 1) * mine, : 3 * part + 128] for j in range(4)], member
    )
    by_head = [back[j][:, : 3 * part].reshape(mine, 3, 4, HEAD_DIM) for j in range(4)]
    qkv_grad = jnp.stack([by_head[head_of.index(p)] for p in range(4)], axis=3)
    qkv_grad = qkv_grad.reshape(mine, 3 * width)
    small = sum(back[j][:, 3 * part : 3 * part + 3] for j in range(4))
    return (
        mixed,
        input_grad,
        qkv_grad,
        out_grad,
        up_grad,
        down_grad,
        small[:, 0],
        small[:, 1],
        small[:, 2],
    )


def solution(mesh):
    placed = (
        P("seq", "grp", None),
        P("seq", None),
        P("seq", None),
        P(("seq", "grp"), None),
        P(("seq", "grp"), None),
        P(("seq", "grp"), None),
        P(("seq", "grp"), None),
        P(("seq", "grp")),
        P(("seq", "grp")),
        P(("seq", "grp")),
        P("seq", "grp", None),
    )
    return jax.shard_map(
        on_device,
        mesh=mesh,
        in_specs=placed,
        out_specs=(
            P("seq", "grp", None),
            P("seq", "grp", None),
            P(("seq", "grp"), None),
            P(("seq", "grp"), None),
            P(("seq", "grp"), None),
            P(("seq", "grp"), None),
            P(("seq", "grp")),
            P(("seq", "grp")),
            P(("seq", "grp")),
        ),
        check_vma=False,
    )
```

```python
import jax
import jax.numpy as jnp
from jax import lax
from jax.experimental import pallas as pl
from jax.experimental.pallas import tpu as pltpu
from jax.sharding import PartitionSpec as P

HEAD_DIM = 64
SEG_COUNT = 4
BLOCKS = 8
epsilon = 1e-06
masked = -1e30
f32 = jnp.float32
bf16 = jnp.bfloat16
gelu_scale = 0.7978845608028654
gelu_cubic = 0.044715

NN = (((1,), (0,)), ((), ()))
NT = (((1,), (1,)), ((), ()))
TN = (((0,), (0,)), ((), ()))


def mm(a, b, dims=NN):
    return lax.dot_general(a, b, dims, preferred_element_type=f32)


VM = pl.BlockSpec(memory_space=pltpu.VMEM)
SM = pl.BlockSpec(memory_space=pltpu.SMEM)
MIB = 1024 * 1024


def call(
    body, args, outs, scratch=(), smem=0, flops=0, name=None, limit=8, keep=True, keep_out=True,
    cold=(),
):
    moved = sum(a.size * a.dtype.itemsize for a in args)
    moved += sum(o.size * o.dtype.itemsize for o in outs)
    if keep:
        args = tuple(
            a
            if n < smem
            else pltpu.with_memory_space_constraint(a, pltpu.HBM if n in cold else pltpu.VMEM)
            for n, a in enumerate(args)
        )
    if keep and keep_out:
        shapes = tuple(pltpu.VMEM(o.shape, o.dtype) for o in outs)
    else:
        shapes = tuple(outs)
    return pl.pallas_call(
        body,
        out_shape=shapes,
        in_specs=[SM] * smem + [VM] * (len(args) - smem),
        out_specs=tuple([VM] * len(outs)),
        scratch_shapes=list(scratch),
        cost_estimate=pl.CostEstimate(flops=flops, bytes_accessed=moved, transcendentals=0),
        compiler_params=pltpu.CompilerParams(vmem_limit_bytes=limit * MIB),
        name=name,
    )(*args)


def out(shape, dtype):
    return jax.ShapeDtypeStruct(shape, dtype)


def pick_body(meta, pos_ref, src_ref, own_ref, oth_ref):
    rows, span = pos_ref.shape[1], src_ref.shape[1]
    core, base = meta[0], meta[1]
    lane = lax.broadcasted_iota(jnp.int32, (rows, span), 1) + base
    for half, ref in ((0, own_ref), (1, oth_ref)):
        seq = core if half == 0 else 1 - core
        hot = jnp.where(pos_ref[half] == lane, 1.0, 0.0).astype(bf16)
        src = src_ref[seq]
        ref[...] = mm(hot, src).astype(bf16)


def place_body(meta, pos_ref, base_ref, own_ref, oth_ref, out_ref):
    rows, span = pos_ref.shape[2], base_ref.shape[1]
    core, base = meta[0], meta[1]
    row = lax.broadcasted_iota(jnp.int32, (span, rows), 0) + base
    for half, ref in ((0, own_ref), (1, oth_ref)):
        seq = core if half == 0 else 1 - core
        hot = jnp.where(pos_ref[half] == row, 1.0, 0.0).astype(bf16)
        added = mm(hot, ref[...])
        out_ref[seq] = (base_ref[seq].astype(f32) + added).astype(bf16)


def attn_fwd_body(
    idx, xo_ref, xt_ref, segc_ref, segr_ref, *refs
):
    packs = refs[:BLOCKS]
    a_ref, qkv_ref, p_ref, o_ref, bo_ref, bt_ref, wq_ref, wo_ref, gr_ref, r_ref, gcol = refs[BLOCKS:]
    rows, width = xo_ref.shape
    part = width // 4
    qcols = 3 * part
    blk = width // BLOCKS
    ob = part // BLOCKS
    for b, pk in enumerate(packs):
        s = idx[b]
        off = pl.multiple_of(s * blk, blk)
        wq_ref[pl.ds(off, blk), :] = pk[:, :qcols]
        gcol[pl.ds(off, blk), :] = pk[:, qcols : qcols + 128]
        off2 = pl.multiple_of(s * ob, ob)
        for j in range(4):
            wo_ref[pl.ds(off2, ob), j * part : (j + 1) * part] = pk[
                j * ob : (j + 1) * ob, qcols + 128 :
            ]
    eye = (
        lax.broadcasted_iota(jnp.int32, (8, 128), 0) == lax.broadcasted_iota(jnp.int32, (8, 128), 1)
    ).astype(f32).astype(bf16)
    gr = mm(eye, gcol[...], NT)
    gr_ref[...] = gr
    gain = gr[0:1]
    for half, x_ref in ((0, xo_ref), (1, xt_ref)):
        span = pl.ds(half * rows, rows)
        xb = x_ref[...]
        x = xb.astype(f32)
        scale = lax.rsqrt(jnp.mean(x * x, axis=-1, keepdims=True) + epsilon)
        a_ref[span, :] = (x * scale * gain).astype(bf16)
        r_ref[span, :] = mm(xb, gcol[...])

    def project(i, carry):
        cols = pl.ds(pl.multiple_of(i * part, part), part)
        qkv_ref[:, cols] = mm(a_ref[...], wq_ref[:, cols]).astype(bf16)
        return carry

    lax.fori_loop(0, 3, project, 0)
    ri = lax.broadcasted_iota(jnp.int32, (rows, rows), 0)
    ci = lax.broadcasted_iota(jnp.int32, (rows, rows), 1)
    causal = ci <= ri
    heads = part // HEAD_DIM
    score_scale = HEAD_DIM ** (-0.5)
    for half in range(2):
        allowed = causal & (segc_ref[half] == segr_ref[half])
        span = pl.ds(half * rows, rows)
        for h in range(heads):
            q = qkv_ref[span, h * HEAD_DIM : (h + 1) * HEAD_DIM]
            k = qkv_ref[span, part + h * HEAD_DIM : part + (h + 1) * HEAD_DIM]
            v = qkv_ref[span, 2 * part + h * HEAD_DIM : 2 * part + (h + 1) * HEAD_DIM]
            logits = jnp.where(allowed, mm(q, k, NT) * score_scale, masked)
            e = jnp.exp(logits - jnp.max(logits, axis=-1, keepdims=True))
            p = e / jnp.sum(e, axis=-1, keepdims=True)
            p_ref[half * heads + h] = p
            o_ref[span, h * HEAD_DIM : (h + 1) * HEAD_DIM] = mm(p.astype(bf16), v).astype(bf16)

    def project_out(i, carry):
        cols = pl.ds(pl.multiple_of(i * part, part), part)
        res = mm(o_ref[...], wo_ref[:, cols]).astype(bf16)
        bo_ref[:, cols] = res[:rows]
        bt_ref[:, cols] = res[rows:]
        return carry

    lax.fori_loop(0, 4, project_out, 0)


def norm_body(t_ref, u_ref, x_ref, gr_ref, m_ref):
    h = x_ref[...].astype(f32) + (t_ref[...].astype(f32) + u_ref[...].astype(f32))
    scale = lax.rsqrt(jnp.mean(h * h, axis=-1, keepdims=True) + epsilon)
    m_ref[...] = (h * scale * gr_ref[1:2]).astype(bf16)


def turn_body(a_ref, o_ref, at_ref, ot_ref):
    tile = 256

    def step(i, carry):
        cols = pl.ds(pl.multiple_of(i * tile, tile), tile)
        at_ref[cols, :] = a_ref[:, cols].T
        return carry

    lax.fori_loop(0, a_ref.shape[1] // tile, step, 0)
    ot_ref[...] = o_ref[...].T


def mlp_body(idx, mo_ref, mt_ref, co_ref, ct_ref, r_ref, *refs):
    packs, rest = refs[:BLOCKS], refs[BLOCKS:]
    g_ref, du_ref, db_ref, wu_ref, wd_ref, dmo_ref, dmt_ref = rest
    rows, width = mo_ref.shape
    units = wu_ref.shape[1]
    blk, sub = width // BLOCKS, units // BLOCKS
    for b in range(BLOCKS):
        wu_ref[pl.ds(pl.multiple_of(idx[b] * blk, blk), blk), :] = packs[b][:, :units]
        wd_ref[pl.ds(pl.multiple_of(idx[b] * sub, sub), sub), :] = packs[b][:, units:]
    r = r_ref[:, 2:3]
    db_ref[:rows, :] = (r[:rows] * co_ref[...].astype(f32)).astype(bf16)
    db_ref[rows:, :] = (r[rows:] * ct_ref[...].astype(f32)).astype(bf16)
    tile = 256

    def step(i, carry):
        cols = pl.ds(pl.multiple_of(i * tile, tile), tile)
        for half, m_ref in ((0, mo_ref), (1, mt_ref)):
            span = pl.ds(half * rows, rows)
            u = mm(m_ref[...], wu_ref[:, cols])
            u2 = u * u
            th = jnp.tanh(gelu_scale * (u + gelu_cubic * (u2 * u)))
            half_up = 0.5 * (1.0 + th)
            g_ref[span, cols] = (u * half_up).astype(bf16)
            slope = half_up + (0.5 * u) * (1.0 - th * th) * (
                gelu_scale * (1.0 + 3.0 * gelu_cubic * u2)
            )
            dg = mm(db_ref[span, :], wd_ref[cols, :], NT)
            du_ref[span, cols] = (dg * slope).astype(bf16)
        return carry

    lax.fori_loop(0, units // tile, step, 0)

    def step2(i, carry):
        cols = pl.ds(pl.multiple_of(i * tile, tile), tile)
        dm = mm(du_ref[...], wu_ref[cols, :], NT).astype(bf16)
        dmo_ref[:, cols] = dm[:rows]
        dmt_ref[:, cols] = dm[rows:]
        return carry

    lax.fori_loop(0, width // tile, step2, 0)


def up_grad_body(idx, du_ref, mo_ref, mt_ref, wu_ref, gcol, *refs):
    col_ref, ups, (flip,) = refs[0], refs[1 : 1 + BLOCKS], refs[1 + BLOCKS :]
    rows, width = mo_ref.shape
    blk = width // BLOCKS
    tile = 256

    def step(i, carry):
        cols = pl.ds(pl.multiple_of(i * tile, tile), tile)
        flip[cols, :rows] = mo_ref[:, cols].T
        flip[cols, rows:] = mt_ref[:, cols].T
        return carry

    lax.fori_loop(0, width // tile, step, 0)
    for b, ref in enumerate(ups):
        off = pl.ds(pl.multiple_of(idx[b] * blk, blk), blk)
        grad = mm(flip[off, :], du_ref[...])
        ref[...] = grad.astype(bf16)
        gain = jnp.sum(grad * wu_ref[off, :].astype(f32), axis=-1, keepdims=True)
        gain = gain / gcol[off, 1:2].astype(f32)
        col_ref[off, :] = jnp.broadcast_to(gain, (blk, 128))


def down_grad_body(
    idx, g_ref, db_ref, wd_ref, col_in, ao_ref, at_ref, co_ref, ct_ref, xo_ref, xt_ref, *refs
):
    bo_ref, bt_ref, col_ref = refs[:3]
    downs, (flip,) = refs[3 : 3 + BLOCKS], refs[3 + BLOCKS :]
    rows, width = bo_ref.shape
    units = wd_ref.shape[0]
    sub = units // BLOCKS
    tile = 256

    def step(i, carry):
        cols = pl.ds(pl.multiple_of(i * tile, tile), tile)
        res = mm(g_ref[...], wd_ref[:, cols])
        bo_ref[:, cols] = res[:rows].astype(bf16)
        bt_ref[:, cols] = res[rows:].astype(bf16)
        flip[cols, :] = g_ref[:, cols].T
        own, other = carry
        own += jnp.sum(
            (res[:rows] + ao_ref[:, cols].astype(f32)) * co_ref[:, cols].astype(f32),
            axis=-1, keepdims=True,
        )
        other += jnp.sum(
            (res[rows:] + at_ref[:, cols].astype(f32)) * ct_ref[:, cols].astype(f32),
            axis=-1, keepdims=True,
        )
        return own, other

    zero = jnp.zeros((rows, 1), f32)
    dots = lax.fori_loop(0, width // tile, step, (zero, zero))
    for b, ref in enumerate(downs):
        off = pl.multiple_of(idx[b] * sub, sub)
        ref[...] = mm(flip[pl.ds(off, sub), :], db_ref[...]).astype(bf16)
    lane = lax.broadcasted_iota(jnp.int32, (rows, 128), 1)
    route = jnp.zeros((width, 128), f32)
    for d, x_ref in zip(dots, (xo_ref, xt_ref)):
        high = d.astype(bf16).astype(f32)
        two = jnp.where(lane == 0, high, jnp.where(lane == 1, d - high, 0.0)).astype(bf16)
        route += mm(x_ref[...], two, TN)
    total = jnp.sum(route[:, :2], axis=-1, keepdims=True)
    wide = lax.broadcasted_iota(jnp.int32, (width, 128), 1)
    col_ref[...] = jnp.where(wide == 1, col_in[...], jnp.where(wide == 2, total, 0.0))


def hidden_grad_body(dt_ref, du_ref, bt_ref, bu_ref, x_ref, c_ref, r_ref, gr_ref, da_ref, dh_ref):
    dm = dt_ref[...].astype(f32) + du_ref[...].astype(f32)
    h = x_ref[...].astype(f32) + (bt_ref[...].astype(f32) + bu_ref[...].astype(f32))
    rows = h.shape[0]
    n = lax.rsqrt(jnp.mean(h * h, axis=-1, keepdims=True) + epsilon)
    t = dm * gr_ref[1:2]
    dh = n * t - h * (n * n * n) * jnp.mean(t * h, axis=-1, keepdims=True)
    dh_ref[...] = dh
    de = r_ref[:rows, 2:3] * c_ref[...].astype(f32)
    da_ref[...] = (de + dh).astype(bf16)


def result_body(at_ref, au_ref, mt_ref, mu_ref, c_ref, r_ref, e_ref, dr_ref):
    branch = (at_ref[...].astype(f32) + au_ref[...].astype(f32)) + (
        mt_ref[...].astype(f32) + mu_ref[...].astype(f32)
    )
    rows = branch.shape[0]
    e_ref[...] = (r_ref[:rows, 2:3] * branch).astype(bf16)
    dr = jnp.sum(c_ref[...].astype(f32) * branch, axis=-1, keepdims=True)
    dr_ref[...] = jnp.broadcast_to(dr, dr_ref.shape)


def attn_bwd_body(
    idx, at_ref, ot_ref, qkv_ref, p_ref, dao_ref, dat_ref, wq_ref, wo_ref, gcol, col_ref, *refs
):
    dqkv = refs[0]
    grads = refs[1 : 1 + BLOCKS]
    (da,) = refs[1 + BLOCKS :]
    rows, width = dao_ref.shape
    part = width // 4
    qcols = 3 * part
    heads = part // HEAD_DIM
    score_scale = HEAD_DIM ** (-0.5)
    da[:rows, :] = dao_ref[...]
    da[rows:, :] = dat_ref[...]
    for half in range(2):
        span = pl.ds(half * rows, rows)
        dmix = mm(da[span, :], wo_ref[...], NT).astype(bf16)
        for h in range(heads):
            lo, hi = h * HEAD_DIM, (h + 1) * HEAD_DIM
            q = qkv_ref[span, lo:hi]
            k = qkv_ref[span, part + lo : part + hi]
            v = qkv_ref[span, 2 * part + lo : 2 * part + hi]
            do = dmix[:, lo:hi]
            p = p_ref[half * heads + h]
            dp = mm(do, v, NT)
            ds = (p * (dp - jnp.sum(p * dp, axis=-1, keepdims=True))).astype(bf16)
            dqkv[span, lo:hi] = (mm(ds, k) * score_scale).astype(bf16)
            dqkv[span, part + lo : part + hi] = (mm(ds, q, TN) * score_scale).astype(bf16)
            dqkv[span, 2 * part + lo : 2 * part + hi] = mm(p.astype(bf16), do, TN).astype(bf16)
    blk = width // BLOCKS
    ob = part // BLOCKS
    lane = lax.broadcasted_iota(jnp.int32, (blk, 128), 1)
    for b, ref in enumerate(grads):
        s = idx[b]
        off = pl.ds(pl.multiple_of(s * blk, blk), blk)
        grad = mm(at_ref[off, :], dqkv[...])
        ref[:, :qcols] = grad.astype(bf16)
        gain = jnp.sum(grad * wq_ref[off, :].astype(f32), axis=-1, keepdims=True)
        gain = gain / gcol[off, 0:1].astype(f32)
        ref[:, qcols : qcols + 128] = jnp.where(lane == 0, gain, col_ref[off, :]).astype(bf16)
        og = mm(ot_ref[pl.ds(pl.multiple_of(s * ob, ob), ob), :], da[...]).astype(bf16)
        for j in range(4):
            ref[j * ob : (j + 1) * ob, qcols + 128 :] = og[:, j * part : (j + 1) * part]


def normed_grad_body(dqkv_ref, wq_ref, do_ref, dt_ref):
    rows, width = do_ref.shape
    tile = 256

    def step(i, carry):
        cols = pl.ds(pl.multiple_of(i * tile, tile), tile)
        d = mm(dqkv_ref[...], wq_ref[cols, :], NT).astype(bf16)
        do_ref[:, cols] = d[:rows]
        dt_ref[:, cols] = d[rows:]
        return carry

    lax.fori_loop(0, width // tile, step, 0)


def input_grad_body(t_ref, u_ref, x_ref, dh_ref, dr_ref, gr_ref, dx_ref):
    d = t_ref[...].astype(f32) + u_ref[...].astype(f32)
    x = x_ref[...].astype(f32)
    m = lax.rsqrt(jnp.mean(x * x, axis=-1, keepdims=True) + epsilon)
    s = d * gr_ref[0:1]
    dxn = m * s - x * (m * m * m) * jnp.mean(s * x, axis=-1, keepdims=True)
    dx_ref[...] = (dxn + dh_ref[...] + dr_ref[:, 0:1] * gr_ref[2:3]).astype(bf16)


HEAD_OF = (0, 2, 1, 3)


def pack_body(meta, qkv_ref, up_ref, gains_ref, *refs):
    outs, (tmp,) = refs[:4], refs[4:]
    width, units = qkv_ref.shape[1] // 3, up_ref.shape[1]
    part = width // 4
    sub = units // (4 * BLOCKS)
    for j in range(4):
        p = HEAD_OF[j]
        for t in range(3):
            for z in range(4):
                src = t * width + (4 * z + p) * HEAD_DIM
                dst = t * part + z * HEAD_DIM
                tmp[j, :, dst : dst + HEAD_DIM] = qkv_ref[:, src : src + HEAD_DIM]
        tmp[j, :, 3 * part : 3 * part + 128] = gains_ref[...]
        for s in range(BLOCKS):
            dst = 3 * part + 128 + s * sub
            src = (4 * s + j) * sub
            tmp[j, :, dst : dst + sub] = up_ref[:, src : src + sub]
    for k, ref in enumerate(outs):
        ref[...] = tmp[meta[3] ^ k]


def join_body(meta, c0, c1, c2, c3, own_ref, moved_ref, down_ref, attn_ref, mlp_ref):
    mine, width = own_ref.shape
    part = width // 4
    head = 3 * part + 128
    for k, ref in enumerate((c0, c1, c2, c3)):
        off = pl.ds(pl.multiple_of((meta[3] ^ k) * mine, mine), mine)
        attn_ref[off, :head] = ref[:, :head]
        mlp_ref[off, : mlp_ref.shape[1] - width] = ref[:, head:]
    mlp_ref[:, mlp_ref.shape[1] - width :] = down_ref[...]
    take = jnp.full(own_ref.shape, meta[4]) == 1
    rows = jnp.where(take, moved_ref[...].astype(f32), own_ref[...].astype(f32)).astype(bf16)
    for j in range(4):
        attn_ref[j * mine : (j + 1) * mine, head:] = rows[:, j * part : (j + 1) * part]


def split_attn_body(meta, a_ref, b_ref, c_ref, c0, c1, c2, c3, out_ref, tmp):
    mine, width = out_ref.shape
    part = width // 4
    head = 3 * part + 128
    tmp[...] = (a_ref[...].astype(f32) + b_ref[...].astype(f32)) + c_ref[...].astype(f32)
    for k, ref in enumerate((c0, c1, c2, c3)):
        off = pl.ds(pl.multiple_of((meta[3] ^ k) * mine, mine), mine)
        ref[...] = tmp[off, :head].astype(ref.dtype)
    for j in range(4):
        out_ref[:, j * part : (j + 1) * part] = tmp[j * mine : (j + 1) * mine, head:]


def split_up_body(meta, a_ref, b_ref, c_ref, c0, c1, c2, c3, tmp):
    mine = c0.shape[0]
    tmp[...] = (a_ref[...].astype(f32) + b_ref[...].astype(f32)) + c_ref[...].astype(f32)
    for k, ref in enumerate((c0, c1, c2, c3)):
        off = pl.ds(pl.multiple_of((meta[3] ^ k) * mine, mine), mine)
        ref[...] = tmp[off, :].astype(ref.dtype)


def final_attn_body(meta, c0, c1, c2, c3, out_ref, small_ref, tmp):
    mine = out_ref.shape[0]
    width = out_ref.shape[1] // 3
    part = width // 4
    for k, ref in enumerate((c0, c1, c2, c3)):
        tmp[meta[3] ^ k] = ref[...].astype(f32)
    for j in range(4):
        for t in range(3):
            for z in range(4):
                dst = t * width + (4 * z + HEAD_OF[j]) * HEAD_DIM
                src = t * part + z * HEAD_DIM
                out_ref[:, dst : dst + HEAD_DIM] = tmp[j, :, src : src + HEAD_DIM]
    head = slice(3 * part, 3 * part + 128)
    small = (tmp[0, :, head] + tmp[1, :, head]) + (tmp[2, :, head] + tmp[3, :, head])
    wide = jnp.concatenate([small, jnp.zeros((128 - mine, 128), f32)], axis=0)
    small_ref[...] = wide.T[:8]


def final_up_body(meta, c0, c1, c2, c3, out_ref, tmp):
    sub = out_ref.shape[1] // (4 * BLOCKS)
    for k, ref in enumerate((c0, c1, c2, c3)):
        tmp[meta[3] ^ k] = ref[...].astype(f32)
    for j in range(4):
        for s in range(BLOCKS):
            dst = (4 * s + j) * sub
            out_ref[:, dst : dst + sub] = tmp[j, :, s * sub : (s + 1) * sub]


def flip_bit(v, axis, size, mask):
    return lax.ppermute(v, axis, [(i, i ^ mask) for i in range(size)])


def swap_core(v):
    return flip_bit(v, "grp", 4, 1)


def swap_pair(v):
    return flip_bit(v, "grp", 4, 2)


def swap_side(v, seqs):
    return flip_bit(v, "seq", seqs, 1)


def ring(v, seqs):
    return lax.ppermute(v, "seq", [(i, (i + 2) % seqs) for i in range(seqs)])


def reorder(parts, member):
    low = (member & 1) == 1
    high = (member & 2) == 2
    res = []
    for j in range(4):
        straight = jnp.where(low, parts[j ^ 1], parts[j])
        crossed = jnp.where(low, parts[j ^ 3], parts[j ^ 2])
        res.append(jnp.where(high, crossed, straight))
    return res


def exchange(chunks, member):
    rel = reorder(chunks, member)
    got = [rel[0]] + [flip_bit(rel[k], "grp", 4, k) for k in range(1, 4)]
    return reorder(got, member)


def native_gather(pack):
    full = lax.all_gather(pack, "seq", axis=0, tiled=True)
    return list(full.reshape((BLOCKS, -1) + full.shape[1:]))


def native_scatter(blocks):
    full = jnp.concatenate(blocks, axis=0)
    return lax.psum_scatter(full.astype(f32), "seq", scatter_dimension=0, tiled=True)


def add(*parts):
    total = parts[0].astype(f32)
    for p in parts[1:]:
        total = total + p.astype(f32)
    return total.astype(bf16)


class Flow:
    def __init__(self):
        self.v = {}

    def __getitem__(self, name):
        return self.v[name]

    def __setitem__(self, name, value):
        self.v[name] = value

    def order(self, value, name):
        token = lax.create_token()
        token, self.v[name] = lax.optimization_barrier((token, self.v[name]))
        return lax.optimization_barrier((token, value))[1]

    def sync(self, *names):
        held = [n for n in names if n in self.v]
        done = lax.optimization_barrier(tuple(self.v[n] for n in held))
        for n, value in zip(held, done):
            self.v[n] = value


def on_device(
    tokens,
    segments,
    routed,
    qkv_weight,
    out_weight,
    up_weight,
    down_weight,
    attn_gain,
    mlp_gain,
    router_weight,
    cotangent,
):
    groups, seqs = lax.axis_size("grp"), lax.axis_size("seq")
    member, place = lax.axis_index("grp"), lax.axis_index("seq")
    seq_dev, span, width = tokens.shape
    rows = routed.shape[1]
    units = down_weight.shape[0] * groups * seqs
    if groups != 4 or seq_dev != 2:
        raise ValueError("mesh")
    native = seqs != BLOCKS
    part, ff = width // 4, units // 4
    core, pair = member & 1, member >> 1
    mine = qkv_weight.shape[0]
    head = 3 * part + 128
    both = 2 * rows
    odd = (place ^ member) & 1
    meta = jnp.stack([core, member * span, pair, member, odd]).astype(jnp.int32)
    half = out((rows, width), bf16)
    v = Flow()

    queue = []

    def side(name, t, lag=3):
        if len(queue) >= lag:
            t = v.order(t, queue[-lag])
        queue.append(name)
        v[name] = swap_side(t, seqs)

    def turn(t):
        return ring(t, seqs)

    flip = core == 1
    pos = jnp.where(flip, routed[::-1], routed)
    starts = jnp.stack(
        [jnp.sum((segments < n).astype(jnp.int32), axis=1) for n in range(1, SEG_COUNT)], axis=0
    )
    seg = jnp.sum((routed[None] >= starts[:, :, None]).astype(jnp.int32), axis=0)
    seg = jnp.where(flip, seg[::-1], seg)
    pos_col, pos_row = pos[:, :, None], pos[:, None, :]
    seg_col, seg_row = seg[:, :, None], seg[:, None, :]

    def pick(source, name):
        return call(
            pick_body, (meta, pos_col, source), (half, half), smem=1,
            flops=4 * rows * span * width, name=name, keep=False, limit=24,
        )

    gains = jnp.stack([attn_gain, mlp_gain, router_weight], axis=1)
    gains = jnp.pad(gains, ((0, 0), (0, 125)))
    x_mine, x_send = pick(tokens, "pick_tokens")
    if native:
        qkv_view = qkv_weight.reshape(mine, 3, 4, 4, HEAD_DIM)
        chunks = [
            jnp.concatenate([qkv_view[:, :, :, p].reshape(mine, 3 * part), gains], axis=1)
            for p in HEAD_OF
        ]
        qkv_blocks = native_gather(jnp.concatenate(exchange(chunks, member), axis=0))
        out_full = lax.all_gather(out_weight, ("seq", "grp"), axis=0, tiled=True)
        out_view = out_full.reshape(4, 4, HEAD_DIM, width)
        head_set = 2 * core + pair
        out_rows = lax.dynamic_index_in_dim(out_view, head_set, 1, keepdims=False)
        out_rows = out_rows.reshape(BLOCKS, part // BLOCKS, width)
        attn_packs = [
            jnp.concatenate(
                [q, jnp.concatenate([o[:, j * part : (j + 1) * part] for j in range(4)], axis=0)],
                axis=1,
            )
            for q, o in zip(qkv_blocks, out_rows)
        ]
        up_view = up_weight.reshape(mine, seqs, 4, ff // seqs)
        chunks = [up_view[:, :, j].reshape(mine, ff) for j in range(4)]
        up_rows = jnp.concatenate(exchange(chunks, member), axis=0)
        mlp_packs = native_gather(jnp.concatenate([up_rows, down_weight], axis=1))
        order = jnp.arange(BLOCKS, dtype=jnp.int32)
        v["tx"] = add(x_mine, swap_core(x_send))
        v["yx"] = swap_pair(v["tx"])
        v["x"] = v["tx"] + v["yx"]
        v["xo"] = swap_core(v["x"])
        c_mine, c_send = pick(cotangent, "pick_cotangent")
        v["tc"] = add(c_mine, swap_core(c_send))
    else:
        order = jnp.stack(
            [((place ^ r) - 2 * k) % seqs for k in range(BLOCKS // 2) for r in range(2)]
        ).astype(jnp.int32)
        swaps = [
            (s * 4 + g, (s ^ 1) * 4 + (g ^ 1)) for s in range(seqs) for g in range(4) if (s ^ g) & 1
        ]
        chunk = out((mine, head + ff), bf16)
        chunks = call(
            pack_body, (meta, qkv_weight, up_weight, gains), (chunk,) * 4,
            scratch=[pltpu.VMEM((4, mine, head + ff), bf16)], smem=1, name="pack", cold=(1, 2, 3),
        )
        got = [chunks[0]] + [flip_bit(chunks[k], "grp", 4, k) for k in range(1, 4)]
        moved = lax.ppermute(out_weight, ("seq", "grp"), swaps)
        v["a0"], v["m0"] = call(
            join_body, (meta, *got, out_weight, moved, down_weight),
            (out((mine * 4, width + 128), bf16), out((mine * 4, ff + width), bf16)), smem=1,
            name="join", cold=(2, 3, 4, 5, 6, 7),
        )
        v["tx"] = add(x_mine, swap_core(x_send))
        v.sync("a0", "m0", "tx")
        v["a1"] = turn(v["a0"])
        v["m1"] = turn(v["m0"])
        side("xa0", v["a0"], 2)
        side("xm0", v["m0"], 2)
        v["yx"] = swap_pair(v["tx"])
        v["a2"] = turn(v["a1"])
        side("xa1", v["a1"], 2)
        v["a3"] = turn(v["a2"])
        side("xa2", v["a2"], 2)
        v["x"] = v["tx"] + v["yx"]
        v["xo"] = swap_core(v["x"])
        side("xa3", v["a3"], 2)
        v["m2"] = turn(v["m1"])
        v["m3"] = turn(v["m2"])
        side("xm1", v["m1"], 2)
        side("xm2", v["m2"], 2)
        side("xm3", v["m3"], 2)
        c_mine, c_send = pick(cotangent, "pick_cotangent")
        v["tc"] = add(c_mine, swap_core(c_send))
        v["yc"] = swap_pair(v["tc"])
        attn_names = [n + str(k) for k in range(4) for n in ("a", "xa")]
        attn_packs = [v[n] for n in attn_names]

    a, qkv, probs, mix, ba_o, ba_t, w_qkv, w_out, gain_rows, r, gain_cols = call(
        attn_fwd_body,
        (order, v["x"], v["xo"], seg_col, seg_row, *attn_packs),
        (
            out((both, width), bf16),
            out((both, 3 * part), bf16),
            out((2 * part // HEAD_DIM, rows, rows), f32),
            out((both, part), bf16),
            half,
            half,
            out((width, 3 * part), bf16),
            out((part, width), bf16),
            out((8, width), f32),
            out((both, 128), f32),
            out((width, 128), bf16),
        ),
        smem=1,
        flops=2 * both * width * width,
        name="attn_fwd",
        cold=range(1, 13),
    )
    v["a"], v["mix"] = a, mix
    v["tb"] = add(ba_o, swap_core(ba_t))
    v.sync("tb", "a", "mix")
    v["yb"] = swap_pair(v["tb"])
    if native:
        v["yc"] = swap_pair(v["tc"])
    a_turned, mix_turned = call(
        turn_body, (v["a"], v["mix"]), (out((width, both), bf16), out((part, both), bf16)),
        name="turn",
    )
    v["c"] = v["tc"] + v["yc"]
    v["co"] = swap_core(v["c"])
    v.sync("yb", "tb", "co", "c")
    (v["h"],) = call(
        norm_body, (v["tb"], v["yb"], v["x"], gain_rows), (half,), name="norm_two", cold=(0, 1, 2)
    )
    v["ho"] = swap_core(v["h"])
    if not native:
        mlp_packs = [v[n + str(k)] for k in range(4) for n in ("m", "xm")]
    g, du, db, w_up, w_down, dm_o, dm_t = call(
        mlp_body,
        (order, v["h"], v["ho"], v["c"], v["co"], r, *mlp_packs),
        (
            out((both, ff), bf16),
            out((both, ff), bf16),
            out((both, width), bf16),
            out((width, ff), bf16),
            out((ff, width), bf16),
            half,
            half,
        ),
        smem=1,
        flops=6 * both * width * ff,
        name="mlp",
        cold=(2, 3, 4, *range(6, 14)),
    )

    v["du"] = du
    v["td"] = add(dm_o, swap_core(dm_t))
    v.sync("td", "du")
    v["yd"] = swap_pair(v["td"])
    col, *up_grads = call(
        up_grad_body,
        (order, v["du"], v["h"], v["ho"], w_up, gain_cols),
        (out((width, 128), f32), *([out((width // BLOCKS, ff), bf16)] * BLOCKS)),
        scratch=[pltpu.VMEM((width, both), bf16)],
        smem=1,
        flops=2 * both * width * ff,
        name="up_grad",
        cold=(3,),
    )
    v["g"] = g
    if not native:
        for k in (1, 2, 3):
            side("xu%d" % k, up_grads[2 * k + 1])
    bm_o, bm_t, cols, *down_grads = call(
        down_grad_body,
        (
            order, v["g"], db, w_down, col, ba_o, ba_t, v["c"], v["co"], v["x"], v["xo"],
        ),
        (half, half, out((width, 128), f32), *([out((ff // BLOCKS, width), bf16)] * BLOCKS)),
        scratch=[pltpu.VMEM((ff, both), bf16)],
        smem=1,
        flops=4 * both * width * ff,
        name="down_grad",
        cold=(7, 8, 9, 10),
    )
    v["bm"], v["bn"], v["col"] = bm_o, bm_t, col
    v.sync("yd", "td", "bm")
    v["tm"] = add(v["bm"], swap_core(v["bn"]))
    da_own, dh = call(
        hidden_grad_body,
        (v["td"], v["yd"], v["tb"], v["yb"], v["x"], v["c"], r, gain_rows),
        (half, out((rows, width), f32)),
        name="hidden_grad",
        cold=range(6),
    )
    v["da"] = da_own
    v["dao"] = swap_core(da_own)

    def attention_back(v):
        dqkv, *attn_grads = call(
            attn_bwd_body,
            (
                order, a_turned, mix_turned, qkv, probs, v["da"], v["dao"], w_qkv, w_out,
                gain_cols, cols,
            ),
            (
                out((both, 3 * part), bf16),
                *([out((width // BLOCKS, width + 128), bf16)] * BLOCKS),
            ),
            scratch=[pltpu.VMEM((both, width), bf16)],
            smem=1,
            flops=3 * both * width * width,
            name="attn_bwd",
            cold=(6,),
        )
        v["dqkv"] = dqkv
        return attn_grads

    def normed_back(dqkv):
        return call(
            normed_grad_body, (dqkv, w_qkv), (half, half), flops=2 * both * width * 3 * part,
            name="normed_grad",
        )

    def give():
        return call(
            result_body,
            (v["tb"], v["yb"], v["tm"], v["ym"], v["c"], r),
            (half, out((rows, 128), f32)),
            name="result",
            cold=range(5),
        )

    def take(dr):
        return call(
            input_grad_body, (v["tx2"], v["yx2"], v["x"], dh, dr, gain_rows), (half,),
            name="input_grad", cold=range(3),
        )[0]

    def place_rows(base, own, other, name):
        return call(
            place_body, (meta, pos_row, base, own, other), (out(base.shape, bf16),), smem=1,
            flops=4 * rows * span * width, name=name, keep=False, limit=24,
        )[0]

    if native:
        attn_grads = attention_back(v)
        dx_o, dx_t = normed_back(v["dqkv"])
        v["ym"] = swap_pair(v["tm"])
        v["tx2"] = add(dx_o, swap_core(dx_t))
        v["yx2"] = swap_pair(v["tx2"])
        v["e"], dr = give()
        v["eo"] = swap_core(v["e"])
        v["dx"] = take(dr)
        v["dxo"] = swap_core(v["dx"])
    else:
        attn_grads = attention_back(v)
        v["ym"] = swap_pair(v.order(v["tm"], "dqkv"))
        v["dxm"], v["dxs"] = normed_back(v["dqkv"])
        down_grads[3] = v.order(down_grads[3], "dqkv")
        parts = {"u": up_grads, "a": attn_grads, "w": down_grads}
        up_grads[2] = v.order(up_grads[2], "dqkv")
        for n, k in (("u", 0), ("w", 1), ("a", 1), ("a", 2), ("a", 3), ("w", 2), ("w", 3), ("a", 0), ("w", 0)):
            side("x%s%d" % (n, k), parts[n][2 * k + 1])
        for n, blocks in parts.items():
            z = turn(add(blocks[2], v["x%s1" % n]))
            z = turn(add(blocks[4], v["x%s2" % n], z))
            v["z%s3" % n] = turn(add(blocks[6], v["x%s3" % n], z))
            v[n + "0"] = blocks[0]
        v["tx2"] = add(v["dxm"], swap_core(v["dxs"]))
        v["yx2"] = swap_pair(v["tx2"])
        v["e"], dr = give()
        v["eo"] = swap_core(v["e"])
        v["dx"] = take(dr)
        v["dxo"] = swap_core(v["dx"])
        piece = [out((mine, ff), f32)] + [out((mine, ff), bf16)] * 3
        cut = call(
            split_up_body, (meta, v["u0"], v["xu0"], v["zu3"]), piece,
            scratch=[pltpu.VMEM((4 * mine, ff), f32)], smem=1, name="split_up", cold=(2, 3),
        )
        cut = [cut[0]] + [flip_bit(cut[k], "grp", 4, k) for k in range(1, 4)]
        (up_grad,) = call(
            final_up_body, (meta, *cut), (out((mine, units), f32),),
            scratch=[pltpu.VMEM((4, mine, ff), f32)], smem=1, name="final_up", keep_out=False,
            cold=(2, 3, 4),
        )
        piece = [out((mine, head), f32)] + [out((mine, head), bf16)] * 3
        *cut, og = call(
            split_attn_body, (meta, v["a0"], v["xa0"], v["za3"]),
            (*piece, out((mine, width), f32)),
            scratch=[pltpu.VMEM((4 * mine, width + 128), f32)], smem=1, name="split_attn",
            cold=(2, 3),
        )
        cut = [cut[0]] + [flip_bit(cut[k], "grp", 4, k) for k in range(1, 4)]
        out_moved = lax.ppermute(og, ("seq", "grp"), swaps)
        out_grad = jnp.where(odd == 1, out_moved, og)
        down_grad = v["w0"].astype(f32) + v["xw0"].astype(f32) + v["zw3"].astype(f32)
        qkv_grad, small = call(
            final_attn_body, (meta, *cut),
            (out((mine, 3 * width), f32), out((8, 128), f32)),
            scratch=[pltpu.VMEM((4, mine, head), f32)], smem=1, name="final_attn", keep_out=False,
            cold=(2, 3, 4),
        )
        small = small[:3, :mine]

    mixed = place_rows(tokens, v["e"], v["eo"], "place_mixed")
    input_grad = place_rows(cotangent, v["dx"], v["dxo"], "place_input_grad")

    if native:
        up_sum = native_scatter(up_grads)
        down_grad = native_scatter(down_grads)
        back = exchange([up_sum[j * mine : (j + 1) * mine] for j in range(4)], member)
        up_grad = jnp.stack([b.reshape(mine, seqs, ff // seqs) for b in back], axis=2)
        up_grad = up_grad.reshape(mine, units)
        step = part // BLOCKS
        out_mine = jnp.concatenate(
            [
                jnp.concatenate([b[j * step : (j + 1) * step, head:] for j in range(4)], axis=1)
                for b in attn_grads
            ],
            axis=0,
        )
        out_mine = out_mine.astype(f32).reshape(4, 1, HEAD_DIM, width)
        slots = (jnp.arange(4) == head_set).astype(f32)[None, :, None, None]
        out_all = (out_mine * slots).reshape(width, width)
        out_grad = lax.psum_scatter(out_all, ("seq", "grp"), scatter_dimension=0, tiled=True)
        attn_sum = native_scatter([b[:, :head] for b in attn_grads])
        back = exchange([attn_sum[j * mine : (j + 1) * mine] for j in range(4)], member)
        by_head = [b[:, : 3 * part].reshape(mine, 3, 4, HEAD_DIM) for b in back]
        qkv_grad = jnp.stack([by_head[HEAD_OF.index(p)] for p in range(4)], axis=3)
        qkv_grad = qkv_grad.reshape(mine, 3 * width)
        small = sum(b[:, 3 * part : 3 * part + 3] for b in back).T
    return (
        mixed,
        input_grad,
        qkv_grad,
        out_grad,
        up_grad,
        down_grad,
        small[0],
        small[1],
        small[2],
    )


def solution(mesh):
    placed = (
        P("seq", "grp", None),
        P("seq", None),
        P("seq", None),
        P(("seq", "grp"), None),
        P(("seq", "grp"), None),
        P(("seq", "grp"), None),
        P(("seq", "grp"), None),
        P(("seq", "grp")),
        P(("seq", "grp")),
        P(("seq", "grp")),
        P("seq", "grp", None),
    )
    return jax.shard_map(
        on_device,
        mesh=mesh,
        in_specs=placed,
        out_specs=(
            P("seq", "grp", None),
            P("seq", "grp", None),
            P(("seq", "grp"), None),
            P(("seq", "grp"), None),
            P(("seq", "grp"), None),
            P(("seq", "grp"), None),
            P(("seq", "grp")),
            P(("seq", "grp")),
            P(("seq", "grp")),
        ),
        check_vma=False,
    )
```

```python
import jax
import jax.numpy as jnp
from jax import lax
from jax.experimental import pallas as pl
from jax.experimental.pallas import tpu as pltpu
from jax.sharding import PartitionSpec as P

HEAD_DIM = 64
SEG_COUNT = 4
BLOCKS = 8
epsilon = 1e-06
masked = -1e30
f32 = jnp.float32
bf16 = jnp.bfloat16
gelu_scale = 0.7978845608028654
gelu_cubic = 0.044715

NN = (((1,), (0,)), ((), ()))
NT = (((1,), (1,)), ((), ()))
TN = (((0,), (0,)), ((), ()))


def mm(a, b, dims=NN):
    return lax.dot_general(a, b, dims, preferred_element_type=f32)


VM = pl.BlockSpec(memory_space=pltpu.VMEM)
SM = pl.BlockSpec(memory_space=pltpu.SMEM)
MIB = 1024 * 1024


def call(
    body, args, outs, scratch=(), smem=0, flops=0, name=None, limit=8, keep=True, keep_out=True,
    cold=(), free=(),
):
    moved = sum(a.size * a.dtype.itemsize for a in args)
    moved += sum(o.size * o.dtype.itemsize for o in outs)
    if keep:
        args = tuple(
            a
            if n < smem or n in free
            else pltpu.with_memory_space_constraint(a, pltpu.HBM if n in cold else pltpu.VMEM)
            for n, a in enumerate(args)
        )
    if keep and keep_out:
        shapes = tuple(pltpu.VMEM(o.shape, o.dtype) for o in outs)
    else:
        shapes = tuple(outs)
    return pl.pallas_call(
        body,
        out_shape=shapes,
        in_specs=[SM] * smem + [VM] * (len(args) - smem),
        out_specs=tuple([VM] * len(outs)),
        scratch_shapes=list(scratch),
        cost_estimate=pl.CostEstimate(flops=flops, bytes_accessed=moved, transcendentals=0),
        compiler_params=pltpu.CompilerParams(vmem_limit_bytes=limit * MIB),
        name=name,
    )(*args)


def out(shape, dtype):
    return jax.ShapeDtypeStruct(shape, dtype)


def pick_body(meta, pos_ref, src_ref, own_ref, oth_ref):
    rows, span = pos_ref.shape[1], src_ref.shape[1]
    core, base = meta[0], meta[1]
    lane = lax.broadcasted_iota(jnp.int32, (rows, span), 1) + base
    for half, ref in ((0, own_ref), (1, oth_ref)):
        seq = core if half == 0 else 1 - core
        hot = jnp.where(pos_ref[half] == lane, 1.0, 0.0).astype(bf16)
        src = src_ref[seq]
        ref[...] = mm(hot, src).astype(bf16)


def place_body(meta, pos_ref, base_ref, own_ref, oth_ref, out_ref):
    rows, span = pos_ref.shape[2], base_ref.shape[1]
    core, base = meta[0], meta[1]
    row = lax.broadcasted_iota(jnp.int32, (span, rows), 0) + base
    for half, ref in ((0, own_ref), (1, oth_ref)):
        seq = core if half == 0 else 1 - core
        hot = jnp.where(pos_ref[half] == row, 1.0, 0.0).astype(bf16)
        added = mm(hot, ref[...])
        out_ref[seq] = (base_ref[seq].astype(f32) + added).astype(bf16)


def attn_fwd_body(
    idx, xo_ref, xt_ref, segc_ref, segr_ref, *refs
):
    packs = refs[:BLOCKS]
    a_ref, qkv_ref, p_ref, o_ref, bo_ref, bt_ref, wq_ref, wo_ref, gr_ref, r_ref, gcol = refs[BLOCKS:]
    rows, width = xo_ref.shape
    part = width // 4
    qcols = 3 * part
    blk = width // BLOCKS
    ob = part // BLOCKS
    for b, pk in enumerate(packs):
        s = idx[b]
        off = pl.multiple_of(s * blk, blk)
        wq_ref[pl.ds(off, blk), :] = pk[:, :qcols]
        gcol[pl.ds(off, blk), :] = pk[:, qcols : qcols + 128]
        off2 = pl.multiple_of(s * ob, ob)
        for j in range(4):
            wo_ref[pl.ds(off2, ob), j * part : (j + 1) * part] = pk[
                j * ob : (j + 1) * ob, qcols + 128 :
            ]
    eye = (
        lax.broadcasted_iota(jnp.int32, (8, 128), 0) == lax.broadcasted_iota(jnp.int32, (8, 128), 1)
    ).astype(f32).astype(bf16)
    gr = mm(eye, gcol[...], NT)
    gr_ref[...] = gr
    gain = gr[0:1]
    for half, x_ref in ((0, xo_ref), (1, xt_ref)):
        span = pl.ds(half * rows, rows)
        xb = x_ref[...]
        x = xb.astype(f32)
        scale = lax.rsqrt(jnp.mean(x * x, axis=-1, keepdims=True) + epsilon)
        a_ref[span, :] = (x * scale * gain).astype(bf16)
        r_ref[span, :] = mm(xb, gcol[...])

    def project(i, carry):
        cols = pl.ds(pl.multiple_of(i * part, part), part)
        qkv_ref[:, cols] = mm(a_ref[...], wq_ref[:, cols]).astype(bf16)
        return carry

    lax.fori_loop(0, 3, project, 0)
    ri = lax.broadcasted_iota(jnp.int32, (rows, rows), 0)
    ci = lax.broadcasted_iota(jnp.int32, (rows, rows), 1)
    causal = ci <= ri
    heads = part // HEAD_DIM
    score_scale = HEAD_DIM ** (-0.5)
    for half in range(2):
        allowed = causal & (segc_ref[half] == segr_ref[half])
        span = pl.ds(half * rows, rows)
        for h in range(heads):
            q = qkv_ref[span, h * HEAD_DIM : (h + 1) * HEAD_DIM]
            k = qkv_ref[span, part + h * HEAD_DIM : part + (h + 1) * HEAD_DIM]
            v = qkv_ref[span, 2 * part + h * HEAD_DIM : 2 * part + (h + 1) * HEAD_DIM]
            logits = jnp.where(allowed, mm(q, k, NT) * score_scale, masked)
            e = jnp.exp(logits - jnp.max(logits, axis=-1, keepdims=True))
            p = e * (1.0 / jnp.sum(e, axis=-1, keepdims=True))
            p_ref[half * heads + h] = p
            o_ref[span, h * HEAD_DIM : (h + 1) * HEAD_DIM] = mm(p.astype(bf16), v).astype(bf16)

    def project_out(i, carry):
        cols = pl.ds(pl.multiple_of(i * part, part), part)
        res = mm(o_ref[...], wo_ref[:, cols]).astype(bf16)
        bo_ref[:, cols] = res[:rows]
        bt_ref[:, cols] = res[rows:]
        return carry

    lax.fori_loop(0, 4, project_out, 0)


def norm_body(t_ref, u_ref, x_ref, gr_ref, m_ref):
    h = x_ref[...].astype(f32) + (t_ref[...].astype(f32) + u_ref[...].astype(f32))
    scale = lax.rsqrt(jnp.mean(h * h, axis=-1, keepdims=True) + epsilon)
    m_ref[...] = (h * scale * gr_ref[1:2]).astype(bf16)


def turn_body(a_ref, o_ref, at_ref, ot_ref):
    tile = 256

    def step(i, carry):
        cols = pl.ds(pl.multiple_of(i * tile, tile), tile)
        at_ref[cols, :] = a_ref[:, cols].T
        return carry

    lax.fori_loop(0, a_ref.shape[1] // tile, step, 0)
    ot_ref[...] = o_ref[...].T


def mlp_body(idx, mo_ref, mt_ref, co_ref, ct_ref, r_ref, *refs):
    packs, rest = refs[:BLOCKS], refs[BLOCKS:]
    g_ref, du_ref, db_ref, wu_ref, wd_ref, dmo_ref, dmt_ref = rest
    rows, width = mo_ref.shape
    units = wu_ref.shape[1]
    blk, sub = width // BLOCKS, units // BLOCKS
    for b in range(BLOCKS):
        wu_ref[pl.ds(pl.multiple_of(idx[b] * blk, blk), blk), :] = packs[b][:, :units]
        wd_ref[pl.ds(pl.multiple_of(idx[b] * sub, sub), sub), :] = packs[b][:, units:]
    r = r_ref[:, 2:3]
    db_ref[:rows, :] = (r[:rows] * co_ref[...].astype(f32)).astype(bf16)
    db_ref[rows:, :] = (r[rows:] * ct_ref[...].astype(f32)).astype(bf16)
    tile = 256

    def step(i, carry):
        cols = pl.ds(pl.multiple_of(i * tile, tile), tile)
        for half, m_ref in ((0, mo_ref), (1, mt_ref)):
            span = pl.ds(half * rows, rows)
            u = mm(m_ref[...], wu_ref[:, cols])
            u2 = u * u
            th = jnp.tanh(gelu_scale * (u + gelu_cubic * (u2 * u)))
            half_up = 0.5 * (1.0 + th)
            g_ref[span, cols] = (u * half_up).astype(bf16)
            slope = half_up + (0.5 * u) * (1.0 - th * th) * (
                gelu_scale * (1.0 + 3.0 * gelu_cubic * u2)
            )
            dg = mm(db_ref[span, :], wd_ref[cols, :], NT)
            du_ref[span, cols] = (dg * slope).astype(bf16)
        return carry

    lax.fori_loop(0, units // tile, step, 0)

    def step2(i, carry):
        cols = pl.ds(pl.multiple_of(i * tile, tile), tile)
        dm = mm(du_ref[...], wu_ref[cols, :], NT).astype(bf16)
        dmo_ref[:, cols] = dm[:rows]
        dmt_ref[:, cols] = dm[rows:]
        return carry

    lax.fori_loop(0, width // tile, step2, 0)


def mlp_grad_body(
    idx, g_ref, du_ref, db_ref, mo_ref, mt_ref, wu_ref, wd_ref, gcol, ao_ref, at_ref, co_ref,
    ct_ref, xo_ref, xt_ref, *refs
):
    bo_ref, bt_ref, col_ref = refs[:3]
    grads, (flip,) = refs[3 : 3 + BLOCKS], refs[3 + BLOCKS :]
    rows, width = mo_ref.shape
    units = wu_ref.shape[1]
    blk, sub = width // BLOCKS, units // BLOCKS
    tile = 256

    def turn_rows(i, carry):
        cols = pl.ds(pl.multiple_of(i * tile, tile), tile)
        flip[cols, :rows] = mo_ref[:, cols].T
        flip[cols, rows:] = mt_ref[:, cols].T
        return carry

    lax.fori_loop(0, width // tile, turn_rows, 0)
    for b, ref in enumerate(grads):
        off = pl.ds(pl.multiple_of(idx[b] * blk, blk), blk)
        grad = mm(flip[off, :], du_ref[...])
        ref[:, :units] = grad.astype(bf16)
        gain = jnp.sum(grad * wu_ref[off, :].astype(f32), axis=-1, keepdims=True)
        gain = gain / gcol[off, 1:2].astype(f32)
        col_ref[off, :] = jnp.broadcast_to(gain, (blk, 128))

    def step(i, carry):
        cols = pl.ds(pl.multiple_of(i * tile, tile), tile)
        res = mm(g_ref[...], wd_ref[:, cols])
        bo_ref[:, cols] = res[:rows].astype(bf16)
        bt_ref[:, cols] = res[rows:].astype(bf16)
        flip[cols, :] = g_ref[:, cols].T
        own, other = carry
        own += jnp.sum(
            (res[:rows] + ao_ref[:, cols].astype(f32)) * co_ref[:, cols].astype(f32),
            axis=-1, keepdims=True,
        )
        other += jnp.sum(
            (res[rows:] + at_ref[:, cols].astype(f32)) * ct_ref[:, cols].astype(f32),
            axis=-1, keepdims=True,
        )
        return own, other

    zero = jnp.zeros((rows, 1), f32)
    dots = lax.fori_loop(0, width // tile, step, (zero, zero))
    for b, ref in enumerate(grads):
        off = pl.multiple_of(idx[b] * sub, sub)
        ref[:, units:] = mm(flip[pl.ds(off, sub), :], db_ref[...]).astype(bf16)
    lane = lax.broadcasted_iota(jnp.int32, (rows, 128), 1)
    route = jnp.zeros((width, 128), f32)
    for d, x_ref in zip(dots, (xo_ref, xt_ref)):
        high = d.astype(bf16).astype(f32)
        two = jnp.where(lane == 0, high, jnp.where(lane == 1, d - high, 0.0)).astype(bf16)
        route += mm(x_ref[...], two, TN)
    total = jnp.sum(route[:, :2], axis=-1, keepdims=True)
    wide = lax.broadcasted_iota(jnp.int32, (width, 128), 1)
    col_ref[...] = jnp.where(wide == 1, col_ref[...], jnp.where(wide == 2, total, 0.0))


def hidden_grad_body(dt_ref, du_ref, bt_ref, bu_ref, x_ref, c_ref, r_ref, gr_ref, da_ref, dh_ref):
    dm = dt_ref[...].astype(f32) + du_ref[...].astype(f32)
    h = x_ref[...].astype(f32) + (bt_ref[...].astype(f32) + bu_ref[...].astype(f32))
    rows = h.shape[0]
    n = lax.rsqrt(jnp.mean(h * h, axis=-1, keepdims=True) + epsilon)
    t = dm * gr_ref[1:2]
    dh = n * t - h * (n * n * n) * jnp.mean(t * h, axis=-1, keepdims=True)
    dh_ref[...] = dh
    de = r_ref[:rows, 2:3] * c_ref[...].astype(f32)
    da_ref[...] = (de + dh).astype(bf16)


def result_body(at_ref, au_ref, mt_ref, mu_ref, c_ref, r_ref, e_ref, dr_ref):
    branch = (at_ref[...].astype(f32) + au_ref[...].astype(f32)) + (
        mt_ref[...].astype(f32) + mu_ref[...].astype(f32)
    )
    rows = branch.shape[0]
    e_ref[...] = (r_ref[:rows, 2:3] * branch).astype(bf16)
    dr = jnp.sum(c_ref[...].astype(f32) * branch, axis=-1, keepdims=True)
    dr_ref[...] = jnp.broadcast_to(dr, dr_ref.shape)


def attn_bwd_body(
    idx, at_ref, ot_ref, qkv_ref, p_ref, dao_ref, dat_ref, wq_ref, wo_ref, gcol, col_ref, *refs
):
    dqkv, near, far, (da,) = refs[0], refs[1:5], refs[5:7], refs[7:]
    rows, width = dao_ref.shape
    part = width // 4
    qcols = 3 * part
    heads = part // HEAD_DIM
    score_scale = HEAD_DIM ** (-0.5)
    da[:rows, :] = dao_ref[...]
    da[rows:, :] = dat_ref[...]
    for half in range(2):
        span = pl.ds(half * rows, rows)
        dmix = mm(da[span, :], wo_ref[...], NT).astype(bf16)
        for h in range(heads):
            lo, hi = h * HEAD_DIM, (h + 1) * HEAD_DIM
            q = qkv_ref[span, lo:hi]
            k = qkv_ref[span, part + lo : part + hi]
            v = qkv_ref[span, 2 * part + lo : 2 * part + hi]
            do = dmix[:, lo:hi]
            p = p_ref[half * heads + h]
            dp = mm(do, v, NT)
            ds = (p * (dp - jnp.sum(p * dp, axis=-1, keepdims=True))).astype(bf16)
            dqkv[span, lo:hi] = (mm(ds, k) * score_scale).astype(bf16)
            dqkv[span, part + lo : part + hi] = (mm(ds, q, TN) * score_scale).astype(bf16)
            dqkv[span, 2 * part + lo : 2 * part + hi] = mm(p.astype(bf16), do, TN).astype(bf16)
    blk = width // BLOCKS
    ob = part // BLOCKS
    lane = lax.broadcasted_iota(jnp.int32, (blk, 128), 1)
    for b in range(BLOCKS):
        s = idx[b]
        k = b // 2
        ref, row = (near[k], 0) if b % 2 == 0 else (far[(k + 3) % 4 // 2], (k + 3) % 2 * blk)
        rows_of = slice(row, row + blk)
        off = pl.ds(pl.multiple_of(s * blk, blk), blk)
        grad = mm(at_ref[off, :], dqkv[...])
        ref[rows_of, :qcols] = grad.astype(bf16)
        gain = jnp.sum(grad * wq_ref[off, :].astype(f32), axis=-1, keepdims=True)
        gain = gain / gcol[off, 0:1].astype(f32)
        ref[rows_of, qcols : qcols + 128] = jnp.where(lane == 0, gain, col_ref[off, :]).astype(bf16)
        og = mm(ot_ref[pl.ds(pl.multiple_of(s * ob, ob), ob), :], da[...]).astype(bf16)
        for j in range(4):
            ref[row + j * ob : row + (j + 1) * ob, qcols + 128 :] = og[:, j * part : (j + 1) * part]


def normed_grad_body(dqkv_ref, wq_ref, do_ref, dt_ref):
    rows, width = do_ref.shape
    tile = 256

    def step(i, carry):
        cols = pl.ds(pl.multiple_of(i * tile, tile), tile)
        d = mm(dqkv_ref[...], wq_ref[cols, :], NT).astype(bf16)
        do_ref[:, cols] = d[:rows]
        dt_ref[:, cols] = d[rows:]
        return carry

    lax.fori_loop(0, width // tile, step, 0)


def input_grad_body(t_ref, u_ref, x_ref, dh_ref, dr_ref, gr_ref, dx_ref):
    d = t_ref[...].astype(f32) + u_ref[...].astype(f32)
    x = x_ref[...].astype(f32)
    m = lax.rsqrt(jnp.mean(x * x, axis=-1, keepdims=True) + epsilon)
    s = d * gr_ref[0:1]
    dxn = m * s - x * (m * m * m) * jnp.mean(s * x, axis=-1, keepdims=True)
    dx_ref[...] = (dxn + dh_ref[...] + dr_ref[:, 0:1] * gr_ref[2:3]).astype(bf16)


HEAD_OF = (0, 2, 1, 3)


def pack_body(meta, qkv_ref, up_ref, gains_ref, *refs):
    outs, (tmp,) = refs[:4], refs[4:]
    width, units = qkv_ref.shape[1] // 3, up_ref.shape[1]
    part = width // 4
    sub = units // (4 * BLOCKS)
    for j in range(4):
        p = HEAD_OF[j]
        for t in range(3):
            for z in range(4):
                src = t * width + (4 * z + p) * HEAD_DIM
                dst = t * part + z * HEAD_DIM
                tmp[j, :, dst : dst + HEAD_DIM] = qkv_ref[:, src : src + HEAD_DIM]
        tmp[j, :, 3 * part : 3 * part + 128] = gains_ref[...]
        for s in range(BLOCKS):
            dst = 3 * part + 128 + s * sub
            src = (4 * s + j) * sub
            tmp[j, :, dst : dst + sub] = up_ref[:, src : src + sub]
    for k, ref in enumerate(outs):
        ref[...] = tmp[meta[3] ^ k]


def join_body(meta, c0, c1, c2, c3, own_ref, moved_ref, down_ref, attn_ref, mlp_ref):
    mine, width = own_ref.shape
    part = width // 4
    head = 3 * part + 128
    for k, ref in enumerate((c0, c1, c2, c3)):
        off = pl.ds(pl.multiple_of((meta[3] ^ k) * mine, mine), mine)
        attn_ref[off, :head] = ref[:, :head]
        mlp_ref[off, : mlp_ref.shape[1] - width] = ref[:, head:]
    mlp_ref[:, mlp_ref.shape[1] - width :] = down_ref[...]
    take = jnp.full(own_ref.shape, meta[4]) == 1
    rows = jnp.where(take, moved_ref[...].astype(f32), own_ref[...].astype(f32)).astype(bf16)
    for j in range(4):
        attn_ref[j * mine : (j + 1) * mine, head:] = rows[:, j * part : (j + 1) * part]


def split_body(
    meta, m0, m1, m2, a0, a1, a2, c0, c1, c2, c3, down_ref, out_ref, tm, ta
):
    mine, width = out_ref.shape
    units = m0.shape[1] - width
    part = width // 4
    head = 3 * part + 128
    for n in range(4):
        span = pl.ds(n * mine, mine)
        total = (m0[span, :].astype(f32) + m1[span, :].astype(f32)) + m2[span, :].astype(f32)
        down_ref[span, :] = total[:, units:]
        tm[span, :] = total[:, :units]
        late = pl.ds((4 + n) * mine, mine)
        total = (a0[span, :].astype(f32) + a1[late, :].astype(f32)) + a2[span, :].astype(f32)
        ta[span, :] = total[:, :head]
        out_ref[:, n * part : (n + 1) * part] = total[:, head:]
    for k, ref in enumerate((c0, c1, c2, c3)):
        off = pl.ds(pl.multiple_of((meta[3] ^ k) * mine, mine), mine)
        ref[:, :head] = ta[off, :].astype(ref.dtype)
        ref[:, head:] = tm[off, :].astype(ref.dtype)


def final_body(meta, c0, c1, c2, c3, qkv_ref, up_ref, small_ref, tmp):
    mine = qkv_ref.shape[0]
    width = qkv_ref.shape[1] // 3
    part = width // 4
    head = 3 * part + 128
    sub = up_ref.shape[1] // (4 * BLOCKS)
    for k, ref in enumerate((c0, c1, c2, c3)):
        tmp[meta[3] ^ k] = ref[...].astype(f32)
    for j in range(4):
        for t in range(3):
            for z in range(4):
                dst = t * width + (4 * z + HEAD_OF[j]) * HEAD_DIM
                src = t * part + z * HEAD_DIM
                qkv_ref[:, dst : dst + HEAD_DIM] = tmp[j, :, src : src + HEAD_DIM]
        for s in range(BLOCKS):
            dst = (4 * s + j) * sub
            up_ref[:, dst : dst + sub] = tmp[j, :, head + s * sub : head + (s + 1) * sub]
    last = slice(3 * part, head)
    small = (tmp[0, :, last] + tmp[1, :, last]) + (tmp[2, :, last] + tmp[3, :, last])
    wide = jnp.concatenate([small, jnp.zeros((128 - mine, 128), f32)], axis=0)
    small_ref[...] = wide.T[:8]


def flip_bit(v, axis, size, mask):
    return lax.ppermute(v, axis, [(i, i ^ mask) for i in range(size)])


def swap_core(v):
    return flip_bit(v, "grp", 4, 1)


def swap_pair(v):
    return flip_bit(v, "grp", 4, 2)


def swap_side(v, seqs):
    return flip_bit(v, "seq", seqs, 1)


def shift_one(v, seqs):
    return lax.ppermute(v, "seq", [(i, (i + 2) % seqs) for i in range(seqs)])


def reorder(parts, member):
    low = (member & 1) == 1
    high = (member & 2) == 2
    res = []
    for j in range(4):
        straight = jnp.where(low, parts[j ^ 1], parts[j])
        crossed = jnp.where(low, parts[j ^ 3], parts[j ^ 2])
        res.append(jnp.where(high, crossed, straight))
    return res


def exchange(chunks, member):
    rel = reorder(chunks, member)
    got = [rel[0]] + [flip_bit(rel[k], "grp", 4, k) for k in range(1, 4)]
    return reorder(got, member)


def native_gather(pack):
    full = lax.all_gather(pack, "seq", axis=0, tiled=True)
    return list(full.reshape((BLOCKS, -1) + full.shape[1:]))


def native_scatter(blocks):
    full = jnp.concatenate(blocks, axis=0)
    return lax.psum_scatter(full.astype(f32), "seq", scatter_dimension=0, tiled=True)


def add(*parts):
    total = parts[0].astype(f32)
    for p in parts[1:]:
        total = total + p.astype(f32)
    return total.astype(bf16)


class Flow:
    def __getitem__(self, name):
        return self.__dict__[name]

    def __setitem__(self, name, value):
        self.__dict__[name] = value

    def order(self, value, name):
        token = lax.create_token()
        token, self[name] = lax.optimization_barrier((token, self[name]))
        return lax.optimization_barrier((token, value))[1]

    def sync(self, *names):
        held = [n for n in names if n in self.__dict__]
        done = lax.optimization_barrier(tuple(self[n] for n in held))
        for n, value in zip(held, done):
            self[n] = value


def on_device(
    tokens,
    segments,
    routed,
    qkv_weight,
    out_weight,
    up_weight,
    down_weight,
    attn_gain,
    mlp_gain,
    router_weight,
    cotangent,
):
    groups, seqs = lax.axis_size("grp"), lax.axis_size("seq")
    member, place = lax.axis_index("grp"), lax.axis_index("seq")
    seq_dev, span, width = tokens.shape
    rows = routed.shape[1]
    units = down_weight.shape[0] * groups * seqs
    if groups != 4 or seq_dev != 2:
        raise ValueError("mesh")
    native = seqs != BLOCKS
    part, ff = width // 4, units // 4
    core, pair = member & 1, member >> 1
    mine = qkv_weight.shape[0]
    head = 3 * part + 128
    both = 2 * rows
    odd = (place ^ member) & 1
    meta = jnp.stack([core, member * span, pair, member, odd]).astype(jnp.int32)
    half = out((rows, width), bf16)
    v = Flow()

    queue = []

    chain = []

    def hop(name, t, lag):
        if len(chain) >= lag:
            t = v.order(t, chain[-lag])
        chain.append(name)
        v[name] = shift_one(t, seqs)

    def side(name, t, lag):
        if len(queue) >= lag:
            t = v.order(t, queue[-lag])
        queue.append(name)
        v[name] = swap_side(t, seqs)


    flip = core == 1
    pos = jnp.where(flip, routed[::-1], routed)
    starts = jnp.stack(
        [jnp.sum((segments < n).astype(jnp.int32), axis=1) for n in range(1, SEG_COUNT)], axis=0
    )
    seg = jnp.sum((routed[None] >= starts[:, :, None]).astype(jnp.int32), axis=0)
    seg = jnp.where(flip, seg[::-1], seg)
    pos_col, pos_row = pos[:, :, None], pos[:, None, :]
    seg_col, seg_row = seg[:, :, None], seg[:, None, :]

    def pick(source, name):
        return call(
            pick_body, (meta, pos_col, source), (half, half), smem=1,
            flops=4 * rows * span * width, name=name, keep=False, limit=24,
        )

    gains = jnp.stack([attn_gain, mlp_gain, router_weight], axis=1)
    gains = jnp.pad(gains, ((0, 0), (0, 125)))
    if native:
        qkv_view = qkv_weight.reshape(mine, 3, 4, 4, HEAD_DIM)
        chunks = [
            jnp.concatenate([qkv_view[:, :, :, p].reshape(mine, 3 * part), gains], axis=1)
            for p in HEAD_OF
        ]
        qkv_blocks = native_gather(jnp.concatenate(exchange(chunks, member), axis=0))
        out_full = lax.all_gather(out_weight, ("seq", "grp"), axis=0, tiled=True)
        out_view = out_full.reshape(4, 4, HEAD_DIM, width)
        head_set = 2 * core + pair
        out_rows = lax.dynamic_index_in_dim(out_view, head_set, 1, keepdims=False)
        out_rows = out_rows.reshape(BLOCKS, part // BLOCKS, width)
        attn_packs = [
            jnp.concatenate(
                [q, jnp.concatenate([o[:, j * part : (j + 1) * part] for j in range(4)], axis=0)],
                axis=1,
            )
            for q, o in zip(qkv_blocks, out_rows)
        ]
        up_view = up_weight.reshape(mine, seqs, 4, ff // seqs)
        chunks = [up_view[:, :, j].reshape(mine, ff) for j in range(4)]
        up_rows = jnp.concatenate(exchange(chunks, member), axis=0)
        mlp_packs = native_gather(jnp.concatenate([up_rows, down_weight], axis=1))
        order = jnp.arange(BLOCKS, dtype=jnp.int32)
        x_mine, x_send = pick(tokens, "pick_tokens")
        v.tx = add(x_mine, swap_core(x_send))
        v.yx = swap_pair(v.tx)
        v.x = v.tx + v.yx
        v.xo = swap_core(v.x)
        c_mine, c_send = pick(cotangent, "pick_cotangent")
        v.tc = add(c_mine, swap_core(c_send))
    else:
        order = jnp.stack(
            [((place ^ r) - 2 * k) % seqs for k in range(BLOCKS // 2) for r in range(2)]
        ).astype(jnp.int32)
        swaps = [
            (s * 4 + g, (s ^ 1) * 4 + (g ^ 1)) for s in range(seqs) for g in range(4) if (s ^ g) & 1
        ]
        chunk = out((mine, head + ff), bf16)
        chunks = call(
            pack_body, (meta, qkv_weight, up_weight, gains), (chunk,) * 4,
            scratch=[pltpu.VMEM((4, mine, head + ff), bf16)], smem=1, name="pack", cold=(1, 2, 3),
        )
        v.k0, v.k1, v.k2, v.k3 = chunks
        v.tokens = tokens
        v.sync("k1", "k2", "k3", "tokens")
        got = [v.k0] + [flip_bit(v["k%d" % k], "grp", 4, k) for k in range(1, 4)]
        x_mine, x_send = pick(v.tokens, "pick_tokens")
        moved = lax.ppermute(out_weight, ("seq", "grp"), swaps)
        v.a0, v.m0 = call(
            join_body, (meta, *got, out_weight, moved, down_weight),
            (out((mine * 4, width + 128), bf16), out((mine * 4, ff + width), bf16)), smem=1,
            name="join", cold=(2, 3, 4, 5, 6, 7),
        )
        v.tx = add(x_mine, swap_core(x_send))
        v.sync("a0", "m0", "tx")
        for n, k in (('a', 1), ('m', 1), ('a', 2), ('a', 3), ('m', 2), ('m', 3)):
            hop("%s%d" % (n, k), v["%s%d" % (n, k - 1)], 3)
        v.yx = swap_pair(v.tx)
        v.x = v.tx + v.yx
        v.xo = swap_core(v.x)
        for n, k in (('m', 0), ('a', 0), ('a', 1), ('a', 2), ('a', 3), ('m', 1), ('m', 2), ('m', 3)):
            side("x%s%d" % (n, k), v["%s%d" % (n, k)], 2)
        c_mine, c_send = pick(cotangent, "pick_cotangent")
        v.tc = add(c_mine, swap_core(c_send))
        v.yc = swap_pair(v.tc)
        v.sync("x", "xo", "m1")
        v.sync("tc", "xo")
        attn_names = [n + str(k) for k in range(4) for n in ("a", "xa")]
        attn_packs = [v[n] for n in attn_names]

    a, qkv, probs, mix, ba_o, ba_t, w_qkv, w_out, gain_rows, r, gain_cols = call(
        attn_fwd_body,
        (order, v.x, v.xo, seg_col, seg_row, *attn_packs),
        (
            out((both, width), bf16),
            out((both, 3 * part), bf16),
            out((2 * part // HEAD_DIM, rows, rows), f32),
            out((both, part), bf16),
            half,
            half,
            out((width, 3 * part), bf16),
            out((part, width), bf16),
            out((8, width), f32),
            out((both, 128), f32),
            out((width, 128), bf16),
        ),
        smem=1,
        flops=2 * both * width * width,
        name="attn_fwd",
        cold=range(1, 13),
    )
    v.a, v.mix = a, mix
    v.tb = add(ba_o, swap_core(ba_t))
    v.sync("tb", "a", "mix", "xm1")
    v.yb = swap_pair(v.tb)
    if native:
        v.yc = swap_pair(v.tc)
    a_turned, mix_turned = call(
        turn_body, (v.a, v.mix), (out((width, both), bf16), out((part, both), bf16)),
        name="turn",
    )
    v.c = v.tc + v.yc
    v.co = swap_core(v.c)
    v.sync("yb", "tb", "co", "c", "xm2")
    (v.h,) = call(
        norm_body, (v.tb, v.yb, v.x, gain_rows), (half,), name="norm_two", free=(0, 1, 2)
    )
    v.ho = swap_core(v.h)
    if not native:
        mlp_packs = [v[n + str(k)] for k in range(4) for n in ("m", "xm")]
    g, du, db, w_up, w_down, dm_o, dm_t = call(
        mlp_body,
        (order, v.h, v.ho, v.c, v.co, r, *mlp_packs),
        (
            out((both, ff), bf16),
            out((both, ff), bf16),
            out((both, width), bf16),
            out((width, ff), bf16),
            out((ff, width), bf16),
            half,
            half,
        ),
        smem=1,
        flops=6 * both * width * ff,
        name="mlp",
        cold=(2, 3, 4, *range(6, 14)),
    )

    v.du = du
    v.td = add(dm_o, swap_core(dm_t))
    v.sync("td", "du")
    v.yd = swap_pair(v.td)
    bm_o, bm_t, cols, *mlp_grads = call(
        mlp_grad_body,
        (
            order, g, v.du, db, v.h, v.ho, w_up, w_down, gain_cols, ba_o, ba_t, v.c,
            v.co, v.x, v.xo,
        ),
        (
            half, half, out((width, 128), f32),
            *([out((width // BLOCKS, ff + width), bf16)] * BLOCKS),
        ),
        scratch=[pltpu.VMEM((width, both), bf16)],
        smem=1,
        flops=6 * both * width * ff,
        name="mlp_grad",
        cold=(5, 11, 12, 13, 14),
    )
    v.bm, v.bn = bm_o, bm_t
    v.tm = add(v.bm, swap_core(v.bn))
    parts = {"m": mlp_grads}
    queue.clear()
    chain.clear()
    v.__dict__.update({n + str(k): None for n in ("xm", "xa") for k in range(4)})
    if not native:
        for n, k in (('m', 1), ('m', 2)):
            side("x%s%d" % (n, k), parts[n][2 * k + 1], 3)
    v.sync("yd", "td", "bm")
    da_own, dh = call(
        hidden_grad_body,
        (v.td, v.yd, v.tb, v.yb, v.x, v.c, r, gain_rows),
        (half, out((rows, width), f32)),
        name="hidden_grad",
        free=range(6),
    )
    v.da = da_own
    v.dao = swap_core(da_own)
    def attention_back(v):
        dqkv, *attn_grads = call(
            attn_bwd_body,
            (
                order, a_turned, mix_turned, qkv, probs, v.da, v.dao, w_qkv, w_out,
                gain_cols, cols,
            ),
            (
                out((both, 3 * part), bf16),
                *([out((width // BLOCKS, width + 128), bf16)] * 4),
                *([out((2 * width // BLOCKS, width + 128), bf16)] * 2),
            ),
            scratch=[pltpu.VMEM((both, width), bf16)],
            smem=1,
            flops=3 * both * width * width,
            name="attn_bwd",
            free=(6,),
        )
        v.dqkv = dqkv
        return attn_grads

    def normed_back(dqkv):
        return call(
            normed_grad_body, (dqkv, w_qkv), (half, half), flops=2 * both * width * 3 * part,
            name="normed_grad",
        )

    def give():
        return call(
            result_body,
            (v.tb, v.yb, v.tm, v.ym, v.c, r),
            (half, out((rows, 128), f32)),
            name="result",
            free=range(5),
        )

    def take(dr):
        return call(
            input_grad_body, (v.tx2, v.yx2, v.x, dh, dr, gain_rows), (half,),
            name="input_grad", free=range(3),
        )[0]

    def place_rows(base, own, other, name):
        return call(
            place_body, (meta, pos_row, base, own, other), (out(base.shape, bf16),), smem=1,
            flops=4 * rows * span * width, name=name, keep=False, limit=24,
        )[0]

    if native:
        attn_grads = attention_back(v)
        blk = width // BLOCKS
        far = {(k + 3) % 4: attn_grads[4 + (k + 3) % 4 // 2] for k in range(4)}
        attn_grads = [
            attn_grads[k] if r == 0 else far[(k + 3) % 4][(k + 3) % 2 * blk :][:blk]
            for k in range(4)
            for r in range(2)
        ]
        dx_o, dx_t = normed_back(v.dqkv)
        v.ym = swap_pair(v.tm)
        v.tx2 = add(dx_o, swap_core(dx_t))
        v.yx2 = swap_pair(v.tx2)
        v.e, dr = give()
        v.eo = swap_core(v.e)
        v.dx = take(dr)
        v.dxo = swap_core(v.dx)
    else:
        attn_grads = attention_back(v)
        v.dxm, v.dxs = normed_back(v.dqkv)
        parts["a"] = attn_grads
        for k in range(4):
            v["m%d" % k], v["a%d" % k] = mlp_grads[2 * k], attn_grads[k]
        v.ym = swap_pair(v.tm)
        for n, k in (('a', 4), ('a', 5), ('m', 3), ('m', 0)):
            side("x%s%d" % (n, k), parts[n][2 * k + 1 if n == "m" else k], 3)
        blk = width // BLOCKS
        v.tx2 = add(v.dxm, swap_core(v.dxs))

        def step(n, k):
            across = v["xm%d" % k] if n == "m" else v["xa%d" % (4 + k // 3)]
            if n == "a":
                across = across[blk:] if k == 2 else across[:blk]
            terms = [v["%s%d" % (n, k)], across]
            if k > 1:
                terms.append(v["z%s%d" % (n, k - 1)])
            hop("z%s%d" % (n, k), add(*terms), 2)

        for n, k in (('m', 1), ('a', 1), ('m', 2), ('a', 2), ('a', 3), ('m', 3)):
            if (n, k) == ("a", 1):
                v.sync("tx2", "a1")
                v.yx2 = swap_pair(v.tx2)
            if (n, k) == ("a", 2):
                v.sync("ym", "tm", "a2")
                v.e, dr = give()
                v.eo = swap_core(v.e)
            if (n, k) == ("a", 3):
                v.sync("yx2", "tx2", "eo", "e", "a3")
            if (n, k) == ("m", 3):
                v.dx = take(dr)
                v.dxo = swap_core(v.dx)
                v.mixed = place_rows(tokens, v.e, v.eo, "place_mixed")
                v.sync("mixed", "dxo", "dx", "m3")
            step(n, k)
        v.input_grad = place_rows(cotangent, v.dx, v.dxo, "place_input_grad")
        v.sync("input_grad", "m0")
        piece = [out((mine, head + ff), f32)] + [out((mine, head + ff), bf16)] * 3
        *cut, down_grad, og = call(
            split_body,
            (meta, v.m0, v.xm0, v.zm3, v.a0, v.xa5, v.za3),
            (*piece, out((4 * mine, width), f32), out((mine, width), f32)),
            scratch=[pltpu.VMEM((4 * mine, ff), f32), pltpu.VMEM((4 * mine, head), f32)], smem=1,
            name="split", cold=(2, 3, 5, 6),
        )
        cut = [cut[0]] + [flip_bit(cut[k], "grp", 4, k) for k in range(1, 4)]
        out_moved = lax.ppermute(og, ("seq", "grp"), swaps)
        out_grad = jnp.where(odd == 1, out_moved, og)
        qkv_grad, up_grad, small = call(
            final_body, (meta, *cut),
            (out((mine, 3 * width), f32), out((mine, units), f32), out((8, 128), f32)),
            scratch=[pltpu.VMEM((4, mine, head + ff), f32)], smem=1, name="final", keep_out=False,
            cold=(2, 3, 4),
        )
        small = small[:3, :mine]

    if native:
        v.mixed = place_rows(tokens, v.e, v.eo, "place_mixed")
        v.input_grad = place_rows(cotangent, v.dx, v.dxo, "place_input_grad")
    mixed, input_grad = v.mixed, v.input_grad

    if native:
        mlp_sum = native_scatter(mlp_grads)
        up_sum, down_grad = mlp_sum[:, :ff], mlp_sum[:, ff:]
        back = exchange([up_sum[j * mine : (j + 1) * mine] for j in range(4)], member)
        up_grad = jnp.stack([b.reshape(mine, seqs, ff // seqs) for b in back], axis=2)
        up_grad = up_grad.reshape(mine, units)
        step = part // BLOCKS
        out_mine = jnp.concatenate(
            [
                jnp.concatenate([b[j * step : (j + 1) * step, head:] for j in range(4)], axis=1)
                for b in attn_grads
            ],
            axis=0,
        )
        out_mine = out_mine.astype(f32).reshape(4, 1, HEAD_DIM, width)
        slots = (jnp.arange(4) == head_set).astype(f32)[None, :, None, None]
        out_all = (out_mine * slots).reshape(width, width)
        out_grad = lax.psum_scatter(out_all, ("seq", "grp"), scatter_dimension=0, tiled=True)
        attn_sum = native_scatter([b[:, :head] for b in attn_grads])
        back = exchange([attn_sum[j * mine : (j + 1) * mine] for j in range(4)], member)
        by_head = [b[:, : 3 * part].reshape(mine, 3, 4, HEAD_DIM) for b in back]
        qkv_grad = jnp.stack([by_head[HEAD_OF.index(p)] for p in range(4)], axis=3)
        qkv_grad = qkv_grad.reshape(mine, 3 * width)
        small = sum(b[:, 3 * part : 3 * part + 3] for b in back).T
    return (
        mixed,
        input_grad,
        qkv_grad,
        out_grad,
        up_grad,
        down_grad,
        small[0],
        small[1],
        small[2],
    )


def solution(mesh):
    placed = (
        P("seq", "grp", None),
        P("seq", None),
        P("seq", None),
        P(("seq", "grp"), None),
        P(("seq", "grp"), None),
        P(("seq", "grp"), None),
        P(("seq", "grp"), None),
        P(("seq", "grp")),
        P(("seq", "grp")),
        P(("seq", "grp")),
        P("seq", "grp", None),
    )
    return jax.shard_map(
        on_device,
        mesh=mesh,
        in_specs=placed,
        out_specs=(
            P("seq", "grp", None),
            P("seq", "grp", None),
            P(("seq", "grp"), None),
            P(("seq", "grp"), None),
            P(("seq", "grp"), None),
            P(("seq", "grp"), None),
            P(("seq", "grp")),
            P(("seq", "grp")),
            P(("seq", "grp")),
        ),
        check_vma=False,
    )
```

```python
import jax
import jax.numpy as jnp
from jax import lax
from jax.experimental import pallas as pl
from jax.experimental.pallas import tpu as pltpu
from jax.sharding import PartitionSpec as P

HEAD_DIM = 64
SEG_COUNT = 4
BLOCKS = 8
epsilon = 1e-06
masked = -1e30
f32 = jnp.float32
bf16 = jnp.bfloat16
gelu_scale = 0.7978845608028654
gelu_cubic = 0.044715

NN = (((1,), (0,)), ((), ()))
NT = (((1,), (1,)), ((), ()))
TN = (((0,), (0,)), ((), ()))


def mm(a, b, dims=NN):
    return lax.dot_general(a, b, dims, preferred_element_type=f32)


VM = pl.BlockSpec(memory_space=pltpu.VMEM)
SM = pl.BlockSpec(memory_space=pltpu.SMEM)
MIB = 1024 * 1024


def call(
    body, args, outs, scratch=(), smem=0, flops=0, name=None, limit=8, keep=True, keep_out=True,
    cold=(), free=(),
):
    moved = sum(a.size * a.dtype.itemsize for a in args)
    moved += sum(o.size * o.dtype.itemsize for o in outs)
    if keep:
        args = tuple(
            a
            if n < smem or n in free
            else pltpu.with_memory_space_constraint(a, pltpu.HBM if n in cold else pltpu.VMEM)
            for n, a in enumerate(args)
        )
    if keep and keep_out:
        shapes = tuple(pltpu.VMEM(o.shape, o.dtype) for o in outs)
    else:
        shapes = tuple(outs)
    return pl.pallas_call(
        body,
        out_shape=shapes,
        in_specs=[SM] * smem + [VM] * (len(args) - smem),
        out_specs=tuple([VM] * len(outs)),
        scratch_shapes=list(scratch),
        cost_estimate=pl.CostEstimate(flops=flops, bytes_accessed=moved, transcendentals=0),
        compiler_params=pltpu.CompilerParams(vmem_limit_bytes=limit * MIB),
        name=name,
    )(*args)


def out(shape, dtype):
    return jax.ShapeDtypeStruct(shape, dtype)


def pick_body(meta, pos_ref, src_ref, own_ref, oth_ref):
    rows, span = pos_ref.shape[1], src_ref.shape[1]
    core, base = meta[0], meta[1]
    lane = lax.broadcasted_iota(jnp.int32, (rows, span), 1) + base
    for half, ref in ((0, own_ref), (1, oth_ref)):
        seq = core if half == 0 else 1 - core
        hot = jnp.where(pos_ref[half] == lane, 1.0, 0.0).astype(bf16)
        src = src_ref[seq]
        ref[...] = mm(hot, src).astype(bf16)


def place_body(meta, pos_ref, base_ref, own_ref, oth_ref, out_ref):
    rows, span = pos_ref.shape[2], base_ref.shape[1]
    core, base = meta[0], meta[1]
    row = lax.broadcasted_iota(jnp.int32, (span, rows), 0) + base
    for half, ref in ((0, own_ref), (1, oth_ref)):
        seq = core if half == 0 else 1 - core
        hot = jnp.where(pos_ref[half] == row, 1.0, 0.0).astype(bf16)
        added = mm(hot, ref[...])
        out_ref[seq] = (base_ref[seq].astype(f32) + added).astype(bf16)


def attn_fwd_body(
    idx, xo_ref, xt_ref, segc_ref, segr_ref, *refs
):
    packs = refs[:BLOCKS]
    a_ref, qkv_ref, p_ref, o_ref, bo_ref, bt_ref, wq_ref, wo_ref, gr_ref, r_ref, gcol = refs[BLOCKS:]
    rows, width = xo_ref.shape
    part = width // 4
    qcols = 3 * part
    blk = width // BLOCKS
    ob = part // BLOCKS
    for b, pk in enumerate(packs):
        s = idx[b]
        off = pl.multiple_of(s * blk, blk)
        wq_ref[pl.ds(off, blk), :] = pk[:, :qcols]
        gcol[pl.ds(off, blk), :] = pk[:, qcols : qcols + 128]
        off2 = pl.multiple_of(s * ob, ob)
        for j in range(4):
            wo_ref[pl.ds(off2, ob), j * part : (j + 1) * part] = pk[
                j * ob : (j + 1) * ob, qcols + 128 :
            ]
    eye = (
        lax.broadcasted_iota(jnp.int32, (8, 128), 0) == lax.broadcasted_iota(jnp.int32, (8, 128), 1)
    ).astype(f32).astype(bf16)
    gr = mm(eye, gcol[...], NT)
    gr_ref[...] = gr
    gain = gr[0:1]
    for half, x_ref in ((0, xo_ref), (1, xt_ref)):
        span = pl.ds(half * rows, rows)
        xb = x_ref[...]
        x = xb.astype(f32)
        scale = lax.rsqrt(jnp.mean(x * x, axis=-1, keepdims=True) + epsilon)
        a_ref[span, :] = (x * scale * gain).astype(bf16)
        r_ref[span, :] = mm(xb, gcol[...])

    def project(i, carry):
        cols = pl.ds(pl.multiple_of(i * part, part), part)
        qkv_ref[:, cols] = mm(a_ref[...], wq_ref[:, cols]).astype(bf16)
        return carry

    lax.fori_loop(0, 3, project, 0)
    ri = lax.broadcasted_iota(jnp.int32, (rows, rows), 0)
    ci = lax.broadcasted_iota(jnp.int32, (rows, rows), 1)
    causal = ci <= ri
    heads = part // HEAD_DIM
    score_scale = HEAD_DIM ** (-0.5)
    for half in range(2):
        allowed = causal & (segc_ref[half] == segr_ref[half])
        span = pl.ds(half * rows, rows)
        for h in range(heads):
            q = qkv_ref[span, h * HEAD_DIM : (h + 1) * HEAD_DIM]
            k = qkv_ref[span, part + h * HEAD_DIM : part + (h + 1) * HEAD_DIM]
            v = qkv_ref[span, 2 * part + h * HEAD_DIM : 2 * part + (h + 1) * HEAD_DIM]
            logits = jnp.where(allowed, mm(q, k, NT) * score_scale, masked)
            e = jnp.exp(logits - jnp.max(logits, axis=-1, keepdims=True))
            p = e * (1.0 / jnp.sum(e, axis=-1, keepdims=True))
            p_ref[half * heads + h] = p
            o_ref[span, h * HEAD_DIM : (h + 1) * HEAD_DIM] = mm(p.astype(bf16), v).astype(bf16)

    def project_out(i, carry):
        cols = pl.ds(pl.multiple_of(i * part, part), part)
        res = mm(o_ref[...], wo_ref[:, cols]).astype(bf16)
        bo_ref[:, cols] = res[:rows]
        bt_ref[:, cols] = res[rows:]
        return carry

    lax.fori_loop(0, 4, project_out, 0)


def norm_body(t_ref, u_ref, x_ref, gr_ref, m_ref):
    h = x_ref[...].astype(f32) + (t_ref[...].astype(f32) + u_ref[...].astype(f32))
    scale = lax.rsqrt(jnp.mean(h * h, axis=-1, keepdims=True) + epsilon)
    m_ref[...] = (h * scale * gr_ref[1:2]).astype(bf16)


def turn_body(a_ref, o_ref, at_ref, ot_ref):
    tile = 256

    def step(i, carry):
        cols = pl.ds(pl.multiple_of(i * tile, tile), tile)
        at_ref[cols, :] = a_ref[:, cols].T
        return carry

    lax.fori_loop(0, a_ref.shape[1] // tile, step, 0)
    ot_ref[...] = o_ref[...].T


def mlp_body(idx, mo_ref, mt_ref, co_ref, ct_ref, r_ref, *refs):
    packs, rest = refs[:BLOCKS], refs[BLOCKS:]
    g_ref, du_ref, db_ref, wu_ref, wd_ref, dmo_ref, dmt_ref = rest
    rows, width = mo_ref.shape
    units = wu_ref.shape[1]
    blk, sub = width // BLOCKS, units // BLOCKS
    for b in range(BLOCKS):
        wu_ref[pl.ds(pl.multiple_of(idx[b] * blk, blk), blk), :] = packs[b][:, :units]
        wd_ref[pl.ds(pl.multiple_of(idx[b] * sub, sub), sub), :] = packs[b][:, units:]
    r = r_ref[:, 2:3]
    db_ref[:rows, :] = (r[:rows] * co_ref[...].astype(f32)).astype(bf16)
    db_ref[rows:, :] = (r[rows:] * ct_ref[...].astype(f32)).astype(bf16)
    tile = 256

    def step(i, carry):
        cols = pl.ds(pl.multiple_of(i * tile, tile), tile)
        for half, m_ref in ((0, mo_ref), (1, mt_ref)):
            span = pl.ds(half * rows, rows)
            u = mm(m_ref[...], wu_ref[:, cols])
            u2 = u * u
            th = jnp.tanh(gelu_scale * (u + gelu_cubic * (u2 * u)))
            half_up = 0.5 * (1.0 + th)
            g_ref[span, cols] = (u * half_up).astype(bf16)
            slope = half_up + (0.5 * u) * (1.0 - th * th) * (
                gelu_scale * (1.0 + 3.0 * gelu_cubic * u2)
            )
            dg = mm(db_ref[span, :], wd_ref[cols, :], NT)
            du_ref[span, cols] = (dg * slope).astype(bf16)
        return carry

    lax.fori_loop(0, units // tile, step, 0)

    def step2(i, carry):
        cols = pl.ds(pl.multiple_of(i * tile, tile), tile)
        dm = mm(du_ref[...], wu_ref[cols, :], NT).astype(bf16)
        dmo_ref[:, cols] = dm[:rows]
        dmt_ref[:, cols] = dm[rows:]
        return carry

    lax.fori_loop(0, width // tile, step2, 0)


EARLY, LATE = (2, 3, 4, 5), (0, 1, 6, 7)


def grad_block(idx, b, ref, fm_ref, fg_ref, du_ref, db_ref, wu_ref, gcol, col_ref):
    width, units = fm_ref.shape[0], fg_ref.shape[0]
    blk, sub = width // BLOCKS, units // BLOCKS
    off = pl.ds(pl.multiple_of(idx[b] * blk, blk), blk)
    grad = mm(fm_ref[off, :], du_ref[...])
    ref[:, :units] = grad.astype(bf16)
    gain = jnp.sum(grad * wu_ref[off, :].astype(f32), axis=-1, keepdims=True)
    gain = gain / gcol[off, 1:2].astype(f32)
    col_ref[off, :] = jnp.broadcast_to(gain, (blk, 128))
    off = pl.ds(pl.multiple_of(idx[b] * sub, sub), sub)
    ref[:, units:] = mm(fg_ref[off, :], db_ref[...]).astype(bf16)


def early_grad_body(
    idx, g_ref, du_ref, db_ref, mo_ref, mt_ref, wu_ref, gcol, col_ref, fm_ref, fg_ref, *grads
):
    rows, width = mo_ref.shape
    tile = 256

    def turn_rows(i, carry):
        cols = pl.ds(pl.multiple_of(i * tile, tile), tile)
        fm_ref[cols, :rows] = mo_ref[:, cols].T
        fm_ref[cols, rows:] = mt_ref[:, cols].T
        fg_ref[cols, :] = g_ref[:, cols].T
        return carry

    lax.fori_loop(0, width // tile, turn_rows, 0)
    for b, ref in zip(EARLY, grads):
        grad_block(idx, b, ref, fm_ref, fg_ref, du_ref, db_ref, wu_ref, gcol, col_ref)


def late_grad_body(
    idx, g_ref, du_ref, db_ref, wu_ref, wd_ref, gcol, col_in, fm_ref, fg_ref, ao_ref, at_ref,
    co_ref, ct_ref, xo_ref, xt_ref, bo_ref, bt_ref, col_ref, *grads
):
    rows, width = bo_ref.shape
    tile = 256
    col_ref[...] = col_in[...]
    for b, ref in zip(LATE, grads):
        grad_block(idx, b, ref, fm_ref, fg_ref, du_ref, db_ref, wu_ref, gcol, col_ref)

    def step(i, carry):
        cols = pl.ds(pl.multiple_of(i * tile, tile), tile)
        res = mm(g_ref[...], wd_ref[:, cols])
        bo_ref[:, cols] = res[:rows].astype(bf16)
        bt_ref[:, cols] = res[rows:].astype(bf16)
        own, other = carry
        own += jnp.sum(
            (res[:rows] + ao_ref[:, cols].astype(f32)) * co_ref[:, cols].astype(f32),
            axis=-1, keepdims=True,
        )
        other += jnp.sum(
            (res[rows:] + at_ref[:, cols].astype(f32)) * ct_ref[:, cols].astype(f32),
            axis=-1, keepdims=True,
        )
        return own, other

    zero = jnp.zeros((rows, 1), f32)
    dots = lax.fori_loop(0, width // tile, step, (zero, zero))
    lane = lax.broadcasted_iota(jnp.int32, (rows, 128), 1)
    route = jnp.zeros((width, 128), f32)
    for d, x_ref in zip(dots, (xo_ref, xt_ref)):
        high = d.astype(bf16).astype(f32)
        two = jnp.where(lane == 0, high, jnp.where(lane == 1, d - high, 0.0)).astype(bf16)
        route += mm(x_ref[...], two, TN)
    total = jnp.sum(route[:, :2], axis=-1, keepdims=True)
    wide = lax.broadcasted_iota(jnp.int32, (width, 128), 1)
    col_ref[...] = jnp.where(wide == 1, col_ref[...], jnp.where(wide == 2, total, 0.0))


def hidden_grad_body(dt_ref, du_ref, bt_ref, bu_ref, x_ref, c_ref, r_ref, gr_ref, da_ref, dh_ref):
    dm = dt_ref[...].astype(f32) + du_ref[...].astype(f32)
    h = x_ref[...].astype(f32) + (bt_ref[...].astype(f32) + bu_ref[...].astype(f32))
    rows = h.shape[0]
    n = lax.rsqrt(jnp.mean(h * h, axis=-1, keepdims=True) + epsilon)
    t = dm * gr_ref[1:2]
    dh = n * t - h * (n * n * n) * jnp.mean(t * h, axis=-1, keepdims=True)
    dh_ref[...] = dh
    de = r_ref[:rows, 2:3] * c_ref[...].astype(f32)
    da_ref[...] = (de + dh).astype(bf16)


def result_body(at_ref, au_ref, mt_ref, mu_ref, c_ref, r_ref, e_ref, dr_ref):
    branch = (at_ref[...].astype(f32) + au_ref[...].astype(f32)) + (
        mt_ref[...].astype(f32) + mu_ref[...].astype(f32)
    )
    rows = branch.shape[0]
    e_ref[...] = (r_ref[:rows, 2:3] * branch).astype(bf16)
    dr = jnp.sum(c_ref[...].astype(f32) * branch, axis=-1, keepdims=True)
    dr_ref[...] = jnp.broadcast_to(dr, dr_ref.shape)


def attn_bwd_body(
    idx, at_ref, ot_ref, qkv_ref, p_ref, dao_ref, dat_ref, wq_ref, wo_ref, gcol, col_ref, *refs
):
    dqkv, near, far, (da,) = refs[0], refs[1:5], refs[5:7], refs[7:]
    rows, width = dao_ref.shape
    part = width // 4
    qcols = 3 * part
    heads = part // HEAD_DIM
    score_scale = HEAD_DIM ** (-0.5)
    da[:rows, :] = dao_ref[...]
    da[rows:, :] = dat_ref[...]
    for half in range(2):
        span = pl.ds(half * rows, rows)
        dmix = mm(da[span, :], wo_ref[...], NT).astype(bf16)
        for h in range(heads):
            lo, hi = h * HEAD_DIM, (h + 1) * HEAD_DIM
            q = qkv_ref[span, lo:hi]
            k = qkv_ref[span, part + lo : part + hi]
            v = qkv_ref[span, 2 * part + lo : 2 * part + hi]
            do = dmix[:, lo:hi]
            p = p_ref[half * heads + h]
            dp = mm(do, v, NT)
            ds = (p * (dp - jnp.sum(p * dp, axis=-1, keepdims=True))).astype(bf16)
            dqkv[span, lo:hi] = (mm(ds, k) * score_scale).astype(bf16)
            dqkv[span, part + lo : part + hi] = (mm(ds, q, TN) * score_scale).astype(bf16)
            dqkv[span, 2 * part + lo : 2 * part + hi] = mm(p.astype(bf16), do, TN).astype(bf16)
    blk = width // BLOCKS
    ob = part // BLOCKS
    lane = lax.broadcasted_iota(jnp.int32, (blk, 128), 1)
    for b in range(BLOCKS):
        s = idx[b]
        k = b // 2
        ref, row = (near[k], 0) if b % 2 == 0 else (far[(k + 3) % 4 // 2], (k + 3) % 2 * blk)
        rows_of = slice(row, row + blk)
        off = pl.ds(pl.multiple_of(s * blk, blk), blk)
        grad = mm(at_ref[off, :], dqkv[...])
        ref[rows_of, :qcols] = grad.astype(bf16)
        gain = jnp.sum(grad * wq_ref[off, :].astype(f32), axis=-1, keepdims=True)
        gain = gain / gcol[off, 0:1].astype(f32)
        ref[rows_of, qcols : qcols + 128] = jnp.where(lane == 0, gain, col_ref[off, :]).astype(bf16)
        og = mm(ot_ref[pl.ds(pl.multiple_of(s * ob, ob), ob), :], da[...]).astype(bf16)
        for j in range(4):
            ref[row + j * ob : row + (j + 1) * ob, qcols + 128 :] = og[:, j * part : (j + 1) * part]


def normed_grad_body(dqkv_ref, wq_ref, do_ref, dt_ref):
    rows, width = do_ref.shape
    tile = 256

    def step(i, carry):
        cols = pl.ds(pl.multiple_of(i * tile, tile), tile)
        d = mm(dqkv_ref[...], wq_ref[cols, :], NT).astype(bf16)
        do_ref[:, cols] = d[:rows]
        dt_ref[:, cols] = d[rows:]
        return carry

    lax.fori_loop(0, width // tile, step, 0)


def input_grad_body(t_ref, u_ref, x_ref, dh_ref, dr_ref, gr_ref, dx_ref):
    d = t_ref[...].astype(f32) + u_ref[...].astype(f32)
    x = x_ref[...].astype(f32)
    m = lax.rsqrt(jnp.mean(x * x, axis=-1, keepdims=True) + epsilon)
    s = d * gr_ref[0:1]
    dxn = m * s - x * (m * m * m) * jnp.mean(s * x, axis=-1, keepdims=True)
    dx_ref[...] = (dxn + dh_ref[...] + dr_ref[:, 0:1] * gr_ref[2:3]).astype(bf16)


HEAD_OF = (0, 2, 1, 3)


def pack_body(meta, qkv_ref, up_ref, gains_ref, *refs):
    outs, (tmp,) = refs[:4], refs[4:]
    width, units = qkv_ref.shape[1] // 3, up_ref.shape[1]
    part = width // 4
    sub = units // (4 * BLOCKS)
    for j in range(4):
        p = HEAD_OF[j]
        for t in range(3):
            for z in range(4):
                src = t * width + (4 * z + p) * HEAD_DIM
                dst = t * part + z * HEAD_DIM
                tmp[j, :, dst : dst + HEAD_DIM] = qkv_ref[:, src : src + HEAD_DIM]
        tmp[j, :, 3 * part : 3 * part + 128] = gains_ref[...]
        for s in range(BLOCKS):
            dst = 3 * part + 128 + s * sub
            src = (4 * s + j) * sub
            tmp[j, :, dst : dst + sub] = up_ref[:, src : src + sub]
    for k, ref in enumerate(outs):
        ref[...] = tmp[meta[3] ^ k]


def join_body(meta, c0, c1, c2, c3, own_ref, moved_ref, down_ref, attn_ref, mlp_ref):
    mine, width = own_ref.shape
    part = width // 4
    head = 3 * part + 128
    for k, ref in enumerate((c0, c1, c2, c3)):
        off = pl.ds(pl.multiple_of((meta[3] ^ k) * mine, mine), mine)
        attn_ref[off, :head] = ref[:, :head]
        mlp_ref[off, : mlp_ref.shape[1] - width] = ref[:, head:]
    mlp_ref[:, mlp_ref.shape[1] - width :] = down_ref[...]
    take = jnp.full(own_ref.shape, meta[4]) == 1
    rows = jnp.where(take, moved_ref[...].astype(f32), own_ref[...].astype(f32)).astype(bf16)
    for j in range(4):
        attn_ref[j * mine : (j + 1) * mine, head:] = rows[:, j * part : (j + 1) * part]


def split_body(
    meta, m0, m1, m2, a0, a1, a2, c0, c1, c2, c3, down_ref, out_ref, tm, ta
):
    mine, width = out_ref.shape
    units = m0.shape[1] - width
    part = width // 4
    head = 3 * part + 128
    for n in range(4):
        span = pl.ds(n * mine, mine)
        total = (m0[span, :].astype(f32) + m1[span, :].astype(f32)) + m2[span, :].astype(f32)
        down_ref[span, :] = total[:, units:]
        tm[span, :] = total[:, :units]
        late = pl.ds((4 + n) * mine, mine)
        total = (a0[span, :].astype(f32) + a1[late, :].astype(f32)) + a2[span, :].astype(f32)
        ta[span, :] = total[:, :head]
        out_ref[:, n * part : (n + 1) * part] = total[:, head:]
    for k, ref in enumerate((c0, c1, c2, c3)):
        off = pl.ds(pl.multiple_of((meta[3] ^ k) * mine, mine), mine)
        ref[:, :head] = ta[off, :].astype(ref.dtype)
        ref[:, head:] = tm[off, :].astype(ref.dtype)


def final_body(meta, c0, c1, c2, c3, qkv_ref, up_ref, small_ref, tmp):
    mine = qkv_ref.shape[0]
    width = qkv_ref.shape[1] // 3
    part = width // 4
    head = 3 * part + 128
    sub = up_ref.shape[1] // (4 * BLOCKS)
    for k, ref in enumerate((c0, c1, c2, c3)):
        tmp[meta[3] ^ k] = ref[...].astype(f32)
    for j in range(4):
        for t in range(3):
            for z in range(4):
                dst = t * width + (4 * z + HEAD_OF[j]) * HEAD_DIM
                src = t * part + z * HEAD_DIM
                qkv_ref[:, dst : dst + HEAD_DIM] = tmp[j, :, src : src + HEAD_DIM]
        for s in range(BLOCKS):
            dst = (4 * s + j) * sub
            up_ref[:, dst : dst + sub] = tmp[j, :, head + s * sub : head + (s + 1) * sub]
    last = slice(3 * part, head)
    small = (tmp[0, :, last] + tmp[1, :, last]) + (tmp[2, :, last] + tmp[3, :, last])
    wide = jnp.concatenate([small, jnp.zeros((128 - mine, 128), f32)], axis=0)
    small_ref[...] = wide.T[:8]


def flip_bit(v, axis, size, mask):
    return lax.ppermute(v, axis, [(i, i ^ mask) for i in range(size)])


def swap_core(v):
    return flip_bit(v, "grp", 4, 1)


def swap_pair(v):
    return flip_bit(v, "grp", 4, 2)


def swap_side(v, seqs):
    return flip_bit(v, "seq", seqs, 1)


def shift_one(v, seqs):
    return lax.ppermute(v, "seq", [(i, (i + 2) % seqs) for i in range(seqs)])


def reorder(parts, member):
    low = (member & 1) == 1
    high = (member & 2) == 2
    res = []
    for j in range(4):
        straight = jnp.where(low, parts[j ^ 1], parts[j])
        crossed = jnp.where(low, parts[j ^ 3], parts[j ^ 2])
        res.append(jnp.where(high, crossed, straight))
    return res


def exchange(chunks, member):
    rel = reorder(chunks, member)
    got = [rel[0]] + [flip_bit(rel[k], "grp", 4, k) for k in range(1, 4)]
    return reorder(got, member)


def native_gather(pack):
    full = lax.all_gather(pack, "seq", axis=0, tiled=True)
    return list(full.reshape((BLOCKS, -1) + full.shape[1:]))


def native_scatter(blocks):
    full = jnp.concatenate(blocks, axis=0)
    return lax.psum_scatter(full.astype(f32), "seq", scatter_dimension=0, tiled=True)


def add(*parts):
    total = parts[0].astype(f32)
    for p in parts[1:]:
        total = total + p.astype(f32)
    return total.astype(bf16)


class Flow:
    def __getitem__(self, name):
        return self.__dict__[name]

    def __setitem__(self, name, value):
        self.__dict__[name] = value

    def order(self, value, name):
        token = lax.create_token()
        token, self[name] = lax.optimization_barrier((token, self[name]))
        return lax.optimization_barrier((token, value))[1]

    def sync(self, *names):
        held = [n for n in names if n in self.__dict__]
        done = lax.optimization_barrier(tuple(self[n] for n in held))
        for n, value in zip(held, done):
            self[n] = value


def on_device(
    tokens,
    segments,
    routed,
    qkv_weight,
    out_weight,
    up_weight,
    down_weight,
    attn_gain,
    mlp_gain,
    router_weight,
    cotangent,
):
    groups, seqs = lax.axis_size("grp"), lax.axis_size("seq")
    member, place = lax.axis_index("grp"), lax.axis_index("seq")
    seq_dev, span, width = tokens.shape
    rows = routed.shape[1]
    units = down_weight.shape[0] * groups * seqs
    if groups != 4 or seq_dev != 2:
        raise ValueError("mesh")
    native = seqs != BLOCKS
    part, ff = width // 4, units // 4
    core, pair = member & 1, member >> 1
    mine = qkv_weight.shape[0]
    head = 3 * part + 128
    both = 2 * rows
    odd = (place ^ member) & 1
    meta = jnp.stack([core, member * span, pair, member, odd]).astype(jnp.int32)
    half = out((rows, width), bf16)
    v = Flow()

    queue = []

    chain = []

    def hop(name, t, lag):
        if len(chain) >= lag:
            t = v.order(t, chain[-lag])
        chain.append(name)
        v[name] = shift_one(t, seqs)

    def side(name, t, lag):
        if len(queue) >= lag:
            t = v.order(t, queue[-lag])
        queue.append(name)
        v[name] = swap_side(t, seqs)


    flip = core == 1
    pos = jnp.where(flip, routed[::-1], routed)
    starts = jnp.stack(
        [jnp.sum((segments < n).astype(jnp.int32), axis=1) for n in range(1, SEG_COUNT)], axis=0
    )
    seg = jnp.sum((routed[None] >= starts[:, :, None]).astype(jnp.int32), axis=0)
    seg = jnp.where(flip, seg[::-1], seg)
    pos_col, pos_row = pos[:, :, None], pos[:, None, :]
    seg_col, seg_row = seg[:, :, None], seg[:, None, :]

    def pick(source, name):
        return call(
            pick_body, (meta, pos_col, source), (half, half), smem=1,
            flops=4 * rows * span * width, name=name, keep=False, limit=24,
        )

    gains = jnp.stack([attn_gain, mlp_gain, router_weight], axis=1)
    gains = jnp.pad(gains, ((0, 0), (0, 125)))
    if native:
        qkv_view = qkv_weight.reshape(mine, 3, 4, 4, HEAD_DIM)
        chunks = [
            jnp.concatenate([qkv_view[:, :, :, p].reshape(mine, 3 * part), gains], axis=1)
            for p in HEAD_OF
        ]
        qkv_blocks = native_gather(jnp.concatenate(exchange(chunks, member), axis=0))
        out_full = lax.all_gather(out_weight, ("seq", "grp"), axis=0, tiled=True)
        out_view = out_full.reshape(4, 4, HEAD_DIM, width)
        head_set = 2 * core + pair
        out_rows = lax.dynamic_index_in_dim(out_view, head_set, 1, keepdims=False)
        out_rows = out_rows.reshape(BLOCKS, part // BLOCKS, width)
        attn_packs = [
            jnp.concatenate(
                [q, jnp.concatenate([o[:, j * part : (j + 1) * part] for j in range(4)], axis=0)],
                axis=1,
            )
            for q, o in zip(qkv_blocks, out_rows)
        ]
        up_view = up_weight.reshape(mine, seqs, 4, ff // seqs)
        chunks = [up_view[:, :, j].reshape(mine, ff) for j in range(4)]
        up_rows = jnp.concatenate(exchange(chunks, member), axis=0)
        mlp_packs = native_gather(jnp.concatenate([up_rows, down_weight], axis=1))
        order = jnp.arange(BLOCKS, dtype=jnp.int32)
        x_mine, x_send = pick(tokens, "pick_tokens")
        v.tx = add(x_mine, swap_core(x_send))
        v.yx = swap_pair(v.tx)
        v.x = v.tx + v.yx
        v.xo = swap_core(v.x)
        c_mine, c_send = pick(cotangent, "pick_cotangent")
        v.tc = add(c_mine, swap_core(c_send))
    else:
        order = jnp.stack(
            [((place ^ r) - 2 * k) % seqs for k in range(BLOCKS // 2) for r in range(2)]
        ).astype(jnp.int32)
        swaps = [
            (s * 4 + g, (s ^ 1) * 4 + (g ^ 1)) for s in range(seqs) for g in range(4) if (s ^ g) & 1
        ]
        chunk = out((mine, head + ff), bf16)
        chunks = call(
            pack_body, (meta, qkv_weight, up_weight, gains), (chunk,) * 4,
            scratch=[pltpu.VMEM((4, mine, head + ff), bf16)], smem=1, name="pack", cold=(1, 2, 3),
        )
        v.k0, v.k1, v.k2, v.k3 = chunks
        v.tokens = tokens
        v.sync("k1", "k2", "k3", "tokens")
        got = [v.k0] + [flip_bit(v["k%d" % k], "grp", 4, k) for k in range(1, 4)]
        x_mine, x_send = pick(v.tokens, "pick_tokens")
        moved = lax.ppermute(out_weight, ("seq", "grp"), swaps)
        v.a0, v.m0 = call(
            join_body, (meta, *got, out_weight, moved, down_weight),
            (out((mine * 4, width + 128), bf16), out((mine * 4, ff + width), bf16)), smem=1,
            name="join", cold=(2, 3, 4, 5, 6, 7),
        )
        v.tx = add(x_mine, swap_core(x_send))
        v.sync("a0", "m0", "tx")
        for n, k in (('a', 1), ('m', 1), ('a', 2), ('a', 3), ('m', 2), ('m', 3)):
            hop("%s%d" % (n, k), v["%s%d" % (n, k - 1)], 3)
        v.yx = swap_pair(v.tx)
        v.x = v.tx + v.yx
        v.xo = swap_core(v.x)
        for n, k in (('m', 0), ('a', 0), ('a', 1), ('a', 2), ('a', 3), ('m', 1), ('m', 2), ('m', 3)):
            side("x%s%d" % (n, k), v["%s%d" % (n, k)], 2)
        c_mine, c_send = pick(cotangent, "pick_cotangent")
        v.tc = add(c_mine, swap_core(c_send))
        v.yc = swap_pair(v.tc)
        v.sync("x", "xo", "m1")
        v.sync("tc", "xo")
        attn_names = [n + str(k) for k in range(4) for n in ("a", "xa")]
        attn_packs = [v[n] for n in attn_names]

    a, qkv, probs, mix, ba_o, ba_t, w_qkv, w_out, gain_rows, r, gain_cols = call(
        attn_fwd_body,
        (order, v.x, v.xo, seg_col, seg_row, *attn_packs),
        (
            out((both, width), bf16),
            out((both, 3 * part), bf16),
            out((2 * part // HEAD_DIM, rows, rows), f32),
            out((both, part), bf16),
            half,
            half,
            out((width, 3 * part), bf16),
            out((part, width), bf16),
            out((8, width), f32),
            out((both, 128), f32),
            out((width, 128), bf16),
        ),
        smem=1,
        flops=2 * both * width * width,
        name="attn_fwd",
        cold=range(1, 13),
    )
    v.a, v.mix = a, mix
    v.tb = add(ba_o, swap_core(ba_t))
    v.sync("tb", "a", "mix", "xm1")
    v.yb = swap_pair(v.tb)
    if native:
        v.yc = swap_pair(v.tc)
    a_turned, mix_turned = call(
        turn_body, (v.a, v.mix), (out((width, both), bf16), out((part, both), bf16)),
        name="turn",
    )
    v.c = v.tc + v.yc
    v.co = swap_core(v.c)
    v.sync("yb", "tb", "co", "c", "xm2")
    (v.h,) = call(
        norm_body, (v.tb, v.yb, v.x, gain_rows), (half,), name="norm_two", free=(0, 1, 2)
    )
    v.ho = swap_core(v.h)
    if not native:
        mlp_packs = [v[n + str(k)] for k in range(4) for n in ("m", "xm")]
    g, du, db, w_up, w_down, dm_o, dm_t = call(
        mlp_body,
        (order, v.h, v.ho, v.c, v.co, r, *mlp_packs),
        (
            out((both, ff), bf16),
            out((both, ff), bf16),
            out((both, width), bf16),
            out((width, ff), bf16),
            out((ff, width), bf16),
            half,
            half,
        ),
        smem=1,
        flops=6 * both * width * ff,
        name="mlp",
        cold=(2, 3, 4, *range(6, 14)),
    )

    v.du = du
    v.td = add(dm_o, swap_core(dm_t))
    v.sync("td", "du")
    v.yd = swap_pair(v.td)
    packet = out((width // BLOCKS, ff + width), bf16)
    col, turned_m, turned_g, *first = call(
        early_grad_body,
        (order, g, v.du, db, v.h, v.ho, w_up, gain_cols),
        (
            out((width, 128), f32), out((width, both), bf16), out((ff, both), bf16),
            *([packet] * 4),
        ),
        smem=1,
        flops=2 * both * width * ff,
        name="early_grad",
        cold=(5,),
    )
    v.g = g
    v.f0, v.f1 = first[1], first[3]
    v.sync("f0", "f1", "g")
    first[1], first[3] = v.f0, v.f1
    bm_o, bm_t, cols, *last = call(
        late_grad_body,
        (
            order, v.g, v.du, db, w_up, w_down, gain_cols, col, turned_m, turned_g, ba_o, ba_t,
            v.c, v.co, v.x, v.xo,
        ),
        (half, half, out((width, 128), f32), *([packet] * 4)),
        smem=1,
        flops=4 * both * width * ff,
        name="late_grad",
        cold=(12, 13, 14, 15),
    )
    mlp_grads = [*last[:2], *first, *last[2:]]
    v.bm, v.bn = bm_o, bm_t
    v.tm = add(v.bm, swap_core(v.bn))
    parts = {"m": mlp_grads}
    queue.clear()
    chain.clear()
    v.__dict__.update({n + str(k): None for n in ("xm", "xa") for k in range(4)})
    if not native:
        for n, k in (('m', 1), ('m', 2)):
            side("x%s%d" % (n, k), parts[n][2 * k + 1], 2)
    v.sync("yd", "td", "bm")
    da_own, dh = call(
        hidden_grad_body,
        (v.td, v.yd, v.tb, v.yb, v.x, v.c, r, gain_rows),
        (half, out((rows, width), f32)),
        name="hidden_grad",
        free=range(6),
    )
    v.da = da_own
    v.dao = swap_core(da_own)
    def attention_back(v):
        dqkv, *attn_grads = call(
            attn_bwd_body,
            (
                order, a_turned, mix_turned, qkv, probs, v.da, v.dao, w_qkv, w_out,
                gain_cols, cols,
            ),
            (
                out((both, 3 * part), bf16),
                *([out((width // BLOCKS, width + 128), bf16)] * 4),
                *([out((2 * width // BLOCKS, width + 128), bf16)] * 2),
            ),
            scratch=[pltpu.VMEM((both, width), bf16)],
            smem=1,
            flops=3 * both * width * width,
            name="attn_bwd",
            free=(6,),
        )
        v.dqkv = dqkv
        return attn_grads

    def normed_back(dqkv):
        return call(
            normed_grad_body, (dqkv, w_qkv), (half, half), flops=2 * both * width * 3 * part,
            name="normed_grad",
        )

    def give():
        return call(
            result_body,
            (v.tb, v.yb, v.tm, v.ym, v.c, r),
            (half, out((rows, 128), f32)),
            name="result",
            free=range(5),
        )

    def take(dr):
        return call(
            input_grad_body, (v.tx2, v.yx2, v.x, dh, dr, gain_rows), (half,),
            name="input_grad", free=range(3),
        )[0]

    def place_rows(base, own, other, name):
        return call(
            place_body, (meta, pos_row, base, own, other), (out(base.shape, bf16),), smem=1,
            flops=4 * rows * span * width, name=name, keep=False, limit=24,
        )[0]

    if native:
        attn_grads = attention_back(v)
        blk = width // BLOCKS
        far = {(k + 3) % 4: attn_grads[4 + (k + 3) % 4 // 2] for k in range(4)}
        attn_grads = [
            attn_grads[k] if r == 0 else far[(k + 3) % 4][(k + 3) % 2 * blk :][:blk]
            for k in range(4)
            for r in range(2)
        ]
        dx_o, dx_t = normed_back(v.dqkv)
        v.ym = swap_pair(v.tm)
        v.tx2 = add(dx_o, swap_core(dx_t))
        v.yx2 = swap_pair(v.tx2)
        v.e, dr = give()
        v.eo = swap_core(v.e)
        v.dx = take(dr)
        v.dxo = swap_core(v.dx)
    else:
        attn_grads = attention_back(v)
        v.dxm, v.dxs = normed_back(v.dqkv)
        parts["a"] = attn_grads
        for k in range(4):
            v["m%d" % k], v["a%d" % k] = mlp_grads[2 * k], attn_grads[k]
        v.ym = swap_pair(v.tm)
        for n, k in (('m', 3), ('a', 4), ('m', 0), ('a', 5)):
            side("x%s%d" % (n, k), parts[n][2 * k + 1 if n == "m" else k], 2)
        blk = width // BLOCKS
        v.tx2 = add(v.dxm, swap_core(v.dxs))

        def step(n, k):
            across = v["xm%d" % k] if n == "m" else v["xa%d" % (4 + k // 3)]
            if n == "a":
                across = across[blk:] if k == 2 else across[:blk]
            terms = [v["%s%d" % (n, k)], across]
            if k > 1:
                terms.append(v["z%s%d" % (n, k - 1)])
            hop("z%s%d" % (n, k), add(*terms), 2)

        for n, k in (('m', 1), ('m', 2), ('a', 1), ('a', 2), ('a', 3), ('m', 3)):
            if (n, k) == ("a", 1):
                v.sync("tx2", "a1")
                v.yx2 = swap_pair(v.tx2)
            if (n, k) == ("a", 2):
                v.sync("ym", "tm", "a2")
                v.e, dr = give()
                v.eo = swap_core(v.e)
            if (n, k) == ("m", 3):
                v.dx = take(dr)
                v.dxo = swap_core(v.dx)
                v.mixed = place_rows(tokens, v.e, v.eo, "place_mixed")
                v.sync("mixed", "dxo", "dx", "m3")
            step(n, k)
        v.input_grad = place_rows(cotangent, v.dx, v.dxo, "place_input_grad")
        v.sync("input_grad", "m0")
        piece = [out((mine, head + ff), f32)] + [out((mine, head + ff), bf16)] * 3
        *cut, down_grad, og = call(
            split_body,
            (meta, v.m0, v.xm0, v.zm3, v.a0, v.xa5, v.za3),
            (*piece, out((4 * mine, width), f32), out((mine, width), f32)),
            scratch=[pltpu.VMEM((4 * mine, ff), f32), pltpu.VMEM((4 * mine, head), f32)], smem=1,
            name="split", cold=(2, 3, 5, 6),
        )
        cut = [cut[0]] + [flip_bit(cut[k], "grp", 4, k) for k in range(1, 4)]
        out_moved = lax.ppermute(og, ("seq", "grp"), swaps)
        out_grad = jnp.where(odd == 1, out_moved, og)
        qkv_grad, up_grad, small = call(
            final_body, (meta, *cut),
            (out((mine, 3 * width), f32), out((mine, units), f32), out((8, 128), f32)),
            scratch=[pltpu.VMEM((4, mine, head + ff), f32)], smem=1, name="final", keep_out=False,
            cold=(2, 3, 4),
        )
        small = small[:3, :mine]

    if native:
        v.mixed = place_rows(tokens, v.e, v.eo, "place_mixed")
        v.input_grad = place_rows(cotangent, v.dx, v.dxo, "place_input_grad")
    mixed, input_grad = v.mixed, v.input_grad

    if native:
        mlp_sum = native_scatter(mlp_grads)
        up_sum, down_grad = mlp_sum[:, :ff], mlp_sum[:, ff:]
        back = exchange([up_sum[j * mine : (j + 1) * mine] for j in range(4)], member)
        up_grad = jnp.stack([b.reshape(mine, seqs, ff // seqs) for b in back], axis=2)
        up_grad = up_grad.reshape(mine, units)
        step = part // BLOCKS
        out_mine = jnp.concatenate(
            [
                jnp.concatenate([b[j * step : (j + 1) * step, head:] for j in range(4)], axis=1)
                for b in attn_grads
            ],
            axis=0,
        )
        out_mine = out_mine.astype(f32).reshape(4, 1, HEAD_DIM, width)
        slots = (jnp.arange(4) == head_set).astype(f32)[None, :, None, None]
        out_all = (out_mine * slots).reshape(width, width)
        out_grad = lax.psum_scatter(out_all, ("seq", "grp"), scatter_dimension=0, tiled=True)
        attn_sum = native_scatter([b[:, :head] for b in attn_grads])
        back = exchange([attn_sum[j * mine : (j + 1) * mine] for j in range(4)], member)
        by_head = [b[:, : 3 * part].reshape(mine, 3, 4, HEAD_DIM) for b in back]
        qkv_grad = jnp.stack([by_head[HEAD_OF.index(p)] for p in range(4)], axis=3)
        qkv_grad = qkv_grad.reshape(mine, 3 * width)
        small = sum(b[:, 3 * part : 3 * part + 3] for b in back).T
    return (
        mixed,
        input_grad,
        qkv_grad,
        out_grad,
        up_grad,
        down_grad,
        small[0],
        small[1],
        small[2],
    )


def solution(mesh):
    placed = (
        P("seq", "grp", None),
        P("seq", None),
        P("seq", None),
        P(("seq", "grp"), None),
        P(("seq", "grp"), None),
        P(("seq", "grp"), None),
        P(("seq", "grp"), None),
        P(("seq", "grp")),
        P(("seq", "grp")),
        P(("seq", "grp")),
        P("seq", "grp", None),
    )
    return jax.shard_map(
        on_device,
        mesh=mesh,
        in_specs=placed,
        out_specs=(
            P("seq", "grp", None),
            P("seq", "grp", None),
            P(("seq", "grp"), None),
            P(("seq", "grp"), None),
            P(("seq", "grp"), None),
            P(("seq", "grp"), None),
            P(("seq", "grp")),
            P(("seq", "grp")),
            P(("seq", "grp")),
        ),
        check_vma=False,
    )
```

```python
import jax
import jax.numpy as jnp
from jax import lax
from jax.experimental import pallas as pl
from jax.experimental.pallas import tpu as pltpu
from jax.sharding import PartitionSpec as P

HEAD_DIM = 64
SEG_COUNT = 4
BLOCKS = 8
epsilon = 1e-06
masked = -1e30
f32 = jnp.float32
bf16 = jnp.bfloat16
gelu_scale = 0.7978845608028654
gelu_cubic = 0.044715

NN = (((1,), (0,)), ((), ()))
NT = (((1,), (1,)), ((), ()))
TN = (((0,), (0,)), ((), ()))


def mm(a, b, dims=NN):
    return lax.dot_general(a, b, dims, preferred_element_type=f32)


VM = pl.BlockSpec(memory_space=pltpu.VMEM)
SM = pl.BlockSpec(memory_space=pltpu.SMEM)
MIB = 1024 * 1024


def call(
    body, args, outs, scratch=(), smem=0, flops=0, name=None, limit=8, keep=True, keep_out=True,
    cold=(), free=(),
):
    moved = sum(a.size * a.dtype.itemsize for a in args)
    moved += sum(o.size * o.dtype.itemsize for o in outs)
    if keep:
        args = tuple(
            a
            if n < smem or n in free
            else pltpu.with_memory_space_constraint(a, pltpu.HBM if n in cold else pltpu.VMEM)
            for n, a in enumerate(args)
        )
    if keep and keep_out:
        shapes = tuple(pltpu.VMEM(o.shape, o.dtype) for o in outs)
    else:
        shapes = tuple(outs)
    return pl.pallas_call(
        body,
        out_shape=shapes,
        in_specs=[SM] * smem + [VM] * (len(args) - smem),
        out_specs=tuple([VM] * len(outs)),
        scratch_shapes=list(scratch),
        cost_estimate=pl.CostEstimate(flops=flops, bytes_accessed=moved, transcendentals=0),
        compiler_params=pltpu.CompilerParams(vmem_limit_bytes=limit * MIB),
        name=name,
    )(*args)


def out(shape, dtype):
    return jax.ShapeDtypeStruct(shape, dtype)


def pick_body(meta, pos_ref, src_ref, own_ref, oth_ref):
    rows, span = pos_ref.shape[1], src_ref.shape[1]
    core, base = meta[0], meta[1]
    lane = lax.broadcasted_iota(jnp.int32, (rows, span), 1) + base
    for half, ref in ((0, own_ref), (1, oth_ref)):
        seq = core if half == 0 else 1 - core
        hot = jnp.where(pos_ref[half] == lane, 1.0, 0.0).astype(bf16)
        src = src_ref[seq]
        ref[...] = mm(hot, src).astype(bf16)


def place_body(meta, pos_ref, base_ref, own_ref, oth_ref, out_ref):
    rows, span = pos_ref.shape[2], base_ref.shape[1]
    core, base = meta[0], meta[1]
    row = lax.broadcasted_iota(jnp.int32, (span, rows), 0) + base
    for half, ref in ((0, own_ref), (1, oth_ref)):
        seq = core if half == 0 else 1 - core
        hot = jnp.where(pos_ref[half] == row, 1.0, 0.0).astype(bf16)
        added = mm(hot, ref[...])
        out_ref[seq] = (base_ref[seq].astype(f32) + added).astype(bf16)


def attn_fwd_body(
    idx, xo_ref, xt_ref, segc_ref, segr_ref, *refs
):
    packs = refs[:BLOCKS]
    a_ref, qkv_ref, p_ref, o_ref, bo_ref, bt_ref, wq_ref, wo_ref, gr_ref, r_ref, gcol = refs[BLOCKS:]
    rows, width = xo_ref.shape
    part = width // 4
    qcols = 3 * part
    blk = width // BLOCKS
    ob = part // BLOCKS
    for b, pk in enumerate(packs):
        s = idx[b]
        off = pl.multiple_of(s * blk, blk)
        wq_ref[pl.ds(off, blk), :] = pk[:, :qcols]
        gcol[pl.ds(off, blk), :] = pk[:, qcols : qcols + 128]
        off2 = pl.multiple_of(s * ob, ob)
        for j in range(4):
            wo_ref[pl.ds(off2, ob), j * part : (j + 1) * part] = pk[
                j * ob : (j + 1) * ob, qcols + 128 :
            ]
    eye = (
        lax.broadcasted_iota(jnp.int32, (8, 128), 0) == lax.broadcasted_iota(jnp.int32, (8, 128), 1)
    ).astype(f32).astype(bf16)
    gr = mm(eye, gcol[...], NT)
    gr_ref[...] = gr
    gain = gr[0:1]
    for half, x_ref in ((0, xo_ref), (1, xt_ref)):
        span = pl.ds(half * rows, rows)
        xb = x_ref[...]
        x = xb.astype(f32)
        scale = lax.rsqrt(jnp.mean(x * x, axis=-1, keepdims=True) + epsilon)
        a_ref[span, :] = (x * scale * gain).astype(bf16)
        r_ref[span, :] = mm(xb, gcol[...])

    def project(i, carry):
        cols = pl.ds(pl.multiple_of(i * part, part), part)
        qkv_ref[:, cols] = mm(a_ref[...], wq_ref[:, cols]).astype(bf16)
        return carry

    lax.fori_loop(0, 3, project, 0)
    ri = lax.broadcasted_iota(jnp.int32, (rows, rows), 0)
    ci = lax.broadcasted_iota(jnp.int32, (rows, rows), 1)
    causal = ci <= ri
    heads = part // HEAD_DIM
    score_scale = HEAD_DIM ** (-0.5)
    for half in range(2):
        allowed = causal & (segc_ref[half] == segr_ref[half])
        span = pl.ds(half * rows, rows)
        for h in range(heads):
            q = qkv_ref[span, h * HEAD_DIM : (h + 1) * HEAD_DIM]
            k = qkv_ref[span, part + h * HEAD_DIM : part + (h + 1) * HEAD_DIM]
            v = qkv_ref[span, 2 * part + h * HEAD_DIM : 2 * part + (h + 1) * HEAD_DIM]
            logits = jnp.where(allowed, mm(q, k, NT) * score_scale, masked)
            e = jnp.exp(logits - jnp.max(logits, axis=-1, keepdims=True))
            p = e * (1.0 / jnp.sum(e, axis=-1, keepdims=True))
            p_ref[half * heads + h] = p
            o_ref[span, h * HEAD_DIM : (h + 1) * HEAD_DIM] = mm(p.astype(bf16), v).astype(bf16)

    def project_out(i, carry):
        cols = pl.ds(pl.multiple_of(i * part, part), part)
        res = mm(o_ref[...], wo_ref[:, cols]).astype(bf16)
        bo_ref[:, cols] = res[:rows]
        bt_ref[:, cols] = res[rows:]
        return carry

    lax.fori_loop(0, 4, project_out, 0)


def norm_body(t_ref, u_ref, x_ref, gr_ref, m_ref):
    h = x_ref[...].astype(f32) + (t_ref[...].astype(f32) + u_ref[...].astype(f32))
    scale = lax.rsqrt(jnp.mean(h * h, axis=-1, keepdims=True) + epsilon)
    m_ref[...] = (h * scale * gr_ref[1:2]).astype(bf16)


def turn_body(a_ref, o_ref, at_ref, ot_ref):
    tile = 256

    def step(i, carry):
        cols = pl.ds(pl.multiple_of(i * tile, tile), tile)
        at_ref[cols, :] = a_ref[:, cols].T
        return carry

    lax.fori_loop(0, a_ref.shape[1] // tile, step, 0)
    ot_ref[...] = o_ref[...].T


def mlp_body(idx, mo_ref, mt_ref, co_ref, ct_ref, r_ref, *refs):
    packs, rest = refs[:BLOCKS], refs[BLOCKS:]
    g_ref, du_ref, db_ref, wu_ref, wd_ref, dmo_ref, dmt_ref = rest
    rows, width = mo_ref.shape
    units = wu_ref.shape[1]
    blk, sub = width // BLOCKS, units // BLOCKS
    for b in range(BLOCKS):
        wu_ref[pl.ds(pl.multiple_of(idx[b] * blk, blk), blk), :] = packs[b][:, :units]
        wd_ref[pl.ds(pl.multiple_of(idx[b] * sub, sub), sub), :] = packs[b][:, units:]
    r = r_ref[:, 2:3]
    db_ref[:rows, :] = (r[:rows] * co_ref[...].astype(f32)).astype(bf16)
    db_ref[rows:, :] = (r[rows:] * ct_ref[...].astype(f32)).astype(bf16)
    tile = 256

    def step(i, carry):
        cols = pl.ds(pl.multiple_of(i * tile, tile), tile)
        for half, m_ref in ((0, mo_ref), (1, mt_ref)):
            span = pl.ds(half * rows, rows)
            u = mm(m_ref[...], wu_ref[:, cols])
            u2 = u * u
            th = jnp.tanh(gelu_scale * (u + gelu_cubic * (u2 * u)))
            half_up = 0.5 * (1.0 + th)
            g_ref[span, cols] = (u * half_up).astype(bf16)
            slope = half_up + (0.5 * u) * (1.0 - th * th) * (
                gelu_scale * (1.0 + 3.0 * gelu_cubic * u2)
            )
            dg = mm(db_ref[span, :], wd_ref[cols, :], NT)
            du_ref[span, cols] = (dg * slope).astype(bf16)
        return carry

    lax.fori_loop(0, units // tile, step, 0)

    def step2(i, carry):
        cols = pl.ds(pl.multiple_of(i * tile, tile), tile)
        dm = mm(du_ref[...], wu_ref[cols, :], NT).astype(bf16)
        dmo_ref[:, cols] = dm[:rows]
        dmt_ref[:, cols] = dm[rows:]
        return carry

    lax.fori_loop(0, width // tile, step2, 0)


EARLY, LATE = (2, 3, 4, 5), (0, 1, 6, 7)


def grad_block(idx, b, ref, fm_ref, fg_ref, du_ref, db_ref, wu_ref, gcol, col_ref):
    width, units = fm_ref.shape[0], fg_ref.shape[0]
    blk, sub = width // BLOCKS, units // BLOCKS
    off = pl.ds(pl.multiple_of(idx[b] * blk, blk), blk)
    grad = mm(fm_ref[off, :], du_ref[...])
    ref[:, :units] = grad.astype(bf16)
    gain = jnp.sum(grad * wu_ref[off, :].astype(f32), axis=-1, keepdims=True)
    gain = gain / gcol[off, 1:2].astype(f32)
    col_ref[off, :] = jnp.broadcast_to(gain, (blk, 128))
    off = pl.ds(pl.multiple_of(idx[b] * sub, sub), sub)
    ref[:, units:] = mm(fg_ref[off, :], db_ref[...]).astype(bf16)


def early_grad_body(
    idx, g_ref, du_ref, db_ref, mo_ref, mt_ref, wu_ref, gcol, col_ref, fm_ref, fg_ref, *grads
):
    rows, width = mo_ref.shape
    tile = 256

    def turn_rows(i, carry):
        cols = pl.ds(pl.multiple_of(i * tile, tile), tile)
        fm_ref[cols, :rows] = mo_ref[:, cols].T
        fm_ref[cols, rows:] = mt_ref[:, cols].T
        fg_ref[cols, :] = g_ref[:, cols].T
        return carry

    lax.fori_loop(0, width // tile, turn_rows, 0)
    for b, ref in zip(EARLY, grads):
        grad_block(idx, b, ref, fm_ref, fg_ref, du_ref, db_ref, wu_ref, gcol, col_ref)


def late_grad_body(
    idx, g_ref, du_ref, db_ref, wu_ref, wd_ref, gcol, col_in, fm_ref, fg_ref, ao_ref, at_ref,
    co_ref, ct_ref, xo_ref, xt_ref, bo_ref, bt_ref, col_ref, *grads
):
    rows, width = bo_ref.shape
    tile = 256
    col_ref[...] = col_in[...]
    for b, ref in zip(LATE, grads):
        grad_block(idx, b, ref, fm_ref, fg_ref, du_ref, db_ref, wu_ref, gcol, col_ref)

    def step(i, carry):
        cols = pl.ds(pl.multiple_of(i * tile, tile), tile)
        res = mm(g_ref[...], wd_ref[:, cols])
        bo_ref[:, cols] = res[:rows].astype(bf16)
        bt_ref[:, cols] = res[rows:].astype(bf16)
        own, other = carry
        own += jnp.sum(
            (res[:rows] + ao_ref[:, cols].astype(f32)) * co_ref[:, cols].astype(f32),
            axis=-1, keepdims=True,
        )
        other += jnp.sum(
            (res[rows:] + at_ref[:, cols].astype(f32)) * ct_ref[:, cols].astype(f32),
            axis=-1, keepdims=True,
        )
        return own, other

    zero = jnp.zeros((rows, 1), f32)
    dots = lax.fori_loop(0, width // tile, step, (zero, zero))
    lane = lax.broadcasted_iota(jnp.int32, (rows, 128), 1)
    route = jnp.zeros((width, 128), f32)
    for d, x_ref in zip(dots, (xo_ref, xt_ref)):
        high = d.astype(bf16).astype(f32)
        two = jnp.where(lane == 0, high, jnp.where(lane == 1, d - high, 0.0)).astype(bf16)
        route += mm(x_ref[...], two, TN)
    total = jnp.sum(route[:, :2], axis=-1, keepdims=True)
    wide = lax.broadcasted_iota(jnp.int32, (width, 128), 1)
    col_ref[...] = jnp.where(wide == 1, col_ref[...], jnp.where(wide == 2, total, 0.0))


def hidden_grad_body(dt_ref, du_ref, bt_ref, bu_ref, x_ref, c_ref, r_ref, gr_ref, da_ref, dh_ref):
    dm = dt_ref[...].astype(f32) + du_ref[...].astype(f32)
    h = x_ref[...].astype(f32) + (bt_ref[...].astype(f32) + bu_ref[...].astype(f32))
    rows = h.shape[0]
    n = lax.rsqrt(jnp.mean(h * h, axis=-1, keepdims=True) + epsilon)
    t = dm * gr_ref[1:2]
    dh = n * t - h * (n * n * n) * jnp.mean(t * h, axis=-1, keepdims=True)
    dh_ref[...] = dh
    de = r_ref[:rows, 2:3] * c_ref[...].astype(f32)
    da_ref[...] = (de + dh).astype(bf16)


def result_body(at_ref, au_ref, mt_ref, mu_ref, c_ref, r_ref, e_ref, dr_ref):
    branch = (at_ref[...].astype(f32) + au_ref[...].astype(f32)) + (
        mt_ref[...].astype(f32) + mu_ref[...].astype(f32)
    )
    rows = branch.shape[0]
    e_ref[...] = (r_ref[:rows, 2:3] * branch).astype(bf16)
    dr = jnp.sum(c_ref[...].astype(f32) * branch, axis=-1, keepdims=True)
    dr_ref[...] = jnp.broadcast_to(dr, dr_ref.shape)


def attn_bwd_body(
    idx, at_ref, ot_ref, qkv_ref, p_ref, dao_ref, dat_ref, wq_ref, wo_ref, gcol, col_ref, *refs
):
    dqkv, near, far, (da,) = refs[0], refs[1:5], refs[5:7], refs[7:]
    rows, width = dao_ref.shape
    part = width // 4
    qcols = 3 * part
    heads = part // HEAD_DIM
    score_scale = HEAD_DIM ** (-0.5)
    da[:rows, :] = dao_ref[...]
    da[rows:, :] = dat_ref[...]
    for half in range(2):
        span = pl.ds(half * rows, rows)
        dmix = mm(da[span, :], wo_ref[...], NT).astype(bf16)
        for h in range(heads):
            lo, hi = h * HEAD_DIM, (h + 1) * HEAD_DIM
            q = qkv_ref[span, lo:hi]
            k = qkv_ref[span, part + lo : part + hi]
            v = qkv_ref[span, 2 * part + lo : 2 * part + hi]
            do = dmix[:, lo:hi]
            p = p_ref[half * heads + h]
            dp = mm(do, v, NT)
            ds = (p * (dp - jnp.sum(p * dp, axis=-1, keepdims=True))).astype(bf16)
            dqkv[span, lo:hi] = (mm(ds, k) * score_scale).astype(bf16)
            dqkv[span, part + lo : part + hi] = (mm(ds, q, TN) * score_scale).astype(bf16)
            dqkv[span, 2 * part + lo : 2 * part + hi] = mm(p.astype(bf16), do, TN).astype(bf16)
    blk = width // BLOCKS
    ob = part // BLOCKS
    lane = lax.broadcasted_iota(jnp.int32, (blk, 128), 1)
    for b in range(BLOCKS):
        s = idx[b]
        k = b // 2
        ref, row = (near[k], 0) if b % 2 == 0 else (far[(k + 3) % 4 // 2], (k + 3) % 2 * blk)
        rows_of = slice(row, row + blk)
        off = pl.ds(pl.multiple_of(s * blk, blk), blk)
        grad = mm(at_ref[off, :], dqkv[...])
        ref[rows_of, :qcols] = grad.astype(bf16)
        gain = jnp.sum(grad * wq_ref[off, :].astype(f32), axis=-1, keepdims=True)
        gain = gain / gcol[off, 0:1].astype(f32)
        ref[rows_of, qcols : qcols + 128] = jnp.where(lane == 0, gain, col_ref[off, :]).astype(bf16)
        og = mm(ot_ref[pl.ds(pl.multiple_of(s * ob, ob), ob), :], da[...]).astype(bf16)
        for j in range(4):
            ref[row + j * ob : row + (j + 1) * ob, qcols + 128 :] = og[:, j * part : (j + 1) * part]


def normed_grad_body(dqkv_ref, wq_ref, do_ref, dt_ref):
    rows, width = do_ref.shape
    tile = 256

    def step(i, carry):
        cols = pl.ds(pl.multiple_of(i * tile, tile), tile)
        d = mm(dqkv_ref[...], wq_ref[cols, :], NT).astype(bf16)
        do_ref[:, cols] = d[:rows]
        dt_ref[:, cols] = d[rows:]
        return carry

    lax.fori_loop(0, width // tile, step, 0)


def input_grad_body(t_ref, u_ref, x_ref, dh_ref, dr_ref, gr_ref, dx_ref):
    d = t_ref[...].astype(f32) + u_ref[...].astype(f32)
    x = x_ref[...].astype(f32)
    m = lax.rsqrt(jnp.mean(x * x, axis=-1, keepdims=True) + epsilon)
    s = d * gr_ref[0:1]
    dxn = m * s - x * (m * m * m) * jnp.mean(s * x, axis=-1, keepdims=True)
    dx_ref[...] = (dxn + dh_ref[...] + dr_ref[:, 0:1] * gr_ref[2:3]).astype(bf16)


HEAD_OF = (0, 2, 1, 3)


def pack_body(meta, qkv_ref, up_ref, gains_ref, *refs):
    outs, (tmp,) = refs[:4], refs[4:]
    width, units = qkv_ref.shape[1] // 3, up_ref.shape[1]
    part = width // 4
    sub = units // (4 * BLOCKS)
    for j in range(4):
        p = HEAD_OF[j]
        for t in range(3):
            for z in range(4):
                src = t * width + (4 * z + p) * HEAD_DIM
                dst = t * part + z * HEAD_DIM
                tmp[j, :, dst : dst + HEAD_DIM] = qkv_ref[:, src : src + HEAD_DIM]
        tmp[j, :, 3 * part : 3 * part + 128] = gains_ref[...]
        for s in range(BLOCKS):
            dst = 3 * part + 128 + s * sub
            src = (4 * s + j) * sub
            tmp[j, :, dst : dst + sub] = up_ref[:, src : src + sub]
    for k, ref in enumerate(outs):
        ref[...] = tmp[meta[3] ^ k]


def join_body(meta, c0, c1, c2, c3, own_ref, moved_ref, down_ref, attn_ref, mlp_ref):
    mine, width = own_ref.shape
    part = width // 4
    head = 3 * part + 128
    for k, ref in enumerate((c0, c1, c2, c3)):
        off = pl.ds(pl.multiple_of((meta[3] ^ k) * mine, mine), mine)
        attn_ref[off, :head] = ref[:, :head]
        mlp_ref[off, : mlp_ref.shape[1] - width] = ref[:, head:]
    mlp_ref[:, mlp_ref.shape[1] - width :] = down_ref[...]
    take = jnp.full(own_ref.shape, meta[4]) == 1
    rows = jnp.where(take, moved_ref[...].astype(f32), own_ref[...].astype(f32)).astype(bf16)
    for j in range(4):
        attn_ref[j * mine : (j + 1) * mine, head:] = rows[:, j * part : (j + 1) * part]


def split_body(
    meta, m0, m1, m2, a0, a1, a2, c0, c1, c2, c3, down_ref, out_ref, tm, ta
):
    mine, width = out_ref.shape
    units = m0.shape[1] - width
    part = width // 4
    head = 3 * part + 128
    for n in range(4):
        span = pl.ds(n * mine, mine)
        total = (m0[span, :].astype(f32) + m1[span, :].astype(f32)) + m2[span, :].astype(f32)
        down_ref[span, :] = total[:, units:]
        tm[span, :] = total[:, :units]
        late = pl.ds((4 + n) * mine, mine)
        total = (a0[span, :].astype(f32) + a1[late, :].astype(f32)) + a2[span, :].astype(f32)
        ta[span, :] = total[:, :head]
        out_ref[:, n * part : (n + 1) * part] = total[:, head:]
    for k, ref in enumerate((c0, c1, c2, c3)):
        off = pl.ds(pl.multiple_of((meta[3] ^ k) * mine, mine), mine)
        ref[:, :head] = ta[off, :].astype(ref.dtype)
        ref[:, head:] = tm[off, :].astype(ref.dtype)


def final_body(meta, c0, c1, c2, c3, qkv_ref, up_ref, small_ref, tmp):
    mine = qkv_ref.shape[0]
    width = qkv_ref.shape[1] // 3
    part = width // 4
    head = 3 * part + 128
    sub = up_ref.shape[1] // (4 * BLOCKS)
    for k, ref in enumerate((c0, c1, c2, c3)):
        tmp[meta[3] ^ k] = ref[...].astype(f32)
    for j in range(4):
        for t in range(3):
            for z in range(4):
                dst = t * width + (4 * z + HEAD_OF[j]) * HEAD_DIM
                src = t * part + z * HEAD_DIM
                qkv_ref[:, dst : dst + HEAD_DIM] = tmp[j, :, src : src + HEAD_DIM]
        for s in range(BLOCKS):
            dst = (4 * s + j) * sub
            up_ref[:, dst : dst + sub] = tmp[j, :, head + s * sub : head + (s + 1) * sub]
    last = slice(3 * part, head)
    small = (tmp[0, :, last] + tmp[1, :, last]) + (tmp[2, :, last] + tmp[3, :, last])
    wide = jnp.concatenate([small, jnp.zeros((128 - mine, 128), f32)], axis=0)
    small_ref[...] = wide.T[:8]


def flip_bit(v, axis, size, mask):
    return lax.ppermute(v, axis, [(i, i ^ mask) for i in range(size)])


def swap_core(v):
    return flip_bit(v, "grp", 4, 1)


def swap_pair(v):
    return flip_bit(v, "grp", 4, 2)


def swap_side(v, seqs):
    return flip_bit(v, "seq", seqs, 1)


def shift_one(v, seqs):
    return lax.ppermute(v, "seq", [(i, (i + 2) % seqs) for i in range(seqs)])


def reorder(parts, member):
    low = (member & 1) == 1
    high = (member & 2) == 2
    res = []
    for j in range(4):
        straight = jnp.where(low, parts[j ^ 1], parts[j])
        crossed = jnp.where(low, parts[j ^ 3], parts[j ^ 2])
        res.append(jnp.where(high, crossed, straight))
    return res


def exchange(chunks, member):
    rel = reorder(chunks, member)
    got = [rel[0]] + [flip_bit(rel[k], "grp", 4, k) for k in range(1, 4)]
    return reorder(got, member)


def native_gather(pack):
    full = lax.all_gather(pack, "seq", axis=0, tiled=True)
    return list(full.reshape((BLOCKS, -1) + full.shape[1:]))


def native_scatter(blocks):
    full = jnp.concatenate(blocks, axis=0)
    return lax.psum_scatter(full.astype(f32), "seq", scatter_dimension=0, tiled=True)


def add(*parts):
    total = parts[0].astype(f32)
    for p in parts[1:]:
        total = total + p.astype(f32)
    return total.astype(bf16)


class Flow:
    def __getitem__(self, name):
        return self.__dict__[name]

    def __setitem__(self, name, value):
        self.__dict__[name] = value

    def order(self, value, name):
        token = lax.create_token()
        token, self[name] = lax.optimization_barrier((token, self[name]))
        return lax.optimization_barrier((token, value))[1]

    def sync(self, *names):
        held = [n for n in names if n in self.__dict__]
        done = lax.optimization_barrier(tuple(self[n] for n in held))
        for n, value in zip(held, done):
            self[n] = value


def on_device(
    tokens,
    segments,
    routed,
    qkv_weight,
    out_weight,
    up_weight,
    down_weight,
    attn_gain,
    mlp_gain,
    router_weight,
    cotangent,
):
    groups, seqs = lax.axis_size("grp"), lax.axis_size("seq")
    member, place = lax.axis_index("grp"), lax.axis_index("seq")
    seq_dev, span, width = tokens.shape
    rows = routed.shape[1]
    units = down_weight.shape[0] * groups * seqs
    if groups != 4 or seq_dev != 2:
        raise ValueError("mesh")
    native = seqs != BLOCKS
    part, ff = width // 4, units // 4
    core, pair = member & 1, member >> 1
    mine = qkv_weight.shape[0]
    head = 3 * part + 128
    both = 2 * rows
    odd = (place ^ member) & 1
    meta = jnp.stack([core, member * span, pair, member, odd]).astype(jnp.int32)
    half = out((rows, width), bf16)
    v = Flow()

    queue = []

    chain = []

    def hop(name, t, lag):
        if len(chain) >= lag:
            t = v.order(t, chain[-lag])
        chain.append(name)
        v[name] = shift_one(t, seqs)

    def side(name, t, lag):
        if len(queue) >= lag:
            t = v.order(t, queue[-lag])
        queue.append(name)
        v[name] = swap_side(t, seqs)


    flip = core == 1
    pos = jnp.where(flip, routed[::-1], routed)
    starts = jnp.stack(
        [jnp.sum((segments < n).astype(jnp.int32), axis=1) for n in range(1, SEG_COUNT)], axis=0
    )
    seg = jnp.sum((routed[None] >= starts[:, :, None]).astype(jnp.int32), axis=0)
    seg = jnp.where(flip, seg[::-1], seg)
    pos_col, pos_row = pos[:, :, None], pos[:, None, :]
    seg_col, seg_row = seg[:, :, None], seg[:, None, :]

    def pick(source, name):
        return call(
            pick_body, (meta, pos_col, source), (half, half), smem=1,
            flops=4 * rows * span * width, name=name, keep=False, limit=24,
        )

    gains = jnp.stack([attn_gain, mlp_gain, router_weight], axis=1)
    gains = jnp.pad(gains, ((0, 0), (0, 125)))
    if native:
        qkv_view = qkv_weight.reshape(mine, 3, 4, 4, HEAD_DIM)
        chunks = [
            jnp.concatenate([qkv_view[:, :, :, p].reshape(mine, 3 * part), gains], axis=1)
            for p in HEAD_OF
        ]
        qkv_blocks = native_gather(jnp.concatenate(exchange(chunks, member), axis=0))
        out_full = lax.all_gather(out_weight, ("seq", "grp"), axis=0, tiled=True)
        out_view = out_full.reshape(4, 4, HEAD_DIM, width)
        head_set = 2 * core + pair
        out_rows = lax.dynamic_index_in_dim(out_view, head_set, 1, keepdims=False)
        out_rows = out_rows.reshape(BLOCKS, part // BLOCKS, width)
        attn_packs = [
            jnp.concatenate(
                [q, jnp.concatenate([o[:, j * part : (j + 1) * part] for j in range(4)], axis=0)],
                axis=1,
            )
            for q, o in zip(qkv_blocks, out_rows)
        ]
        up_view = up_weight.reshape(mine, seqs, 4, ff // seqs)
        chunks = [up_view[:, :, j].reshape(mine, ff) for j in range(4)]
        up_rows = jnp.concatenate(exchange(chunks, member), axis=0)
        mlp_packs = native_gather(jnp.concatenate([up_rows, down_weight], axis=1))
        order = jnp.arange(BLOCKS, dtype=jnp.int32)
        x_mine, x_send = pick(tokens, "pick_tokens")
        v.tx = add(x_mine, swap_core(x_send))
        v.yx = swap_pair(v.tx)
        v.x = v.tx + v.yx
        v.xo = swap_core(v.x)
        c_mine, c_send = pick(cotangent, "pick_cotangent")
        v.tc = add(c_mine, swap_core(c_send))
    else:
        order = jnp.stack(
            [((place ^ r) - 2 * k) % seqs for k in range(BLOCKS // 2) for r in range(2)]
        ).astype(jnp.int32)
        swaps = [
            (s * 4 + g, (s ^ 1) * 4 + (g ^ 1)) for s in range(seqs) for g in range(4) if (s ^ g) & 1
        ]
        chunk = out((mine, head + ff), bf16)
        chunks = call(
            pack_body, (meta, qkv_weight, up_weight, gains), (chunk,) * 4,
            scratch=[pltpu.VMEM((4, mine, head + ff), bf16)], smem=1, name="pack", cold=(1, 2, 3),
        )
        v.k0, v.k1, v.k2, v.k3 = chunks
        v.tokens = tokens
        v.sync("k1", "k2", "k3", "tokens")
        got = [v.k0] + [flip_bit(v["k%d" % k], "grp", 4, k) for k in range(1, 4)]
        x_mine, x_send = pick(v.tokens, "pick_tokens")
        moved = lax.ppermute(out_weight, ("seq", "grp"), swaps)
        v.a0, v.m0 = call(
            join_body, (meta, *got, out_weight, moved, down_weight),
            (out((mine * 4, width + 128), bf16), out((mine * 4, ff + width), bf16)), smem=1,
            name="join", cold=(2, 3, 4, 5, 6, 7),
        )
        v.tx = add(x_mine, swap_core(x_send))
        v.sync("a0", "m0", "tx")
        for n, k in (('a', 1), ('m', 1), ('a', 2), ('a', 3), ('m', 2), ('m', 3)):
            hop("%s%d" % (n, k), v["%s%d" % (n, k - 1)], 3)
        v.yx = swap_pair(v.tx)
        v.x = v.tx + v.yx
        v.xo = swap_core(v.x)
        for n, k in (('m', 0), ('a', 0), ('a', 1), ('a', 2), ('a', 3), ('m', 1), ('m', 2), ('m', 3)):
            side("x%s%d" % (n, k), v["%s%d" % (n, k)], 2)
        c_mine, c_send = pick(cotangent, "pick_cotangent")
        v.tc = add(c_mine, swap_core(c_send))
        v.yc = swap_pair(v.tc)
        v.sync("x", "xo", "m1")
        attn_names = [n + str(k) for k in range(4) for n in ("a", "xa")]
        attn_packs = [v[n] for n in attn_names]

    a, qkv, probs, mix, ba_o, ba_t, w_qkv, w_out, gain_rows, r, gain_cols = call(
        attn_fwd_body,
        (order, v.x, v.xo, seg_col, seg_row, *attn_packs),
        (
            out((both, width), bf16),
            out((both, 3 * part), bf16),
            out((2 * part // HEAD_DIM, rows, rows), f32),
            out((both, part), bf16),
            half,
            half,
            out((width, 3 * part), bf16),
            out((part, width), bf16),
            out((8, width), f32),
            out((both, 128), f32),
            out((width, 128), bf16),
        ),
        smem=1,
        flops=2 * both * width * width,
        name="attn_fwd",
        cold=range(1, 13),
    )
    v.a, v.mix = a, mix
    v.tb = add(ba_o, swap_core(ba_t))
    v.sync("tb", "a", "mix", "xm1")
    v.yb = swap_pair(v.tb)
    if native:
        v.yc = swap_pair(v.tc)
    a_turned, mix_turned = call(
        turn_body, (v.a, v.mix), (out((width, both), bf16), out((part, both), bf16)),
        name="turn",
    )
    v.c = v.tc + v.yc
    v.co = swap_core(v.c)
    v.sync("yb", "tb", "co", "c", "xm2")
    (v.h,) = call(
        norm_body, (v.tb, v.yb, v.x, gain_rows), (half,), name="norm_two", free=(0, 1, 2)
    )
    v.ho = swap_core(v.h)
    if not native:
        mlp_packs = [v[n + str(k)] for k in range(4) for n in ("m", "xm")]
    g, du, db, w_up, w_down, dm_o, dm_t = call(
        mlp_body,
        (order, v.h, v.ho, v.c, v.co, r, *mlp_packs),
        (
            out((both, ff), bf16),
            out((both, ff), bf16),
            out((both, width), bf16),
            out((width, ff), bf16),
            out((ff, width), bf16),
            half,
            half,
        ),
        smem=1,
        flops=6 * both * width * ff,
        name="mlp",
        cold=(2, 3, 4, *range(6, 14)),
    )

    v.du = du
    v.td = add(dm_o, swap_core(dm_t))
    v.sync("td", "du")
    v.yd = swap_pair(v.td)
    packet = out((width // BLOCKS, ff + width), bf16)
    col, turned_m, turned_g, *first = call(
        early_grad_body,
        (order, g, v.du, db, v.h, v.ho, w_up, gain_cols),
        (
            out((width, 128), f32), out((width, both), bf16), out((ff, both), bf16),
            *([packet] * 4),
        ),
        smem=1,
        flops=2 * both * width * ff,
        name="early_grad",
        cold=(5,),
    )
    v.g = g
    v.f0, v.f1 = first[1], first[3]
    v.sync("f0", "f1", "g")
    first[1], first[3] = v.f0, v.f1
    bm_o, bm_t, cols, *last = call(
        late_grad_body,
        (
            order, v.g, v.du, db, w_up, w_down, gain_cols, col, turned_m, turned_g, ba_o, ba_t,
            v.c, v.co, v.x, v.xo,
        ),
        (half, half, out((width, 128), f32), *([packet] * 4)),
        smem=1,
        flops=4 * both * width * ff,
        name="late_grad",
        cold=(12, 13, 14, 15),
    )
    mlp_grads = [*last[:2], *first, *last[2:]]
    v.bm, v.bn = bm_o, bm_t
    v.tm = add(v.bm, swap_core(v.bn))
    parts = {"m": mlp_grads}
    queue.clear()
    chain.clear()
    v.__dict__.update({n + str(k): None for n in ("xm", "xa") for k in range(4)})
    if not native:
        for n, k in (('m', 1), ('m', 2)):
            side("x%s%d" % (n, k), parts[n][2 * k + 1], 2)
    v.sync("yd", "td", "bm")
    da_own, dh = call(
        hidden_grad_body,
        (v.td, v.yd, v.tb, v.yb, v.x, v.c, r, gain_rows),
        (half, out((rows, width), f32)),
        name="hidden_grad",
        free=range(6),
    )
    v.da = da_own
    v.dao = swap_core(da_own)
    def attention_back(v):
        dqkv, *attn_grads = call(
            attn_bwd_body,
            (
                order, a_turned, mix_turned, qkv, probs, v.da, v.dao, w_qkv, w_out,
                gain_cols, cols,
            ),
            (
                out((both, 3 * part), bf16),
                *([out((width // BLOCKS, width + 128), bf16)] * 4),
                *([out((2 * width // BLOCKS, width + 128), bf16)] * 2),
            ),
            scratch=[pltpu.VMEM((both, width), bf16)],
            smem=1,
            flops=3 * both * width * width,
            name="attn_bwd",
            free=(6,),
        )
        v.dqkv = dqkv
        return attn_grads

    def normed_back(dqkv):
        return call(
            normed_grad_body, (dqkv, w_qkv), (half, half), flops=2 * both * width * 3 * part,
            name="normed_grad",
        )

    def give():
        return call(
            result_body,
            (v.tb, v.yb, v.tm, v.ym, v.c, r),
            (half, out((rows, 128), f32)),
            name="result",
            free=range(5),
        )

    def take(dr):
        return call(
            input_grad_body, (v.tx2, v.yx2, v.x, dh, dr, gain_rows), (half,),
            name="input_grad", free=range(3),
        )[0]

    def place_rows(base, own, other, name):
        return call(
            place_body, (meta, pos_row, base, own, other), (out(base.shape, bf16),), smem=1,
            flops=4 * rows * span * width, name=name, keep=False, limit=24,
        )[0]

    if native:
        attn_grads = attention_back(v)
        blk = width // BLOCKS
        far = {(k + 3) % 4: attn_grads[4 + (k + 3) % 4 // 2] for k in range(4)}
        attn_grads = [
            attn_grads[k] if r == 0 else far[(k + 3) % 4][(k + 3) % 2 * blk :][:blk]
            for k in range(4)
            for r in range(2)
        ]
        dx_o, dx_t = normed_back(v.dqkv)
        v.ym = swap_pair(v.tm)
        v.tx2 = add(dx_o, swap_core(dx_t))
        v.yx2 = swap_pair(v.tx2)
        v.e, dr = give()
        v.eo = swap_core(v.e)
        v.dx = take(dr)
        v.dxo = swap_core(v.dx)
    else:
        attn_grads = attention_back(v)
        v.dxm, v.dxs = normed_back(v.dqkv)
        parts["a"] = attn_grads
        for k in range(4):
            v["m%d" % k], v["a%d" % k] = mlp_grads[2 * k], attn_grads[k]
        v.ym = swap_pair(v.tm)
        for n, k in (('m', 3), ('a', 4), ('m', 0), ('a', 5)):
            side("x%s%d" % (n, k), parts[n][2 * k + 1 if n == "m" else k], 2)
        blk = width // BLOCKS
        v.tx2 = add(v.dxm, swap_core(v.dxs))

        def step(n, k):
            across = v["xm%d" % k] if n == "m" else v["xa%d" % (4 + k // 3)]
            if n == "a":
                across = across[blk:] if k == 2 else across[:blk]
            terms = [v["%s%d" % (n, k)], across]
            if k > 1:
                terms.append(v["z%s%d" % (n, k - 1)])
            hop("z%s%d" % (n, k), add(*terms), 2)

        for n, k in (('m', 1), ('m', 2), ('a', 1), ('a', 2), ('a', 3), ('m', 3)):
            if (n, k) == ("a", 1):
                v.sync("tx2", "a1")
                v.yx2 = swap_pair(v.tx2)
            if (n, k) == ("a", 2):
                v.sync("ym", "tm", "a2")
                v.e, dr = give()
                v.eo = swap_core(v.e)
            if (n, k) == ("a", 3):
                v.sync("yx2", "tx2", "eo", "e", "a3")
            if (n, k) == ("m", 3):
                v.dx = take(dr)
                v.dxo = swap_core(v.dx)
                v.mixed = place_rows(tokens, v.e, v.eo, "place_mixed")
                v.sync("mixed", "dxo", "dx", "m3")
            step(n, k)
        v.input_grad = place_rows(cotangent, v.dx, v.dxo, "place_input_grad")
        v.sync("input_grad", "m0")
        piece = [out((mine, head + ff), f32)] + [out((mine, head + ff), bf16)] * 3
        *cut, down_grad, og = call(
            split_body,
            (meta, v.m0, v.xm0, v.zm3, v.a0, v.xa5, v.za3),
            (*piece, out((4 * mine, width), f32), out((mine, width), f32)),
            scratch=[pltpu.VMEM((4 * mine, ff), f32), pltpu.VMEM((4 * mine, head), f32)], smem=1,
            name="split", cold=(2, 3, 5, 6),
        )
        cut = [cut[0]] + [flip_bit(cut[k], "grp", 4, k) for k in range(1, 4)]
        out_moved = lax.ppermute(og, ("seq", "grp"), swaps)
        out_grad = jnp.where(odd == 1, out_moved, og)
        qkv_grad, up_grad, small = call(
            final_body, (meta, *cut),
            (out((mine, 3 * width), f32), out((mine, units), f32), out((8, 128), f32)),
            scratch=[pltpu.VMEM((4, mine, head + ff), f32)], smem=1, name="final", keep_out=False,
            cold=(2, 3, 4),
        )
        small = small[:3, :mine]

    if native:
        v.mixed = place_rows(tokens, v.e, v.eo, "place_mixed")
        v.input_grad = place_rows(cotangent, v.dx, v.dxo, "place_input_grad")
    mixed, input_grad = v.mixed, v.input_grad

    if native:
        mlp_sum = native_scatter(mlp_grads)
        up_sum, down_grad = mlp_sum[:, :ff], mlp_sum[:, ff:]
        back = exchange([up_sum[j * mine : (j + 1) * mine] for j in range(4)], member)
        up_grad = jnp.stack([b.reshape(mine, seqs, ff // seqs) for b in back], axis=2)
        up_grad = up_grad.reshape(mine, units)
        step = part // BLOCKS
        out_mine = jnp.concatenate(
            [
                jnp.concatenate([b[j * step : (j + 1) * step, head:] for j in range(4)], axis=1)
                for b in attn_grads
            ],
            axis=0,
        )
        out_mine = out_mine.astype(f32).reshape(4, 1, HEAD_DIM, width)
        slots = (jnp.arange(4) == head_set).astype(f32)[None, :, None, None]
        out_all = (out_mine * slots).reshape(width, width)
        out_grad = lax.psum_scatter(out_all, ("seq", "grp"), scatter_dimension=0, tiled=True)
        attn_sum = native_scatter([b[:, :head] for b in attn_grads])
        back = exchange([attn_sum[j * mine : (j + 1) * mine] for j in range(4)], member)
        by_head = [b[:, : 3 * part].reshape(mine, 3, 4, HEAD_DIM) for b in back]
        qkv_grad = jnp.stack([by_head[HEAD_OF.index(p)] for p in range(4)], axis=3)
        qkv_grad = qkv_grad.reshape(mine, 3 * width)
        small = sum(b[:, 3 * part : 3 * part + 3] for b in back).T
    return (
        mixed,
        input_grad,
        qkv_grad,
        out_grad,
        up_grad,
        down_grad,
        small[0],
        small[1],
        small[2],
    )


def solution(mesh):
    placed = (
        P("seq", "grp", None),
        P("seq", None),
        P("seq", None),
        P(("seq", "grp"), None),
        P(("seq", "grp"), None),
        P(("seq", "grp"), None),
        P(("seq", "grp"), None),
        P(("seq", "grp")),
        P(("seq", "grp")),
        P(("seq", "grp")),
        P("seq", "grp", None),
    )
    return jax.shard_map(
        on_device,
        mesh=mesh,
        in_specs=placed,
        out_specs=(
            P("seq", "grp", None),
            P("seq", "grp", None),
            P(("seq", "grp"), None),
            P(("seq", "grp"), None),
            P(("seq", "grp"), None),
            P(("seq", "grp"), None),
            P(("seq", "grp")),
            P(("seq", "grp")),
            P(("seq", "grp")),
        ),
        check_vma=False,
    )
```

```python
import jax
import jax.numpy as jnp
from jax import lax
from jax.experimental import pallas as pl
from jax.experimental.pallas import tpu as pltpu
from jax.sharding import PartitionSpec as P

HEAD_DIM = 64
SEG_COUNT = 4
BLOCKS = 8
epsilon = 1e-06
masked = -1e30
f32 = jnp.float32
bf16 = jnp.bfloat16
gelu_scale = 0.7978845608028654
gelu_cubic = 0.044715

NN = (((1,), (0,)), ((), ()))
NT = (((1,), (1,)), ((), ()))
TN = (((0,), (0,)), ((), ()))


def mm(a, b, dims=NN):
    return lax.dot_general(a, b, dims, preferred_element_type=f32)


VM = pl.BlockSpec(memory_space=pltpu.VMEM)
SM = pl.BlockSpec(memory_space=pltpu.SMEM)
MIB = 1024 * 1024


def call(
    body, args, outs, scratch=(), smem=0, flops=0, name=None, limit=8, keep=True, keep_out=True,
    cold=(), free=(),
):
    moved = sum(a.size * a.dtype.itemsize for a in args)
    moved += sum(o.size * o.dtype.itemsize for o in outs)
    if keep:
        args = tuple(
            a
            if n < smem or n in free
            else pltpu.with_memory_space_constraint(a, pltpu.HBM if n in cold else pltpu.VMEM)
            for n, a in enumerate(args)
        )
    if keep and keep_out:
        shapes = tuple(pltpu.VMEM(o.shape, o.dtype) for o in outs)
    else:
        shapes = tuple(outs)
    return pl.pallas_call(
        body,
        out_shape=shapes,
        in_specs=[SM] * smem + [VM] * (len(args) - smem),
        out_specs=tuple([VM] * len(outs)),
        scratch_shapes=list(scratch),
        cost_estimate=pl.CostEstimate(flops=flops, bytes_accessed=moved, transcendentals=0),
        compiler_params=pltpu.CompilerParams(vmem_limit_bytes=limit * MIB),
        name=name,
    )(*args)


def out(shape, dtype):
    return jax.ShapeDtypeStruct(shape, dtype)


def pick_body(meta, pos_ref, src_ref, own_ref, oth_ref):
    rows, span = pos_ref.shape[1], src_ref.shape[1]
    core, base = meta[0], meta[1]
    lane = lax.broadcasted_iota(jnp.int32, (rows, span), 1) + base
    for half, ref in ((0, own_ref), (1, oth_ref)):
        seq = core if half == 0 else 1 - core
        hot = jnp.where(pos_ref[half] == lane, 1.0, 0.0).astype(bf16)
        src = src_ref[seq]
        ref[...] = mm(hot, src).astype(bf16)


def place_body(meta, pos_ref, base_ref, own_ref, oth_ref, out_ref):
    rows, span = pos_ref.shape[2], base_ref.shape[1]
    core, base = meta[0], meta[1]
    row = lax.broadcasted_iota(jnp.int32, (span, rows), 0) + base
    for half, ref in ((0, own_ref), (1, oth_ref)):
        seq = core if half == 0 else 1 - core
        hot = jnp.where(pos_ref[half] == row, 1.0, 0.0).astype(bf16)
        added = mm(hot, ref[...])
        out_ref[seq] = (base_ref[seq].astype(f32) + added).astype(bf16)


def attn_fwd_body(
    idx, xo_ref, xt_ref, segc_ref, segr_ref, *refs
):
    packs = refs[:BLOCKS]
    a_ref, qkv_ref, p_ref, o_ref, bo_ref, bt_ref, wq_ref, wo_ref, gr_ref, r_ref, gcol = refs[BLOCKS:]
    rows, width = xo_ref.shape
    part = width // 4
    qcols = 3 * part
    blk = width // BLOCKS
    ob = part // BLOCKS
    for b, pk in enumerate(packs):
        s = idx[b]
        off = pl.multiple_of(s * blk, blk)
        wq_ref[pl.ds(off, blk), :] = pk[:, :qcols]
        gcol[pl.ds(off, blk), :] = pk[:, qcols : qcols + 128]
        off2 = pl.multiple_of(s * ob, ob)
        for j in range(4):
            wo_ref[pl.ds(off2, ob), j * part : (j + 1) * part] = pk[
                j * ob : (j + 1) * ob, qcols + 128 :
            ]
    eye = (
        lax.broadcasted_iota(jnp.int32, (8, 128), 0) == lax.broadcasted_iota(jnp.int32, (8, 128), 1)
    ).astype(f32).astype(bf16)
    gr = mm(eye, gcol[...], NT)
    gr_ref[...] = gr
    gain = gr[0:1]
    for half, x_ref in ((0, xo_ref), (1, xt_ref)):
        span = pl.ds(half * rows, rows)
        xb = x_ref[...]
        x = xb.astype(f32)
        scale = lax.rsqrt(jnp.mean(x * x, axis=-1, keepdims=True) + epsilon)
        a_ref[span, :] = (x * scale * gain).astype(bf16)
        r_ref[span, :] = mm(xb, gcol[...])

    def project(i, carry):
        cols = pl.ds(pl.multiple_of(i * part, part), part)
        qkv_ref[:, cols] = mm(a_ref[...], wq_ref[:, cols]).astype(bf16)
        return carry

    lax.fori_loop(0, 3, project, 0)
    ri = lax.broadcasted_iota(jnp.int32, (rows, rows), 0)
    ci = lax.broadcasted_iota(jnp.int32, (rows, rows), 1)
    causal = ci <= ri
    heads = part // HEAD_DIM
    score_scale = HEAD_DIM ** (-0.5)
    for half in range(2):
        allowed = causal & (segc_ref[half] == segr_ref[half])
        span = pl.ds(half * rows, rows)
        for h in range(heads):
            q = qkv_ref[span, h * HEAD_DIM : (h + 1) * HEAD_DIM]
            k = qkv_ref[span, part + h * HEAD_DIM : part + (h + 1) * HEAD_DIM]
            v = qkv_ref[span, 2 * part + h * HEAD_DIM : 2 * part + (h + 1) * HEAD_DIM]
            logits = jnp.where(allowed, mm(q, k, NT) * score_scale, masked)
            e = jnp.exp(logits - jnp.max(logits, axis=-1, keepdims=True))
            p = e * (1.0 / jnp.sum(e, axis=-1, keepdims=True))
            p_ref[half * heads + h] = p
            o_ref[span, h * HEAD_DIM : (h + 1) * HEAD_DIM] = mm(p.astype(bf16), v).astype(bf16)

    def project_out(i, carry):
        cols = pl.ds(pl.multiple_of(i * part, part), part)
        res = mm(o_ref[...], wo_ref[:, cols]).astype(bf16)
        bo_ref[:, cols] = res[:rows]
        bt_ref[:, cols] = res[rows:]
        return carry

    lax.fori_loop(0, 4, project_out, 0)


def norm_body(t_ref, u_ref, x_ref, gr_ref, m_ref):
    h = x_ref[...].astype(f32) + (t_ref[...].astype(f32) + u_ref[...].astype(f32))
    scale = lax.rsqrt(jnp.mean(h * h, axis=-1, keepdims=True) + epsilon)
    m_ref[...] = (h * scale * gr_ref[1:2]).astype(bf16)


def turn_body(a_ref, o_ref, at_ref, ot_ref):
    tile = 256

    def step(i, carry):
        cols = pl.ds(pl.multiple_of(i * tile, tile), tile)
        at_ref[cols, :] = a_ref[:, cols].T
        return carry

    lax.fori_loop(0, a_ref.shape[1] // tile, step, 0)
    ot_ref[...] = o_ref[...].T


def mlp_body(idx, mo_ref, mt_ref, co_ref, ct_ref, r_ref, *refs):
    packs, rest = refs[:BLOCKS], refs[BLOCKS:]
    g_ref, du_ref, db_ref, wu_ref, wd_ref, dmo_ref, dmt_ref = rest
    rows, width = mo_ref.shape
    units = wu_ref.shape[1]
    blk, sub = width // BLOCKS, units // BLOCKS
    for b in range(BLOCKS):
        wu_ref[pl.ds(pl.multiple_of(idx[b] * blk, blk), blk), :] = packs[b][:, :units]
        wd_ref[pl.ds(pl.multiple_of(idx[b] * sub, sub), sub), :] = packs[b][:, units:]
    r = r_ref[:, 2:3]
    db_ref[:rows, :] = (r[:rows] * co_ref[...].astype(f32)).astype(bf16)
    db_ref[rows:, :] = (r[rows:] * ct_ref[...].astype(f32)).astype(bf16)
    tile = 256

    def step(i, carry):
        cols = pl.ds(pl.multiple_of(i * tile, tile), tile)
        for half, m_ref in ((0, mo_ref), (1, mt_ref)):
            span = pl.ds(half * rows, rows)
            u = mm(m_ref[...], wu_ref[:, cols])
            u2 = u * u
            th = jnp.tanh(gelu_scale * (u + gelu_cubic * (u2 * u)))
            half_up = 0.5 * (1.0 + th)
            g_ref[span, cols] = (u * half_up).astype(bf16)
            slope = half_up + (0.5 * u) * (1.0 - th * th) * (
                gelu_scale * (1.0 + 3.0 * gelu_cubic * u2)
            )
            dg = mm(db_ref[span, :], wd_ref[cols, :], NT)
            du_ref[span, cols] = (dg * slope).astype(bf16)
        return carry

    lax.fori_loop(0, units // tile, step, 0)

    def step2(i, carry):
        cols = pl.ds(pl.multiple_of(i * tile, tile), tile)
        dm = mm(du_ref[...], wu_ref[cols, :], NT).astype(bf16)
        dmo_ref[:, cols] = dm[:rows]
        dmt_ref[:, cols] = dm[rows:]
        return carry

    lax.fori_loop(0, width // tile, step2, 0)


EARLY, LATE = (2, 3, 4, 5), (0, 1, 6, 7)


def grad_block(idx, b, ref, fm_ref, fg_ref, du_ref, db_ref, wu_ref, gcol, col_ref):
    width, units = fm_ref.shape[0], fg_ref.shape[0]
    blk, sub = width // BLOCKS, units // BLOCKS
    off = pl.ds(pl.multiple_of(idx[b] * blk, blk), blk)
    grad = mm(fm_ref[off, :], du_ref[...])
    ref[:, :units] = grad.astype(bf16)
    gain = jnp.sum(grad * wu_ref[off, :].astype(f32), axis=-1, keepdims=True)
    gain = gain / gcol[off, 1:2].astype(f32)
    col_ref[off, :] = jnp.broadcast_to(gain, (blk, 128))
    off = pl.ds(pl.multiple_of(idx[b] * sub, sub), sub)
    ref[:, units:] = mm(fg_ref[off, :], db_ref[...]).astype(bf16)


def early_grad_body(
    idx, g_ref, du_ref, db_ref, mo_ref, mt_ref, wu_ref, gcol, col_ref, fm_ref, fg_ref, *grads
):
    rows, width = mo_ref.shape
    tile = 256

    def turn_rows(i, carry):
        cols = pl.ds(pl.multiple_of(i * tile, tile), tile)
        fm_ref[cols, :rows] = mo_ref[:, cols].T
        fm_ref[cols, rows:] = mt_ref[:, cols].T
        fg_ref[cols, :] = g_ref[:, cols].T
        return carry

    lax.fori_loop(0, width // tile, turn_rows, 0)
    for b, ref in zip(EARLY, grads):
        grad_block(idx, b, ref, fm_ref, fg_ref, du_ref, db_ref, wu_ref, gcol, col_ref)


def late_grad_body(
    idx, g_ref, du_ref, db_ref, wu_ref, wd_ref, gcol, col_in, fm_ref, fg_ref, ao_ref, at_ref,
    co_ref, ct_ref, xo_ref, xt_ref, bo_ref, bt_ref, col_ref, *grads
):
    rows, width = bo_ref.shape
    tile = 256
    col_ref[...] = col_in[...]
    for b, ref in zip(LATE, grads):
        grad_block(idx, b, ref, fm_ref, fg_ref, du_ref, db_ref, wu_ref, gcol, col_ref)

    def step(i, carry):
        cols = pl.ds(pl.multiple_of(i * tile, tile), tile)
        res = mm(g_ref[...], wd_ref[:, cols])
        bo_ref[:, cols] = res[:rows].astype(bf16)
        bt_ref[:, cols] = res[rows:].astype(bf16)
        own, other = carry
        own += jnp.sum(
            (res[:rows] + ao_ref[:, cols].astype(f32)) * co_ref[:, cols].astype(f32),
            axis=-1, keepdims=True,
        )
        other += jnp.sum(
            (res[rows:] + at_ref[:, cols].astype(f32)) * ct_ref[:, cols].astype(f32),
            axis=-1, keepdims=True,
        )
        return own, other

    zero = jnp.zeros((rows, 1), f32)
    dots = lax.fori_loop(0, width // tile, step, (zero, zero))
    lane = lax.broadcasted_iota(jnp.int32, (rows, 128), 1)
    route = jnp.zeros((width, 128), f32)
    for d, x_ref in zip(dots, (xo_ref, xt_ref)):
        high = d.astype(bf16).astype(f32)
        two = jnp.where(lane == 0, high, jnp.where(lane == 1, d - high, 0.0)).astype(bf16)
        route += mm(x_ref[...], two, TN)
    total = jnp.sum(route[:, :2], axis=-1, keepdims=True)
    wide = lax.broadcasted_iota(jnp.int32, (width, 128), 1)
    col_ref[...] = jnp.where(wide == 1, col_ref[...], jnp.where(wide == 2, total, 0.0))


def hidden_grad_body(dt_ref, du_ref, bt_ref, bu_ref, x_ref, c_ref, r_ref, gr_ref, da_ref, dh_ref):
    dm = dt_ref[...].astype(f32) + du_ref[...].astype(f32)
    h = x_ref[...].astype(f32) + (bt_ref[...].astype(f32) + bu_ref[...].astype(f32))
    rows = h.shape[0]
    n = lax.rsqrt(jnp.mean(h * h, axis=-1, keepdims=True) + epsilon)
    t = dm * gr_ref[1:2]
    dh = n * t - h * (n * n * n) * jnp.mean(t * h, axis=-1, keepdims=True)
    dh_ref[...] = dh
    de = r_ref[:rows, 2:3] * c_ref[...].astype(f32)
    da_ref[...] = (de + dh).astype(bf16)


def result_body(at_ref, au_ref, mt_ref, mu_ref, c_ref, r_ref, e_ref, dr_ref):
    branch = (at_ref[...].astype(f32) + au_ref[...].astype(f32)) + (
        mt_ref[...].astype(f32) + mu_ref[...].astype(f32)
    )
    rows = branch.shape[0]
    e_ref[...] = (r_ref[:rows, 2:3] * branch).astype(bf16)
    dr = jnp.sum(c_ref[...].astype(f32) * branch, axis=-1, keepdims=True)
    dr_ref[...] = jnp.broadcast_to(dr, dr_ref.shape)


def attn_bwd_body(
    idx, at_ref, ot_ref, qkv_ref, p_ref, dao_ref, dat_ref, wq_ref, wo_ref, gcol, col_ref, *refs
):
    dqkv, near, far, (da,) = refs[0], refs[1:5], refs[5:7], refs[7:]
    rows, width = dao_ref.shape
    part = width // 4
    qcols = 3 * part
    heads = part // HEAD_DIM
    score_scale = HEAD_DIM ** (-0.5)
    da[:rows, :] = dao_ref[...]
    da[rows:, :] = dat_ref[...]
    for half in range(2):
        span = pl.ds(half * rows, rows)
        dmix = mm(da[span, :], wo_ref[...], NT).astype(bf16)
        for h in range(heads):
            lo, hi = h * HEAD_DIM, (h + 1) * HEAD_DIM
            q = qkv_ref[span, lo:hi]
            k = qkv_ref[span, part + lo : part + hi]
            v = qkv_ref[span, 2 * part + lo : 2 * part + hi]
            do = dmix[:, lo:hi]
            p = p_ref[half * heads + h]
            dp = mm(do, v, NT)
            ds = (p * (dp - jnp.sum(p * dp, axis=-1, keepdims=True))).astype(bf16)
            dqkv[span, lo:hi] = (mm(ds, k) * score_scale).astype(bf16)
            dqkv[span, part + lo : part + hi] = (mm(ds, q, TN) * score_scale).astype(bf16)
            dqkv[span, 2 * part + lo : 2 * part + hi] = mm(p.astype(bf16), do, TN).astype(bf16)
    blk = width // BLOCKS
    ob = part // BLOCKS
    lane = lax.broadcasted_iota(jnp.int32, (blk, 128), 1)
    for b in range(BLOCKS):
        s = idx[b]
        k = b // 2
        ref, row = (near[k], 0) if b % 2 == 0 else (far[(k + 3) % 4 // 2], (k + 3) % 2 * blk)
        rows_of = slice(row, row + blk)
        off = pl.ds(pl.multiple_of(s * blk, blk), blk)
        grad = mm(at_ref[off, :], dqkv[...])
        ref[rows_of, :qcols] = grad.astype(bf16)
        gain = jnp.sum(grad * wq_ref[off, :].astype(f32), axis=-1, keepdims=True)
        gain = gain / gcol[off, 0:1].astype(f32)
        ref[rows_of, qcols : qcols + 128] = jnp.where(lane == 0, gain, col_ref[off, :]).astype(bf16)
        og = mm(ot_ref[pl.ds(pl.multiple_of(s * ob, ob), ob), :], da[...]).astype(bf16)
        for j in range(4):
            ref[row + j * ob : row + (j + 1) * ob, qcols + 128 :] = og[:, j * part : (j + 1) * part]


def normed_grad_body(dqkv_ref, wq_ref, do_ref, dt_ref):
    rows, width = do_ref.shape
    tile = 256

    def step(i, carry):
        cols = pl.ds(pl.multiple_of(i * tile, tile), tile)
        d = mm(dqkv_ref[...], wq_ref[cols, :], NT).astype(bf16)
        do_ref[:, cols] = d[:rows]
        dt_ref[:, cols] = d[rows:]
        return carry

    lax.fori_loop(0, width // tile, step, 0)


def input_grad_body(t_ref, u_ref, x_ref, dh_ref, dr_ref, gr_ref, dx_ref):
    d = t_ref[...].astype(f32) + u_ref[...].astype(f32)
    x = x_ref[...].astype(f32)
    m = lax.rsqrt(jnp.mean(x * x, axis=-1, keepdims=True) + epsilon)
    s = d * gr_ref[0:1]
    dxn = m * s - x * (m * m * m) * jnp.mean(s * x, axis=-1, keepdims=True)
    dx_ref[...] = (dxn + dh_ref[...] + dr_ref[:, 0:1] * gr_ref[2:3]).astype(bf16)


HEAD_OF = (0, 2, 1, 3)


def pack_body(meta, qkv_ref, up_ref, gains_ref, *refs):
    outs, (tmp,) = refs[:4], refs[4:]
    width, units = qkv_ref.shape[1] // 3, up_ref.shape[1]
    part = width // 4
    sub = units // (4 * BLOCKS)
    for j in range(4):
        p = HEAD_OF[j]
        for t in range(3):
            for z in range(4):
                src = t * width + (4 * z + p) * HEAD_DIM
                dst = t * part + z * HEAD_DIM
                tmp[j, :, dst : dst + HEAD_DIM] = qkv_ref[:, src : src + HEAD_DIM]
        tmp[j, :, 3 * part : 3 * part + 128] = gains_ref[...]
        for s in range(BLOCKS):
            dst = 3 * part + 128 + s * sub
            src = (4 * s + j) * sub
            tmp[j, :, dst : dst + sub] = up_ref[:, src : src + sub]
    for k, ref in enumerate(outs):
        ref[...] = tmp[meta[3] ^ k]


def join_body(meta, c0, c1, c2, c3, own_ref, moved_ref, down_ref, attn_ref, mlp_ref):
    mine, width = own_ref.shape
    part = width // 4
    head = 3 * part + 128
    for k, ref in enumerate((c0, c1, c2, c3)):
        off = pl.ds(pl.multiple_of((meta[3] ^ k) * mine, mine), mine)
        attn_ref[off, :head] = ref[:, :head]
        mlp_ref[off, : mlp_ref.shape[1] - width] = ref[:, head:]
    mlp_ref[:, mlp_ref.shape[1] - width :] = down_ref[...]
    take = jnp.full(own_ref.shape, meta[4]) == 1
    rows = jnp.where(take, moved_ref[...].astype(f32), own_ref[...].astype(f32)).astype(bf16)
    for j in range(4):
        attn_ref[j * mine : (j + 1) * mine, head:] = rows[:, j * part : (j + 1) * part]


def split_body(
    meta, m0, m1, m2, a0, a1, a2, c0, c1, c2, c3, down_ref, out_ref, tm, ta
):
    mine, width = out_ref.shape
    units = m0.shape[1] - width
    part = width // 4
    head = 3 * part + 128
    for n in range(4):
        span = pl.ds(n * mine, mine)
        total = (m0[span, :].astype(f32) + m1[span, :].astype(f32)) + m2[span, :].astype(f32)
        down_ref[span, :] = total[:, units:]
        tm[span, :] = total[:, :units]
        late = pl.ds((4 + n) * mine, mine)
        total = (a0[span, :].astype(f32) + a1[late, :].astype(f32)) + a2[span, :].astype(f32)
        ta[span, :] = total[:, :head]
        out_ref[:, n * part : (n + 1) * part] = total[:, head:]
    for k, ref in enumerate((c0, c1, c2, c3)):
        off = pl.ds(pl.multiple_of((meta[3] ^ k) * mine, mine), mine)
        ref[:, :head] = ta[off, :].astype(ref.dtype)
        ref[:, head:] = tm[off, :].astype(ref.dtype)


def final_body(meta, c0, c1, c2, c3, qkv_ref, up_ref, small_ref, tmp):
    mine = qkv_ref.shape[0]
    width = qkv_ref.shape[1] // 3
    part = width // 4
    head = 3 * part + 128
    sub = up_ref.shape[1] // (4 * BLOCKS)
    for k, ref in enumerate((c0, c1, c2, c3)):
        tmp[meta[3] ^ k] = ref[...].astype(f32)
    for j in range(4):
        for t in range(3):
            for z in range(4):
                dst = t * width + (4 * z + HEAD_OF[j]) * HEAD_DIM
                src = t * part + z * HEAD_DIM
                qkv_ref[:, dst : dst + HEAD_DIM] = tmp[j, :, src : src + HEAD_DIM]
        for s in range(BLOCKS):
            dst = (4 * s + j) * sub
            up_ref[:, dst : dst + sub] = tmp[j, :, head + s * sub : head + (s + 1) * sub]
    last = slice(3 * part, head)
    small = (tmp[0, :, last] + tmp[1, :, last]) + (tmp[2, :, last] + tmp[3, :, last])
    wide = jnp.concatenate([small, jnp.zeros((128 - mine, 128), f32)], axis=0)
    small_ref[...] = wide.T[:8]


def flip_bit(v, axis, size, mask):
    return lax.ppermute(v, axis, [(i, i ^ mask) for i in range(size)])


def swap_core(v):
    return flip_bit(v, "grp", 4, 1)


def swap_pair(v):
    return flip_bit(v, "grp", 4, 2)


def swap_side(v, seqs):
    return flip_bit(v, "seq", seqs, 1)


def shift_one(v, seqs):
    return lax.ppermute(v, "seq", [(i, (i + 2) % seqs) for i in range(seqs)])


def reorder(parts, member):
    low = (member & 1) == 1
    high = (member & 2) == 2
    res = []
    for j in range(4):
        straight = jnp.where(low, parts[j ^ 1], parts[j])
        crossed = jnp.where(low, parts[j ^ 3], parts[j ^ 2])
        res.append(jnp.where(high, crossed, straight))
    return res


def exchange(chunks, member):
    rel = reorder(chunks, member)
    got = [rel[0]] + [flip_bit(rel[k], "grp", 4, k) for k in range(1, 4)]
    return reorder(got, member)


def native_gather(pack):
    full = lax.all_gather(pack, "seq", axis=0, tiled=True)
    return list(full.reshape((BLOCKS, -1) + full.shape[1:]))


def native_scatter(blocks):
    full = jnp.concatenate(blocks, axis=0)
    return lax.psum_scatter(full.astype(f32), "seq", scatter_dimension=0, tiled=True)


def add(*parts):
    total = parts[0].astype(f32)
    for p in parts[1:]:
        total = total + p.astype(f32)
    return total.astype(bf16)


class Flow:
    def __getitem__(self, name):
        return self.__dict__[name]

    def __setitem__(self, name, value):
        self.__dict__[name] = value

    def order(self, value, name):
        token = lax.create_token()
        token, self[name] = lax.optimization_barrier((token, self[name]))
        return lax.optimization_barrier((token, value))[1]

    def sync(self, *names):
        held = [n for n in names if n in self.__dict__]
        done = lax.optimization_barrier(tuple(self[n] for n in held))
        for n, value in zip(held, done):
            self[n] = value


def on_device(
    tokens,
    segments,
    routed,
    qkv_weight,
    out_weight,
    up_weight,
    down_weight,
    attn_gain,
    mlp_gain,
    router_weight,
    cotangent,
):
    groups, seqs = lax.axis_size("grp"), lax.axis_size("seq")
    member, place = lax.axis_index("grp"), lax.axis_index("seq")
    seq_dev, span, width = tokens.shape
    rows = routed.shape[1]
    units = down_weight.shape[0] * groups * seqs
    if groups != 4 or seq_dev != 2:
        raise ValueError("mesh")
    native = seqs != BLOCKS
    part, ff = width // 4, units // 4
    core, pair = member & 1, member >> 1
    mine = qkv_weight.shape[0]
    head = 3 * part + 128
    both = 2 * rows
    odd = (place ^ member) & 1
    meta = jnp.stack([core, member * span, pair, member, odd]).astype(jnp.int32)
    half = out((rows, width), bf16)
    v = Flow()

    queue = []

    chain = []

    def hop(name, t, lag):
        if len(chain) >= lag:
            t = v.order(t, chain[-lag])
        chain.append(name)
        v[name] = shift_one(t, seqs)

    def side(name, t, lag):
        if len(queue) >= lag:
            t = v.order(t, queue[-lag])
        queue.append(name)
        v[name] = swap_side(t, seqs)


    flip = core == 1
    pos = jnp.where(flip, routed[::-1], routed)
    starts = jnp.stack(
        [jnp.sum((segments < n).astype(jnp.int32), axis=1) for n in range(1, SEG_COUNT)], axis=0
    )
    seg = jnp.sum((routed[None] >= starts[:, :, None]).astype(jnp.int32), axis=0)
    seg = jnp.where(flip, seg[::-1], seg)
    pos_col, pos_row = pos[:, :, None], pos[:, None, :]
    seg_col, seg_row = seg[:, :, None], seg[:, None, :]

    def pick(source, name):
        return call(
            pick_body, (meta, pos_col, source), (half, half), smem=1,
            flops=4 * rows * span * width, name=name, keep=False, limit=24,
        )

    gains = jnp.stack([attn_gain, mlp_gain, router_weight], axis=1)
    gains = jnp.pad(gains, ((0, 0), (0, 125)))
    if native:
        qkv_view = qkv_weight.reshape(mine, 3, 4, 4, HEAD_DIM)
        chunks = [
            jnp.concatenate([qkv_view[:, :, :, p].reshape(mine, 3 * part), gains], axis=1)
            for p in HEAD_OF
        ]
        qkv_blocks = native_gather(jnp.concatenate(exchange(chunks, member), axis=0))
        out_full = lax.all_gather(out_weight, ("seq", "grp"), axis=0, tiled=True)
        out_view = out_full.reshape(4, 4, HEAD_DIM, width)
        head_set = 2 * core + pair
        out_rows = lax.dynamic_index_in_dim(out_view, head_set, 1, keepdims=False)
        out_rows = out_rows.reshape(BLOCKS, part // BLOCKS, width)
        attn_packs = [
            jnp.concatenate(
                [q, jnp.concatenate([o[:, j * part : (j + 1) * part] for j in range(4)], axis=0)],
                axis=1,
            )
            for q, o in zip(qkv_blocks, out_rows)
        ]
        up_view = up_weight.reshape(mine, seqs, 4, ff // seqs)
        chunks = [up_view[:, :, j].reshape(mine, ff) for j in range(4)]
        up_rows = jnp.concatenate(exchange(chunks, member), axis=0)
        mlp_packs = native_gather(jnp.concatenate([up_rows, down_weight], axis=1))
        order = jnp.arange(BLOCKS, dtype=jnp.int32)
        x_mine, x_send = pick(tokens, "pick_tokens")
        v.tx = add(x_mine, swap_core(x_send))
        v.yx = swap_pair(v.tx)
        v.x = v.tx + v.yx
        v.xo = swap_core(v.x)
        c_mine, c_send = pick(cotangent, "pick_cotangent")
        v.tc = add(c_mine, swap_core(c_send))
    else:
        order = jnp.stack(
            [((place ^ r) - 2 * k) % seqs for k in range(BLOCKS // 2) for r in range(2)]
        ).astype(jnp.int32)
        swaps = [
            (s * 4 + g, (s ^ 1) * 4 + (g ^ 1)) for s in range(seqs) for g in range(4) if (s ^ g) & 1
        ]
        chunk = out((mine, head + ff), bf16)
        chunks = call(
            pack_body, (meta, qkv_weight, up_weight, gains), (chunk,) * 4,
            scratch=[pltpu.VMEM((4, mine, head + ff), bf16)], smem=1, name="pack", cold=(1, 2, 3),
        )
        v.k0, v.k1, v.k2, v.k3 = chunks
        v.tokens = tokens
        v.sync("k1", "k2", "k3", "tokens")
        got = [v.k0] + [flip_bit(v["k%d" % k], "grp", 4, k) for k in range(1, 4)]
        x_mine, x_send = pick(v.tokens, "pick_tokens")
        moved = lax.ppermute(out_weight, ("seq", "grp"), swaps)
        v.a0, v.m0 = call(
            join_body, (meta, *got, out_weight, moved, down_weight),
            (out((mine * 4, width + 128), bf16), out((mine * 4, ff + width), bf16)), smem=1,
            name="join", cold=(2, 3, 4, 5, 6, 7),
        )
        v.tx = add(x_mine, swap_core(x_send))
        v.sync("a0", "m0", "tx")
        for n, k in (('a', 1), ('m', 1), ('a', 2), ('a', 3), ('m', 2), ('m', 3)):
            hop("%s%d" % (n, k), v["%s%d" % (n, k - 1)], 3)
        v.yx = swap_pair(v.tx)
        v.x = v.tx + v.yx
        v.xo = swap_core(v.x)
        for n, k in (('m', 0), ('a', 0), ('a', 1), ('a', 2), ('a', 3), ('m', 1), ('m', 2), ('m', 3)):
            side("x%s%d" % (n, k), v["%s%d" % (n, k)], 2)
        c_mine, c_send = pick(cotangent, "pick_cotangent")
        v.tc = add(c_mine, swap_core(c_send))
        v.yc = swap_pair(v.tc)
        v.sync("x", "xo", "m1")
        attn_names = [n + str(k) for k in range(4) for n in ("a", "xa")]
        attn_packs = [v[n] for n in attn_names]

    a, qkv, probs, mix, ba_o, ba_t, w_qkv, w_out, gain_rows, r, gain_cols = call(
        attn_fwd_body,
        (order, v.x, v.xo, seg_col, seg_row, *attn_packs),
        (
            out((both, width), bf16),
            out((both, 3 * part), bf16),
            out((2 * part // HEAD_DIM, rows, rows), f32),
            out((both, part), bf16),
            half,
            half,
            out((width, 3 * part), bf16),
            out((part, width), bf16),
            out((8, width), f32),
            out((both, 128), f32),
            out((width, 128), bf16),
        ),
        smem=1,
        flops=2 * both * width * width,
        name="attn_fwd",
        cold=range(1, 13),
    )
    v.a, v.mix = a, mix
    v.tb = add(ba_o, swap_core(ba_t))
    v.sync("tb", "a", "mix", "xm1")
    v.yb = swap_pair(v.tb)
    if native:
        v.yc = swap_pair(v.tc)
    a_turned, mix_turned = call(
        turn_body, (v.a, v.mix), (out((width, both), bf16), out((part, both), bf16)),
        name="turn",
    )
    v.c = v.tc + v.yc
    v.co = swap_core(v.c)
    v.sync("yb", "tb", "co", "c", "xm2")
    (v.h,) = call(
        norm_body, (v.tb, v.yb, v.x, gain_rows), (half,), name="norm_two", free=(0, 1, 2)
    )
    v.ho = swap_core(v.h)
    if not native:
        mlp_packs = [v[n + str(k)] for k in range(4) for n in ("m", "xm")]
    g, du, db, w_up, w_down, dm_o, dm_t = call(
        mlp_body,
        (order, v.h, v.ho, v.c, v.co, r, *mlp_packs),
        (
            out((both, ff), bf16),
            out((both, ff), bf16),
            out((both, width), bf16),
            out((width, ff), bf16),
            out((ff, width), bf16),
            half,
            half,
        ),
        smem=1,
        flops=6 * both * width * ff,
        name="mlp",
        cold=(2, 3, 4, *range(6, 13)),
        free=(13,),
    )

    v.du = du
    v.td = add(dm_o, swap_core(dm_t))
    v.sync("td", "du")
    v.yd = swap_pair(v.td)
    packet = out((width // BLOCKS, ff + width), bf16)
    col, turned_m, turned_g, *first = call(
        early_grad_body,
        (order, g, v.du, db, v.h, v.ho, w_up, gain_cols),
        (
            out((width, 128), f32), out((width, both), bf16), out((ff, both), bf16),
            *([packet] * 4),
        ),
        smem=1,
        flops=2 * both * width * ff,
        name="early_grad",
        cold=(5,),
    )
    v.g = g
    v.f0, v.f1 = first[1], first[3]
    v.sync("f0", "f1", "g")
    first[1], first[3] = v.f0, v.f1
    bm_o, bm_t, cols, *last = call(
        late_grad_body,
        (
            order, v.g, v.du, db, w_up, w_down, gain_cols, col, turned_m, turned_g, ba_o, ba_t,
            v.c, v.co, v.x, v.xo,
        ),
        (half, half, out((width, 128), f32), *([packet] * 4)),
        smem=1,
        flops=4 * both * width * ff,
        name="late_grad",
        cold=(12, 13, 14, 15),
    )
    mlp_grads = [*last[:2], *first, *last[2:]]
    v.bm, v.bn = bm_o, bm_t
    v.tm = add(v.bm, swap_core(v.bn))
    parts = {"m": mlp_grads}
    queue.clear()
    chain.clear()
    v.__dict__.update({n + str(k): None for n in ("xm", "xa") for k in range(4)})
    if not native:
        for n, k in (('m', 1), ('m', 2)):
            side("x%s%d" % (n, k), parts[n][2 * k + 1], 4)
    v.sync("yd", "td", "bm")
    da_own, dh = call(
        hidden_grad_body,
        (v.td, v.yd, v.tb, v.yb, v.x, v.c, r, gain_rows),
        (half, out((rows, width), f32)),
        name="hidden_grad",
        free=range(6),
    )
    v.da = da_own
    v.dao = swap_core(da_own)
    def attention_back(v):
        dqkv, *attn_grads = call(
            attn_bwd_body,
            (
                order, a_turned, mix_turned, qkv, probs, v.da, v.dao, w_qkv, w_out,
                gain_cols, cols,
            ),
            (
                out((both, 3 * part), bf16),
                *([out((width // BLOCKS, width + 128), bf16)] * 4),
                *([out((2 * width // BLOCKS, width + 128), bf16)] * 2),
            ),
            scratch=[pltpu.VMEM((both, width), bf16)],
            smem=1,
            flops=3 * both * width * width,
            name="attn_bwd",
            free=(6,),
        )
        v.dqkv = dqkv
        return attn_grads

    def normed_back(dqkv):
        return call(
            normed_grad_body, (dqkv, w_qkv), (half, half), flops=2 * both * width * 3 * part,
            name="normed_grad",
        )

    def give():
        return call(
            result_body,
            (v.tb, v.yb, v.tm, v.ym, v.c, r),
            (half, out((rows, 128), f32)),
            name="result",
            free=range(5),
        )

    def take(dr):
        return call(
            input_grad_body, (v.tx2, v.yx2, v.x, dh, dr, gain_rows), (half,),
            name="input_grad", free=range(3),
        )[0]

    def place_rows(base, own, other, name):
        return call(
            place_body, (meta, pos_row, base, own, other), (out(base.shape, bf16),), smem=1,
            flops=4 * rows * span * width, name=name, keep=False, limit=24,
        )[0]

    if native:
        attn_grads = attention_back(v)
        blk = width // BLOCKS
        far = {(k + 3) % 4: attn_grads[4 + (k + 3) % 4 // 2] for k in range(4)}
        attn_grads = [
            attn_grads[k] if r == 0 else far[(k + 3) % 4][(k + 3) % 2 * blk :][:blk]
            for k in range(4)
            for r in range(2)
        ]
        dx_o, dx_t = normed_back(v.dqkv)
        v.ym = swap_pair(v.tm)
        v.tx2 = add(dx_o, swap_core(dx_t))
        v.yx2 = swap_pair(v.tx2)
        v.e, dr = give()
        v.eo = swap_core(v.e)
        v.dx = take(dr)
        v.dxo = swap_core(v.dx)
    else:
        attn_grads = attention_back(v)
        v.dxm, v.dxs = normed_back(v.dqkv)
        parts["a"] = attn_grads
        for k in range(4):
            v["m%d" % k], v["a%d" % k] = mlp_grads[2 * k], attn_grads[k]
        v.ym = swap_pair(v.tm)
        for n, k in (('a', 4), ('m', 3), ('a', 5), ('m', 0)):
            side("x%s%d" % (n, k), parts[n][2 * k + 1 if n == "m" else k], 4)
        blk = width // BLOCKS
        v.tx2 = add(v.dxm, swap_core(v.dxs))

        def step(n, k):
            across = v["xm%d" % k] if n == "m" else v["xa%d" % (4 + k // 3)]
            if n == "a":
                across = across[blk:] if k == 2 else across[:blk]
            terms = [v["%s%d" % (n, k)], across]
            if k > 1:
                terms.append(v["z%s%d" % (n, k - 1)])
            hop("z%s%d" % (n, k), add(*terms), 2)

        for n, k in (('m', 1), ('m', 2), ('a', 1), ('a', 2), ('a', 3), ('m', 3)):
            if (n, k) == ("a", 1):
                v.sync("tx2", "a1")
                v.yx2 = swap_pair(v.tx2)
            if (n, k) == ("a", 2):
                v.sync("ym", "tm", "a2")
                v.e, dr = give()
                v.eo = swap_core(v.e)
            if (n, k) == ("a", 3):
                v.sync("yx2", "tx2", "eo", "e", "a3")
            if (n, k) == ("m", 3):
                v.dx = take(dr)
                v.dxo = swap_core(v.dx)
                v.mixed = place_rows(tokens, v.e, v.eo, "place_mixed")
                v.sync("mixed", "dxo", "dx", "m3")
            step(n, k)
        v.input_grad = place_rows(cotangent, v.dx, v.dxo, "place_input_grad")
        v.sync("input_grad", "m0")
        piece = [out((mine, head + ff), f32)] + [out((mine, head + ff), bf16)] * 3
        *cut, down_grad, og = call(
            split_body,
            (meta, v.m0, v.xm0, v.zm3, v.a0, v.xa5, v.za3),
            (*piece, out((4 * mine, width), f32), out((mine, width), f32)),
            scratch=[pltpu.VMEM((4 * mine, ff), f32), pltpu.VMEM((4 * mine, head), f32)], smem=1,
            name="split", cold=(2, 3, 5, 6),
        )
        cut = [cut[0]] + [flip_bit(cut[k], "grp", 4, k) for k in range(1, 4)]
        out_moved = lax.ppermute(og, ("seq", "grp"), swaps)
        out_grad = jnp.where(odd == 1, out_moved, og)
        qkv_grad, up_grad, small = call(
            final_body, (meta, *cut),
            (out((mine, 3 * width), f32), out((mine, units), f32), out((8, 128), f32)),
            scratch=[pltpu.VMEM((4, mine, head + ff), f32)], smem=1, name="final", keep_out=False,
            cold=(2, 3, 4),
        )
        small = small[:3, :mine]

    if native:
        v.mixed = place_rows(tokens, v.e, v.eo, "place_mixed")
        v.input_grad = place_rows(cotangent, v.dx, v.dxo, "place_input_grad")
    mixed, input_grad = v.mixed, v.input_grad

    if native:
        mlp_sum = native_scatter(mlp_grads)
        up_sum, down_grad = mlp_sum[:, :ff], mlp_sum[:, ff:]
        back = exchange([up_sum[j * mine : (j + 1) * mine] for j in range(4)], member)
        up_grad = jnp.stack([b.reshape(mine, seqs, ff // seqs) for b in back], axis=2)
        up_grad = up_grad.reshape(mine, units)
        step = part // BLOCKS
        out_mine = jnp.concatenate(
            [
                jnp.concatenate([b[j * step : (j + 1) * step, head:] for j in range(4)], axis=1)
                for b in attn_grads
            ],
            axis=0,
        )
        out_mine = out_mine.astype(f32).reshape(4, 1, HEAD_DIM, width)
        slots = (jnp.arange(4) == head_set).astype(f32)[None, :, None, None]
        out_all = (out_mine * slots).reshape(width, width)
        out_grad = lax.psum_scatter(out_all, ("seq", "grp"), scatter_dimension=0, tiled=True)
        attn_sum = native_scatter([b[:, :head] for b in attn_grads])
        back = exchange([attn_sum[j * mine : (j + 1) * mine] for j in range(4)], member)
        by_head = [b[:, : 3 * part].reshape(mine, 3, 4, HEAD_DIM) for b in back]
        qkv_grad = jnp.stack([by_head[HEAD_OF.index(p)] for p in range(4)], axis=3)
        qkv_grad = qkv_grad.reshape(mine, 3 * width)
        small = sum(b[:, 3 * part : 3 * part + 3] for b in back).T
    return (
        mixed,
        input_grad,
        qkv_grad,
        out_grad,
        up_grad,
        down_grad,
        small[0],
        small[1],
        small[2],
    )


def solution(mesh):
    placed = (
        P("seq", "grp", None),
        P("seq", None),
        P("seq", None),
        P(("seq", "grp"), None),
        P(("seq", "grp"), None),
        P(("seq", "grp"), None),
        P(("seq", "grp"), None),
        P(("seq", "grp")),
        P(("seq", "grp")),
        P(("seq", "grp")),
        P("seq", "grp", None),
    )
    return jax.shard_map(
        on_device,
        mesh=mesh,
        in_specs=placed,
        out_specs=(
            P("seq", "grp", None),
            P("seq", "grp", None),
            P(("seq", "grp"), None),
            P(("seq", "grp"), None),
            P(("seq", "grp"), None),
            P(("seq", "grp"), None),
            P(("seq", "grp")),
            P(("seq", "grp")),
            P(("seq", "grp")),
        ),
        check_vma=False,
    )
```

```python
import jax
import jax.numpy as jnp
from jax import lax
from jax.experimental import pallas as pl
from jax.experimental.pallas import tpu as pltpu
from jax.sharding import PartitionSpec as P

HEAD_DIM = 64
SEG_COUNT = 4
BLOCKS = 8
epsilon = 1e-06
masked = -1e30
f32 = jnp.float32
bf16 = jnp.bfloat16
gelu_scale = 0.7978845608028654
gelu_cubic = 0.044715

NN = (((1,), (0,)), ((), ()))
NT = (((1,), (1,)), ((), ()))
TN = (((0,), (0,)), ((), ()))


def mm(a, b, dims=NN):
    return lax.dot_general(a, b, dims, preferred_element_type=f32)


VM = pl.BlockSpec(memory_space=pltpu.VMEM)
SM = pl.BlockSpec(memory_space=pltpu.SMEM)
MIB = 1024 * 1024


def call(
    body, args, outs, scratch=(), smem=0, flops=0, name=None, limit=8, keep=True, keep_out=True,
    cold=(), free=(),
):
    moved = sum(a.size * a.dtype.itemsize for a in args)
    moved += sum(o.size * o.dtype.itemsize for o in outs)
    if keep:
        args = tuple(
            a
            if n < smem or n in free
            else pltpu.with_memory_space_constraint(a, pltpu.HBM if n in cold else pltpu.VMEM)
            for n, a in enumerate(args)
        )
    if keep and keep_out:
        shapes = tuple(pltpu.VMEM(o.shape, o.dtype) for o in outs)
    else:
        shapes = tuple(outs)
    return pl.pallas_call(
        body,
        out_shape=shapes,
        in_specs=[SM] * smem + [VM] * (len(args) - smem),
        out_specs=tuple([VM] * len(outs)),
        scratch_shapes=list(scratch),
        cost_estimate=pl.CostEstimate(flops=flops, bytes_accessed=moved, transcendentals=0),
        compiler_params=pltpu.CompilerParams(vmem_limit_bytes=limit * MIB),
        name=name,
    )(*args)


def out(shape, dtype):
    return jax.ShapeDtypeStruct(shape, dtype)


def pick_body(meta, pos_ref, src_ref, own_ref, oth_ref):
    rows, span = pos_ref.shape[1], src_ref.shape[1]
    core, base = meta[0], meta[1]
    lane = lax.broadcasted_iota(jnp.int32, (rows, span), 1) + base
    for half, ref in ((0, own_ref), (1, oth_ref)):
        seq = core if half == 0 else 1 - core
        hot = jnp.where(pos_ref[half] == lane, 1.0, 0.0).astype(bf16)
        src = src_ref[seq]
        ref[...] = mm(hot, src).astype(bf16)


def place_body(meta, pos_ref, base_ref, own_ref, oth_ref, out_ref):
    rows, span = pos_ref.shape[2], base_ref.shape[1]
    core, base = meta[0], meta[1]
    row = lax.broadcasted_iota(jnp.int32, (span, rows), 0) + base
    for half, ref in ((0, own_ref), (1, oth_ref)):
        seq = core if half == 0 else 1 - core
        hot = jnp.where(pos_ref[half] == row, 1.0, 0.0).astype(bf16)
        added = mm(hot, ref[...])
        out_ref[seq] = (base_ref[seq].astype(f32) + added).astype(bf16)


def attn_fwd_body(
    idx, xo_ref, xt_ref, segc_ref, segr_ref, *refs
):
    packs = refs[:BLOCKS]
    a_ref, qkv_ref, p_ref, o_ref, bo_ref, bt_ref, wq_ref, wo_ref, gr_ref, r_ref, gcol = refs[BLOCKS:]
    rows, width = xo_ref.shape
    part = width // 4
    qcols = 3 * part
    blk = width // BLOCKS
    ob = part // BLOCKS
    for b, pk in enumerate(packs):
        s = idx[b]
        off = pl.multiple_of(s * blk, blk)
        wq_ref[pl.ds(off, blk), :] = pk[:, :qcols]
        gcol[pl.ds(off, blk), :] = pk[:, qcols : qcols + 128]
        off2 = pl.multiple_of(s * ob, ob)
        for j in range(4):
            wo_ref[pl.ds(off2, ob), j * part : (j + 1) * part] = pk[
                j * ob : (j + 1) * ob, qcols + 128 :
            ]
    eye = (
        lax.broadcasted_iota(jnp.int32, (8, 128), 0) == lax.broadcasted_iota(jnp.int32, (8, 128), 1)
    ).astype(f32).astype(bf16)
    gr = mm(eye, gcol[...], NT)
    gr_ref[...] = gr
    gain = gr[0:1]
    for half, x_ref in ((0, xo_ref), (1, xt_ref)):
        span = pl.ds(half * rows, rows)
        xb = x_ref[...]
        x = xb.astype(f32)
        scale = lax.rsqrt(jnp.mean(x * x, axis=-1, keepdims=True) + epsilon)
        a_ref[span, :] = (x * scale * gain).astype(bf16)
        r_ref[span, :] = mm(xb, gcol[...])

    def project(i, carry):
        cols = pl.ds(pl.multiple_of(i * part, part), part)
        qkv_ref[:, cols] = mm(a_ref[...], wq_ref[:, cols]).astype(bf16)
        return carry

    lax.fori_loop(0, 3, project, 0)
    ri = lax.broadcasted_iota(jnp.int32, (rows, rows), 0)
    ci = lax.broadcasted_iota(jnp.int32, (rows, rows), 1)
    causal = ci <= ri
    heads = part // HEAD_DIM
    score_scale = HEAD_DIM ** (-0.5)
    for half in range(2):
        allowed = causal & (segc_ref[half] == segr_ref[half])
        span = pl.ds(half * rows, rows)
        for h in range(heads):
            q = qkv_ref[span, h * HEAD_DIM : (h + 1) * HEAD_DIM]
            k = qkv_ref[span, part + h * HEAD_DIM : part + (h + 1) * HEAD_DIM]
            v = qkv_ref[span, 2 * part + h * HEAD_DIM : 2 * part + (h + 1) * HEAD_DIM]
            logits = jnp.where(allowed, mm(q, k, NT) * score_scale, masked)
            e = jnp.exp(logits - jnp.max(logits, axis=-1, keepdims=True))
            p = e * (1.0 / jnp.sum(e, axis=-1, keepdims=True))
            p_ref[half * heads + h] = p
            o_ref[span, h * HEAD_DIM : (h + 1) * HEAD_DIM] = mm(p.astype(bf16), v).astype(bf16)

    def project_out(i, carry):
        cols = pl.ds(pl.multiple_of(i * part, part), part)
        res = mm(o_ref[...], wo_ref[:, cols]).astype(bf16)
        bo_ref[:, cols] = res[:rows]
        bt_ref[:, cols] = res[rows:]
        return carry

    lax.fori_loop(0, 4, project_out, 0)


def norm_body(t_ref, u_ref, x_ref, gr_ref, m_ref):
    h = x_ref[...].astype(f32) + (t_ref[...].astype(f32) + u_ref[...].astype(f32))
    scale = lax.rsqrt(jnp.mean(h * h, axis=-1, keepdims=True) + epsilon)
    m_ref[...] = (h * scale * gr_ref[1:2]).astype(bf16)


def turn_body(a_ref, o_ref, at_ref, ot_ref):
    tile = 256

    def step(i, carry):
        cols = pl.ds(pl.multiple_of(i * tile, tile), tile)
        at_ref[cols, :] = a_ref[:, cols].T
        return carry

    lax.fori_loop(0, a_ref.shape[1] // tile, step, 0)
    ot_ref[...] = o_ref[...].T


def mlp_body(idx, mo_ref, mt_ref, co_ref, ct_ref, r_ref, *refs):
    packs, rest = refs[:BLOCKS], refs[BLOCKS:]
    g_ref, du_ref, db_ref, wu_ref, wd_ref, dmo_ref, dmt_ref = rest
    rows, width = mo_ref.shape
    units = wu_ref.shape[1]
    blk, sub = width // BLOCKS, units // BLOCKS
    for b in range(BLOCKS):
        wu_ref[pl.ds(pl.multiple_of(idx[b] * blk, blk), blk), :] = packs[b][:, :units]
        wd_ref[pl.ds(pl.multiple_of(idx[b] * sub, sub), sub), :] = packs[b][:, units:]
    r = r_ref[:, 2:3]
    db_ref[:rows, :] = (r[:rows] * co_ref[...].astype(f32)).astype(bf16)
    db_ref[rows:, :] = (r[rows:] * ct_ref[...].astype(f32)).astype(bf16)
    tile = 256

    def step(i, carry):
        cols = pl.ds(pl.multiple_of(i * tile, tile), tile)
        for half, m_ref in ((0, mo_ref), (1, mt_ref)):
            span = pl.ds(half * rows, rows)
            u = mm(m_ref[...], wu_ref[:, cols])
            u2 = u * u
            th = jnp.tanh(gelu_scale * (u + gelu_cubic * (u2 * u)))
            half_up = 0.5 * (1.0 + th)
            g_ref[span, cols] = (u * half_up).astype(bf16)
            slope = half_up + (0.5 * u) * (1.0 - th * th) * (
                gelu_scale * (1.0 + 3.0 * gelu_cubic * u2)
            )
            dg = mm(db_ref[span, :], wd_ref[cols, :], NT)
            du_ref[span, cols] = (dg * slope).astype(bf16)
        return carry

    lax.fori_loop(0, units // tile, step, 0)

    def step2(i, carry):
        cols = pl.ds(pl.multiple_of(i * tile, tile), tile)
        dm = mm(du_ref[...], wu_ref[cols, :], NT).astype(bf16)
        dmo_ref[:, cols] = dm[:rows]
        dmt_ref[:, cols] = dm[rows:]
        return carry

    lax.fori_loop(0, width // tile, step2, 0)


EARLY, LATE = (2, 3, 4, 5), (0, 1, 6, 7)


def grad_block(idx, b, ref, fm_ref, fg_ref, du_ref, db_ref, wu_ref, gcol, col_ref):
    width, units = fm_ref.shape[0], fg_ref.shape[0]
    blk, sub = width // BLOCKS, units // BLOCKS
    off = pl.ds(pl.multiple_of(idx[b] * blk, blk), blk)
    grad = mm(fm_ref[off, :], du_ref[...])
    ref[:, :units] = grad.astype(bf16)
    gain = jnp.sum(grad * wu_ref[off, :].astype(f32), axis=-1, keepdims=True)
    gain = gain / gcol[off, 1:2].astype(f32)
    col_ref[off, :] = jnp.broadcast_to(gain, (blk, 128))
    off = pl.ds(pl.multiple_of(idx[b] * sub, sub), sub)
    ref[:, units:] = mm(fg_ref[off, :], db_ref[...]).astype(bf16)


def early_grad_body(
    idx, g_ref, du_ref, db_ref, mo_ref, mt_ref, wu_ref, gcol, col_ref, fm_ref, fg_ref, *grads
):
    rows, width = mo_ref.shape
    tile = 256

    def turn_rows(i, carry):
        cols = pl.ds(pl.multiple_of(i * tile, tile), tile)
        fm_ref[cols, :rows] = mo_ref[:, cols].T
        fm_ref[cols, rows:] = mt_ref[:, cols].T
        fg_ref[cols, :] = g_ref[:, cols].T
        return carry

    lax.fori_loop(0, width // tile, turn_rows, 0)
    for b, ref in zip(EARLY, grads):
        grad_block(idx, b, ref, fm_ref, fg_ref, du_ref, db_ref, wu_ref, gcol, col_ref)


def late_grad_body(
    idx, g_ref, du_ref, db_ref, wu_ref, wd_ref, gcol, col_in, fm_ref, fg_ref, ao_ref, at_ref,
    co_ref, ct_ref, xo_ref, xt_ref, bo_ref, bt_ref, col_ref, *grads
):
    rows, width = bo_ref.shape
    tile = 256
    col_ref[...] = col_in[...]
    for b, ref in zip(LATE, grads):
        grad_block(idx, b, ref, fm_ref, fg_ref, du_ref, db_ref, wu_ref, gcol, col_ref)

    def step(i, carry):
        cols = pl.ds(pl.multiple_of(i * tile, tile), tile)
        res = mm(g_ref[...], wd_ref[:, cols])
        bo_ref[:, cols] = res[:rows].astype(bf16)
        bt_ref[:, cols] = res[rows:].astype(bf16)
        own, other = carry
        own += jnp.sum(
            (res[:rows] + ao_ref[:, cols].astype(f32)) * co_ref[:, cols].astype(f32),
            axis=-1, keepdims=True,
        )
        other += jnp.sum(
            (res[rows:] + at_ref[:, cols].astype(f32)) * ct_ref[:, cols].astype(f32),
            axis=-1, keepdims=True,
        )
        return own, other

    zero = jnp.zeros((rows, 1), f32)
    dots = lax.fori_loop(0, width // tile, step, (zero, zero))
    lane = lax.broadcasted_iota(jnp.int32, (rows, 128), 1)
    route = jnp.zeros((width, 128), f32)
    for d, x_ref in zip(dots, (xo_ref, xt_ref)):
        high = d.astype(bf16).astype(f32)
        two = jnp.where(lane == 0, high, jnp.where(lane == 1, d - high, 0.0)).astype(bf16)
        route += mm(x_ref[...], two, TN)
    total = jnp.sum(route[:, :2], axis=-1, keepdims=True)
    wide = lax.broadcasted_iota(jnp.int32, (width, 128), 1)
    col_ref[...] = jnp.where(wide == 1, col_ref[...], jnp.where(wide == 2, total, 0.0))


def hidden_grad_body(dt_ref, du_ref, bt_ref, bu_ref, x_ref, c_ref, r_ref, gr_ref, da_ref, dh_ref):
    dm = dt_ref[...].astype(f32) + du_ref[...].astype(f32)
    h = x_ref[...].astype(f32) + (bt_ref[...].astype(f32) + bu_ref[...].astype(f32))
    rows = h.shape[0]
    n = lax.rsqrt(jnp.mean(h * h, axis=-1, keepdims=True) + epsilon)
    t = dm * gr_ref[1:2]
    dh = n * t - h * (n * n * n) * jnp.mean(t * h, axis=-1, keepdims=True)
    dh_ref[...] = dh
    de = r_ref[:rows, 2:3] * c_ref[...].astype(f32)
    da_ref[...] = (de + dh).astype(bf16)


def result_body(at_ref, au_ref, mt_ref, mu_ref, c_ref, r_ref, e_ref, dr_ref):
    branch = (at_ref[...].astype(f32) + au_ref[...].astype(f32)) + (
        mt_ref[...].astype(f32) + mu_ref[...].astype(f32)
    )
    rows = branch.shape[0]
    e_ref[...] = (r_ref[:rows, 2:3] * branch).astype(bf16)
    dr = jnp.sum(c_ref[...].astype(f32) * branch, axis=-1, keepdims=True)
    dr_ref[...] = jnp.broadcast_to(dr, dr_ref.shape)


def attn_bwd_body(
    idx, at_ref, ot_ref, qkv_ref, p_ref, dao_ref, dat_ref, wq_ref, wo_ref, gcol, col_ref, *refs
):
    dqkv, near, far, (da,) = refs[0], refs[1:5], refs[5:7], refs[7:]
    rows, width = dao_ref.shape
    part = width // 4
    qcols = 3 * part
    heads = part // HEAD_DIM
    score_scale = HEAD_DIM ** (-0.5)
    da[:rows, :] = dao_ref[...]
    da[rows:, :] = dat_ref[...]
    for half in range(2):
        span = pl.ds(half * rows, rows)
        dmix = mm(da[span, :], wo_ref[...], NT).astype(bf16)
        for h in range(heads):
            lo, hi = h * HEAD_DIM, (h + 1) * HEAD_DIM
            q = qkv_ref[span, lo:hi]
            k = qkv_ref[span, part + lo : part + hi]
            v = qkv_ref[span, 2 * part + lo : 2 * part + hi]
            do = dmix[:, lo:hi]
            p = p_ref[half * heads + h]
            dp = mm(do, v, NT)
            ds = (p * (dp - jnp.sum(p * dp, axis=-1, keepdims=True))).astype(bf16)
            dqkv[span, lo:hi] = (mm(ds, k) * score_scale).astype(bf16)
            dqkv[span, part + lo : part + hi] = (mm(ds, q, TN) * score_scale).astype(bf16)
            dqkv[span, 2 * part + lo : 2 * part + hi] = mm(p.astype(bf16), do, TN).astype(bf16)
    blk = width // BLOCKS
    ob = part // BLOCKS
    lane = lax.broadcasted_iota(jnp.int32, (blk, 128), 1)
    for b in range(BLOCKS):
        s = idx[b]
        k = b // 2
        ref, row = (near[k], 0) if b % 2 == 0 else (far[(k + 3) % 4 // 2], (k + 3) % 2 * blk)
        rows_of = slice(row, row + blk)
        off = pl.ds(pl.multiple_of(s * blk, blk), blk)
        grad = mm(at_ref[off, :], dqkv[...])
        ref[rows_of, :qcols] = grad.astype(bf16)
        gain = jnp.sum(grad * wq_ref[off, :].astype(f32), axis=-1, keepdims=True)
        gain = gain / gcol[off, 0:1].astype(f32)
        ref[rows_of, qcols : qcols + 128] = jnp.where(lane == 0, gain, col_ref[off, :]).astype(bf16)
        og = mm(ot_ref[pl.ds(pl.multiple_of(s * ob, ob), ob), :], da[...]).astype(bf16)
        for j in range(4):
            ref[row + j * ob : row + (j + 1) * ob, qcols + 128 :] = og[:, j * part : (j + 1) * part]


def normed_grad_body(dqkv_ref, wq_ref, do_ref, dt_ref):
    rows, width = do_ref.shape
    tile = 256

    def step(i, carry):
        cols = pl.ds(pl.multiple_of(i * tile, tile), tile)
        d = mm(dqkv_ref[...], wq_ref[cols, :], NT).astype(bf16)
        do_ref[:, cols] = d[:rows]
        dt_ref[:, cols] = d[rows:]
        return carry

    lax.fori_loop(0, width // tile, step, 0)


def input_grad_body(t_ref, u_ref, x_ref, dh_ref, dr_ref, gr_ref, dx_ref):
    d = t_ref[...].astype(f32) + u_ref[...].astype(f32)
    x = x_ref[...].astype(f32)
    m = lax.rsqrt(jnp.mean(x * x, axis=-1, keepdims=True) + epsilon)
    s = d * gr_ref[0:1]
    dxn = m * s - x * (m * m * m) * jnp.mean(s * x, axis=-1, keepdims=True)
    dx_ref[...] = (dxn + dh_ref[...] + dr_ref[:, 0:1] * gr_ref[2:3]).astype(bf16)


HEAD_OF = (0, 2, 1, 3)


def pack_body(meta, qkv_ref, up_ref, gains_ref, *refs):
    outs, (tmp,) = refs[:4], refs[4:]
    width, units = qkv_ref.shape[1] // 3, up_ref.shape[1]
    part = width // 4
    sub = units // (4 * BLOCKS)
    for j in range(4):
        p = HEAD_OF[j]
        for t in range(3):
            for z in range(4):
                src = t * width + (4 * z + p) * HEAD_DIM
                dst = t * part + z * HEAD_DIM
                tmp[j, :, dst : dst + HEAD_DIM] = qkv_ref[:, src : src + HEAD_DIM]
        tmp[j, :, 3 * part : 3 * part + 128] = gains_ref[...]
        for s in range(BLOCKS):
            dst = 3 * part + 128 + s * sub
            src = (4 * s + j) * sub
            tmp[j, :, dst : dst + sub] = up_ref[:, src : src + sub]
    for k, ref in enumerate(outs):
        ref[...] = tmp[meta[3] ^ k]


def join_body(meta, c0, c1, c2, c3, own_ref, moved_ref, down_ref, attn_ref, mlp_ref):
    mine, width = own_ref.shape
    part = width // 4
    head = 3 * part + 128
    for k, ref in enumerate((c0, c1, c2, c3)):
        off = pl.ds(pl.multiple_of((meta[3] ^ k) * mine, mine), mine)
        attn_ref[off, :head] = ref[:, :head]
        mlp_ref[off, : mlp_ref.shape[1] - width] = ref[:, head:]
    mlp_ref[:, mlp_ref.shape[1] - width :] = down_ref[...]
    take = jnp.full(own_ref.shape, meta[4]) == 1
    rows = jnp.where(take, moved_ref[...].astype(f32), own_ref[...].astype(f32)).astype(bf16)
    for j in range(4):
        attn_ref[j * mine : (j + 1) * mine, head:] = rows[:, j * part : (j + 1) * part]


def split_body(
    meta, m0, m1, m2, a0, a1, a2, c0, c1, c2, c3, down_ref, out_ref, tm, ta
):
    mine, width = out_ref.shape
    units = m0.shape[1] - width
    part = width // 4
    head = 3 * part + 128
    for n in range(4):
        span = pl.ds(n * mine, mine)
        total = (m0[span, :].astype(f32) + m1[span, :].astype(f32)) + m2[span, :].astype(f32)
        down_ref[span, :] = total[:, units:]
        tm[span, :] = total[:, :units]
        late = pl.ds((4 + n) * mine, mine)
        total = (a0[span, :].astype(f32) + a1[late, :].astype(f32)) + a2[span, :].astype(f32)
        ta[span, :] = total[:, :head]
        out_ref[:, n * part : (n + 1) * part] = total[:, head:]
    for k, ref in enumerate((c0, c1, c2, c3)):
        off = pl.ds(pl.multiple_of((meta[3] ^ k) * mine, mine), mine)
        ref[:, :head] = ta[off, :].astype(ref.dtype)
        ref[:, head:] = tm[off, :].astype(ref.dtype)


def final_body(meta, c0, c1, c2, c3, qkv_ref, up_ref, small_ref, tmp):
    mine = qkv_ref.shape[0]
    width = qkv_ref.shape[1] // 3
    part = width // 4
    head = 3 * part + 128
    sub = up_ref.shape[1] // (4 * BLOCKS)
    for k, ref in enumerate((c0, c1, c2, c3)):
        tmp[meta[3] ^ k] = ref[...].astype(f32)
    for j in range(4):
        for t in range(3):
            for z in range(4):
                dst = t * width + (4 * z + HEAD_OF[j]) * HEAD_DIM
                src = t * part + z * HEAD_DIM
                qkv_ref[:, dst : dst + HEAD_DIM] = tmp[j, :, src : src + HEAD_DIM]
        for s in range(BLOCKS):
            dst = (4 * s + j) * sub
            up_ref[:, dst : dst + sub] = tmp[j, :, head + s * sub : head + (s + 1) * sub]
    last = slice(3 * part, head)
    small = (tmp[0, :, last] + tmp[1, :, last]) + (tmp[2, :, last] + tmp[3, :, last])
    wide = jnp.concatenate([small, jnp.zeros((128 - mine, 128), f32)], axis=0)
    small_ref[...] = wide.T[:8]


def flip_bit(v, axis, size, mask):
    return lax.ppermute(v, axis, [(i, i ^ mask) for i in range(size)])


def swap_core(v):
    return flip_bit(v, "grp", 4, 1)


def swap_pair(v):
    return flip_bit(v, "grp", 4, 2)


def swap_side(v, seqs):
    return flip_bit(v, "seq", seqs, 1)


def shift_one(v, seqs):
    return lax.ppermute(v, "seq", [(i, (i + 2) % seqs) for i in range(seqs)])


def reorder(parts, member):
    low = (member & 1) == 1
    high = (member & 2) == 2
    res = []
    for j in range(4):
        straight = jnp.where(low, parts[j ^ 1], parts[j])
        crossed = jnp.where(low, parts[j ^ 3], parts[j ^ 2])
        res.append(jnp.where(high, crossed, straight))
    return res


def exchange(chunks, member):
    rel = reorder(chunks, member)
    got = [rel[0]] + [flip_bit(rel[k], "grp", 4, k) for k in range(1, 4)]
    return reorder(got, member)


def native_gather(pack):
    full = lax.all_gather(pack, "seq", axis=0, tiled=True)
    return list(full.reshape((BLOCKS, -1) + full.shape[1:]))


def native_scatter(blocks):
    full = jnp.concatenate(blocks, axis=0)
    return lax.psum_scatter(full.astype(f32), "seq", scatter_dimension=0, tiled=True)


def add(*parts):
    total = parts[0].astype(f32)
    for p in parts[1:]:
        total = total + p.astype(f32)
    return total.astype(bf16)


class Flow:
    def __getitem__(self, name):
        return self.__dict__[name]

    def __setitem__(self, name, value):
        self.__dict__[name] = value

    def order(self, value, name):
        token = lax.create_token()
        token, self[name] = lax.optimization_barrier((token, self[name]))
        return lax.optimization_barrier((token, value))[1]

    def sync(self, *names):
        held = [n for n in names if n in self.__dict__]
        done = lax.optimization_barrier(tuple(self[n] for n in held))
        for n, value in zip(held, done):
            self[n] = value


def on_device(
    tokens,
    segments,
    routed,
    qkv_weight,
    out_weight,
    up_weight,
    down_weight,
    attn_gain,
    mlp_gain,
    router_weight,
    cotangent,
):
    groups, seqs = lax.axis_size("grp"), lax.axis_size("seq")
    member, place = lax.axis_index("grp"), lax.axis_index("seq")
    seq_dev, span, width = tokens.shape
    rows = routed.shape[1]
    units = down_weight.shape[0] * groups * seqs
    if groups != 4 or seq_dev != 2:
        raise ValueError("mesh")
    native = seqs != BLOCKS
    part, ff = width // 4, units // 4
    core, pair = member & 1, member >> 1
    mine = qkv_weight.shape[0]
    head = 3 * part + 128
    both = 2 * rows
    odd = (place ^ member) & 1
    meta = jnp.stack([core, member * span, pair, member, odd]).astype(jnp.int32)
    half = out((rows, width), bf16)
    v = Flow()

    queue = []

    chain = []

    def hop(name, t, lag):
        if len(chain) >= lag:
            t = v.order(t, chain[-lag])
        chain.append(name)
        v[name] = shift_one(t, seqs)

    def side(name, t, lag):
        if len(queue) >= lag:
            t = v.order(t, queue[-lag])
        queue.append(name)
        v[name] = swap_side(t, seqs)


    flip = core == 1
    pos = jnp.where(flip, routed[::-1], routed)
    starts = jnp.stack(
        [jnp.sum((segments < n).astype(jnp.int32), axis=1) for n in range(1, SEG_COUNT)], axis=0
    )
    seg = jnp.sum((routed[None] >= starts[:, :, None]).astype(jnp.int32), axis=0)
    seg = jnp.where(flip, seg[::-1], seg)
    pos_col, pos_row = pos[:, :, None], pos[:, None, :]
    seg_col, seg_row = seg[:, :, None], seg[:, None, :]

    def pick(source, name):
        return call(
            pick_body, (meta, pos_col, source), (half, half), smem=1,
            flops=4 * rows * span * width, name=name, keep_out=False, cold=(2,), free=(1,),
            limit=24,
        )

    gains = jnp.stack([attn_gain, mlp_gain, router_weight], axis=1)
    gains = jnp.pad(gains, ((0, 0), (0, 125)))
    if native:
        qkv_view = qkv_weight.reshape(mine, 3, 4, 4, HEAD_DIM)
        chunks = [
            jnp.concatenate([qkv_view[:, :, :, p].reshape(mine, 3 * part), gains], axis=1)
            for p in HEAD_OF
        ]
        qkv_blocks = native_gather(jnp.concatenate(exchange(chunks, member), axis=0))
        out_full = lax.all_gather(out_weight, ("seq", "grp"), axis=0, tiled=True)
        out_view = out_full.reshape(4, 4, HEAD_DIM, width)
        head_set = 2 * core + pair
        out_rows = lax.dynamic_index_in_dim(out_view, head_set, 1, keepdims=False)
        out_rows = out_rows.reshape(BLOCKS, part // BLOCKS, width)
        attn_packs = [
            jnp.concatenate(
                [q, jnp.concatenate([o[:, j * part : (j + 1) * part] for j in range(4)], axis=0)],
                axis=1,
            )
            for q, o in zip(qkv_blocks, out_rows)
        ]
        up_view = up_weight.reshape(mine, seqs, 4, ff // seqs)
        chunks = [up_view[:, :, j].reshape(mine, ff) for j in range(4)]
        up_rows = jnp.concatenate(exchange(chunks, member), axis=0)
        mlp_packs = native_gather(jnp.concatenate([up_rows, down_weight], axis=1))
        order = jnp.arange(BLOCKS, dtype=jnp.int32)
        x_mine, x_send = pick(tokens, "pick_tokens")
        v.tx = add(x_mine, swap_core(x_send))
        v.yx = swap_pair(v.tx)
        v.x = v.tx + v.yx
        v.xo = swap_core(v.x)
        c_mine, c_send = pick(cotangent, "pick_cotangent")
        v.tc = add(c_mine, swap_core(c_send))
    else:
        order = jnp.stack(
            [((place ^ r) - 2 * k) % seqs for k in range(BLOCKS // 2) for r in range(2)]
        ).astype(jnp.int32)
        swaps = [
            (s * 4 + g, (s ^ 1) * 4 + (g ^ 1)) for s in range(seqs) for g in range(4) if (s ^ g) & 1
        ]
        chunk = out((mine, head + ff), bf16)
        chunks = call(
            pack_body, (meta, qkv_weight, up_weight, gains), (chunk,) * 4,
            scratch=[pltpu.VMEM((4, mine, head + ff), bf16)], smem=1, name="pack", cold=(1, 2, 3),
        )
        v.k0, v.k1, v.k2, v.k3 = chunks
        v.tokens = tokens
        v.sync("k1", "k2", "k3", "tokens")
        got = [v.k0] + [flip_bit(v["k%d" % k], "grp", 4, k) for k in range(1, 4)]
        x_mine, x_send = pick(v.tokens, "pick_tokens")
        moved = lax.ppermute(out_weight, ("seq", "grp"), swaps)
        v.a0, v.m0 = call(
            join_body, (meta, *got, out_weight, moved, down_weight),
            (out((mine * 4, width + 128), bf16), out((mine * 4, ff + width), bf16)), smem=1,
            name="join", cold=(2, 3, 4, 5, 6, 7),
        )
        v.tx = add(x_mine, swap_core(x_send))
        v.sync("a0", "m0", "tx")
        for n, k in (('a', 1), ('m', 1), ('a', 2), ('a', 3), ('m', 2), ('m', 3)):
            hop("%s%d" % (n, k), v["%s%d" % (n, k - 1)], 3)
        v.yx = swap_pair(v.tx)
        v.x = v.tx + v.yx
        v.xo = swap_core(v.x)
        for n, k in (('m', 0), ('a', 0), ('a', 1), ('a', 2), ('a', 3), ('m', 1), ('m', 2), ('m', 3)):
            side("x%s%d" % (n, k), v["%s%d" % (n, k)], 2)
        c_mine, c_send = pick(cotangent, "pick_cotangent")
        v.tc = add(c_mine, swap_core(c_send))
        v.yc = swap_pair(v.tc)
        v.sync("x", "xo", "m1")
        attn_names = [n + str(k) for k in range(4) for n in ("a", "xa")]
        attn_packs = [v[n] for n in attn_names]

    a, qkv, probs, mix, ba_o, ba_t, w_qkv, w_out, gain_rows, r, gain_cols = call(
        attn_fwd_body,
        (order, v.x, v.xo, seg_col, seg_row, *attn_packs),
        (
            out((both, width), bf16),
            out((both, 3 * part), bf16),
            out((2 * part // HEAD_DIM, rows, rows), f32),
            out((both, part), bf16),
            half,
            half,
            out((width, 3 * part), bf16),
            out((part, width), bf16),
            out((8, width), f32),
            out((both, 128), f32),
            out((width, 128), bf16),
        ),
        smem=1,
        flops=2 * both * width * width,
        name="attn_fwd",
        cold=range(1, 12),
        free=(12,),
    )
    v.a, v.mix = a, mix
    v.tb = add(ba_o, swap_core(ba_t))
    v.sync("tb", "a", "mix", "xm1")
    v.yb = swap_pair(v.tb)
    if native:
        v.yc = swap_pair(v.tc)
    a_turned, mix_turned = call(
        turn_body, (v.a, v.mix), (out((width, both), bf16), out((part, both), bf16)),
        name="turn",
    )
    v.c = v.tc + v.yc
    v.co = swap_core(v.c)
    v.sync("yb", "tb", "co", "c", "xm2")
    (v.h,) = call(
        norm_body, (v.tb, v.yb, v.x, gain_rows), (half,), name="norm_two", free=(0, 1, 2)
    )
    v.ho = swap_core(v.h)
    if not native:
        mlp_packs = [v[n + str(k)] for k in range(4) for n in ("m", "xm")]
    g, du, db, w_up, w_down, dm_o, dm_t = call(
        mlp_body,
        (order, v.h, v.ho, v.c, v.co, r, *mlp_packs),
        (
            out((both, ff), bf16),
            out((both, ff), bf16),
            out((both, width), bf16),
            out((width, ff), bf16),
            out((ff, width), bf16),
            half,
            half,
        ),
        smem=1,
        flops=6 * both * width * ff,
        name="mlp",
        cold=(2, 3, 4, *range(6, 13)),
        free=(13,),
    )

    v.du = du
    v.td = add(dm_o, swap_core(dm_t))
    v.sync("td", "du")
    v.yd = swap_pair(v.td)
    packet = out((width // BLOCKS, ff + width), bf16)
    col, turned_m, turned_g, *first = call(
        early_grad_body,
        (order, g, v.du, db, v.h, v.ho, w_up, gain_cols),
        (
            out((width, 128), f32), out((width, both), bf16), out((ff, both), bf16),
            *([packet] * 4),
        ),
        smem=1,
        flops=2 * both * width * ff,
        name="early_grad",
        cold=(5,),
    )
    v.g = g
    v.f0, v.f1 = first[1], first[3]
    v.sync("f0", "f1", "g")
    first[1], first[3] = v.f0, v.f1
    bm_o, bm_t, cols, *last = call(
        late_grad_body,
        (
            order, v.g, v.du, db, w_up, w_down, gain_cols, col, turned_m, turned_g, ba_o, ba_t,
            v.c, v.co, v.x, v.xo,
        ),
        (half, half, out((width, 128), f32), *([packet] * 4)),
        smem=1,
        flops=4 * both * width * ff,
        name="late_grad",
        cold=(12, 13, 14, 15),
    )
    mlp_grads = [*last[:2], *first, *last[2:]]
    v.bm, v.bn = bm_o, bm_t
    v.tm = add(v.bm, swap_core(v.bn))
    parts = {"m": mlp_grads}
    queue.clear()
    chain.clear()
    v.__dict__.update({n + str(k): None for n in ("xm", "xa") for k in range(4)})
    if not native:
        for n, k in (('m', 1),):
            side("x%s%d" % (n, k), parts[n][2 * k + 1], 2)
    v.sync("yd", "td", "bm")
    da_own, dh = call(
        hidden_grad_body,
        (v.td, v.yd, v.tb, v.yb, v.x, v.c, r, gain_rows),
        (half, out((rows, width), f32)),
        name="hidden_grad",
        free=range(6),
    )
    v.da = da_own
    v.dao = swap_core(da_own)
    def attention_back(v):
        dqkv, *attn_grads = call(
            attn_bwd_body,
            (
                order, a_turned, mix_turned, qkv, probs, v.da, v.dao, w_qkv, w_out,
                gain_cols, cols,
            ),
            (
                out((both, 3 * part), bf16),
                *([out((width // BLOCKS, width + 128), bf16)] * 4),
                *([out((2 * width // BLOCKS, width + 128), bf16)] * 2),
            ),
            scratch=[pltpu.VMEM((both, width), bf16)],
            smem=1,
            flops=3 * both * width * width,
            name="attn_bwd",
            free=(6,),
        )
        v.dqkv = dqkv
        return attn_grads

    def normed_back(dqkv):
        return call(
            normed_grad_body, (dqkv, w_qkv), (half, half), flops=2 * both * width * 3 * part,
            name="normed_grad",
        )

    def give():
        return call(
            result_body,
            (v.tb, v.yb, v.tm, v.ym, v.c, r),
            (half, out((rows, 128), f32)),
            name="result",
            free=range(5),
        )

    def take(dr):
        return call(
            input_grad_body, (v.tx2, v.yx2, v.x, dh, dr, gain_rows), (half,),
            name="input_grad", free=range(3),
        )[0]

    def place_rows(base, own, other, name):
        return call(
            place_body, (meta, pos_row, base, own, other), (out(base.shape, bf16),), smem=1,
            flops=4 * rows * span * width, name=name, keep=False, limit=24,
        )[0]

    if native:
        attn_grads = attention_back(v)
        blk = width // BLOCKS
        far = {(k + 3) % 4: attn_grads[4 + (k + 3) % 4 // 2] for k in range(4)}
        attn_grads = [
            attn_grads[k] if r == 0 else far[(k + 3) % 4][(k + 3) % 2 * blk :][:blk]
            for k in range(4)
            for r in range(2)
        ]
        dx_o, dx_t = normed_back(v.dqkv)
        v.ym = swap_pair(v.tm)
        v.tx2 = add(dx_o, swap_core(dx_t))
        v.yx2 = swap_pair(v.tx2)
        v.e, dr = give()
        v.eo = swap_core(v.e)
        v.dx = take(dr)
        v.dxo = swap_core(v.dx)
    else:
        attn_grads = attention_back(v)
        v.dxm, v.dxs = normed_back(v.dqkv)
        parts["a"] = attn_grads
        for k in range(4):
            v["m%d" % k], v["a%d" % k] = mlp_grads[2 * k], attn_grads[k]
        v.ym = swap_pair(v.tm)
        for n, k in (('m', 2), ('m', 3), ('a', 4), ('m', 0), ('a', 5)):
            side("x%s%d" % (n, k), parts[n][2 * k + 1 if n == "m" else k], 2)
        blk = width // BLOCKS
        v.tx2 = add(v.dxm, swap_core(v.dxs))

        def step(n, k):
            across = v["xm%d" % k] if n == "m" else v["xa%d" % (4 + k // 3)]
            if n == "a":
                across = across[blk:] if k == 2 else across[:blk]
            terms = [v["%s%d" % (n, k)], across]
            if k > 1:
                terms.append(v["z%s%d" % (n, k - 1)])
            hop("z%s%d" % (n, k), add(*terms), 2)

        for n, k in (('m', 1), ('m', 2), ('a', 1), ('a', 2), ('a', 3), ('m', 3)):
            if (n, k) == ("a", 1):
                v.sync("tx2", "a1")
                v.yx2 = swap_pair(v.tx2)
            if (n, k) == ("a", 2):
                v.sync("ym", "tm", "a2")
                v.e, dr = give()
                v.eo = swap_core(v.e)
            if (n, k) == ("a", 3):
                v.sync("yx2", "tx2", "eo", "e", "a3")
            if (n, k) == ("m", 3):
                v.dx = take(dr)
                v.dxo = swap_core(v.dx)
                v.mixed = place_rows(tokens, v.e, v.eo, "place_mixed")
                v.sync("mixed", "dxo", "dx", "m3")
            step(n, k)
        v.input_grad = place_rows(cotangent, v.dx, v.dxo, "place_input_grad")
        v.sync("input_grad", "m0")
        piece = [out((mine, head + ff), f32)] + [out((mine, head + ff), bf16)] * 3
        *cut, down_grad, og = call(
            split_body,
            (meta, v.m0, v.xm0, v.zm3, v.a0, v.xa5, v.za3),
            (*piece, out((4 * mine, width), f32), out((mine, width), f32)),
            scratch=[pltpu.VMEM((4 * mine, ff), f32), pltpu.VMEM((4 * mine, head), f32)], smem=1,
            name="split", cold=(2, 3), free=(5, 6),
        )
        cut = [cut[0]] + [flip_bit(cut[k], "grp", 4, k) for k in range(1, 4)]
        out_moved = lax.ppermute(og, ("seq", "grp"), swaps)
        out_grad = jnp.where(odd == 1, out_moved, og)
        qkv_grad, up_grad, small = call(
            final_body, (meta, *cut),
            (out((mine, 3 * width), f32), out((mine, units), f32), out((8, 128), f32)),
            scratch=[pltpu.VMEM((4, mine, head + ff), f32)], smem=1, name="final", keep_out=False,
            cold=(2, 3, 4),
        )
        small = small[:3, :mine]

    if native:
        v.mixed = place_rows(tokens, v.e, v.eo, "place_mixed")
        v.input_grad = place_rows(cotangent, v.dx, v.dxo, "place_input_grad")
    mixed, input_grad = v.mixed, v.input_grad

    if native:
        mlp_sum = native_scatter(mlp_grads)
        up_sum, down_grad = mlp_sum[:, :ff], mlp_sum[:, ff:]
        back = exchange([up_sum[j * mine : (j + 1) * mine] for j in range(4)], member)
        up_grad = jnp.stack([b.reshape(mine, seqs, ff // seqs) for b in back], axis=2)
        up_grad = up_grad.reshape(mine, units)
        step = part // BLOCKS
        out_mine = jnp.concatenate(
            [
                jnp.concatenate([b[j * step : (j + 1) * step, head:] for j in range(4)], axis=1)
                for b in attn_grads
            ],
            axis=0,
        )
        out_mine = out_mine.astype(f32).reshape(4, 1, HEAD_DIM, width)
        slots = (jnp.arange(4) == head_set).astype(f32)[None, :, None, None]
        out_all = (out_mine * slots).reshape(width, width)
        out_grad = lax.psum_scatter(out_all, ("seq", "grp"), scatter_dimension=0, tiled=True)
        attn_sum = native_scatter([b[:, :head] for b in attn_grads])
        back = exchange([attn_sum[j * mine : (j + 1) * mine] for j in range(4)], member)
        by_head = [b[:, : 3 * part].reshape(mine, 3, 4, HEAD_DIM) for b in back]
        qkv_grad = jnp.stack([by_head[HEAD_OF.index(p)] for p in range(4)], axis=3)
        qkv_grad = qkv_grad.reshape(mine, 3 * width)
        small = sum(b[:, 3 * part : 3 * part + 3] for b in back).T
    return (
        mixed,
        input_grad,
        qkv_grad,
        out_grad,
        up_grad,
        down_grad,
        small[0],
        small[1],
        small[2],
    )


def solution(mesh):
    placed = (
        P("seq", "grp", None),
        P("seq", None),
        P("seq", None),
        P(("seq", "grp"), None),
        P(("seq", "grp"), None),
        P(("seq", "grp"), None),
        P(("seq", "grp"), None),
        P(("seq", "grp")),
        P(("seq", "grp")),
        P(("seq", "grp")),
        P("seq", "grp", None),
    )
    return jax.shard_map(
        on_device,
        mesh=mesh,
        in_specs=placed,
        out_specs=(
            P("seq", "grp", None),
            P("seq", "grp", None),
            P(("seq", "grp"), None),
            P(("seq", "grp"), None),
            P(("seq", "grp"), None),
            P(("seq", "grp"), None),
            P(("seq", "grp")),
            P(("seq", "grp")),
            P(("seq", "grp")),
        ),
        check_vma=False,
    )
```
